32 devices in a mesh: dp: 8 (over y, x, core), tensor: 4 (over z).
Axes of the slice: x: 2, y: 2, z: 4, core: 2. Of those that a mesh axis runs over, the one named last changes fastest.
Arguments:
- latents: bfloat16 [1024, 16, 1408], P('tensor', 'dp'), may hold values from -6 to 6
- skips: bfloat16 [1024, 16, 1408], P('tensor', 'dp'), may hold values from -6 to 6
- text_states: bfloat16 [16, 333, 1024], P('dp'), may hold values from -6 to 6
- time_embedding: bfloat16 [16, 1408], P('dp'), may hold values from -6 to 6
- merger: bfloat16 [2816, 1408], P(('dp', 'tensor')), may hold values from -0.109375 to 0.109375
- modulator: bfloat16 [1408, 1408], P(('dp', 'tensor')), may hold values from -0.15625 to 0.15625
- norm_gains: float32 [5, 1408], P(None, ('dp', 'tensor')), may hold values from 0.1 to 1.9
- norm_biases: float32 [9, 1408], P(None, ('dp', 'tensor')), may hold values from -1.75 to 1.75
- output_bias: float32 [1408], P(('dp', 'tensor')), may hold values from -8 to 8
- projector: bfloat16 [1408, 3, 1408], P('dp', None, 'tensor'), may hold values from -0.15625 to 0.15625
- combiner: bfloat16 [1408, 1408], P('tensor', 'dp'), may hold values from -1.25 to 1.25
- cross_query: bfloat16 [1408, 1408], P('dp', 'tensor'), may hold values from -0.15625 to 0.15625
- cross_memory: bfloat16 [1024, 2, 1408], P('dp', None, 'tensor'), may hold values from -0.1875 to 0.1875
- blender: bfloat16 [1408, 1408], P('tensor', 'dp'), may hold values from -1.25 to 1.25
- expander: bfloat16 [1408, 6144], P('dp', 'tensor'), may hold values from -0.15625 to 0.15625
- reducer: bfloat16 [6144, 1408], P('tensor', 'dp'), may hold values from -0.078125 to 0.078125
- column_biases: float32 [6, 1408], P(None, ('dp', 'tensor')), may hold values from -1.75 to 1.75
- hidden_bias: float32 [6144], P(('dp', 'tensor')), may hold values from -1.75 to 1.75
- per_head_norm_gains: float32 [4, 88], replicated, may hold values from 0.1 to 1.9
- head_shifts: float32 [3, 88], replicated, may hold values from -1.75 to 1.75
- cotangent: bfloat16 [1024, 16, 1408], P('tensor', 'dp'), may hold values from -6 to 6
Outputs:
- block_out: float32 [1024, 16, 1408], P('tensor', 'dp')
- latent_grads: float32 [1024, 16, 1408], P('tensor', 'dp')
- skip_grads: float32 [1024, 16, 1408], P('tensor', 'dp')
- text_grads: float32 [16, 333, 1024], P('dp', None, 'tensor')
- time_grads: float32 [16, 1408], P('dp', 'tensor')
- merger_grads: float32 [2816, 1408], P(('dp', 'tensor'))
- modulator_grads: float32 [1408, 1408], P(('dp', 'tensor'))
- gain_grads: float32 [5, 1408], P(None, ('dp', 'tensor'))
- bias_grads: float32 [9, 1408], P(None, ('dp', 'tensor'))
- output_bias_grads: float32 [1408], P(('dp', 'tensor'))
- projector_grads: float32 [1408, 3, 1408], P('dp', None, 'tensor')
- combiner_grads: float32 [1408, 1408], P('tensor', 'dp')
- query_grads: float32 [1408, 1408], P('dp', 'tensor')
- memory_grads: float32 [1024, 2, 1408], P('dp', None, 'tensor')
- blender_grads: float32 [1408, 1408], P('tensor', 'dp')
- expander_grads: float32 [1408, 6144], P('dp', 'tensor')
- reducer_grads: float32 [6144, 1408], P('tensor', 'dp')
- column_grads: float32 [6, 1408], P(None, ('dp', 'tensor'))
- hidden_grads: float32 [6144], P(('dp', 'tensor'))
- scale_grads: float32 [4, 88], replicated
- shift_grads: float32 [3, 88], replicated
The draws below stay inside these ranges and needn't reach their ends.
All inputs are finite; a program needn't handle non-finite values.
Results may differ from the reference program's by a relative error of at most 0.038.
Values may be sent and summed in bfloat16 or wider, within the bound.
A program may use at most 320 MiB of HBM per device.

```python
import jax
import jax.numpy as jnp
from jax import lax

HD = 88
D = 1408
FF = 6144
TXT_D = 1024
TXT = 333
GRID_W = 32
LEN = 1024
LATENTS = 16


def block_scale(rng, extent, pieces, smallest, high):
    level, own = 1.0, jax.random.fold_in(rng, 6)
    for dim, parts in pieces:
        draws = jnp.exp(jax.random.uniform(jax.random.fold_in(own, dim), (parts,), jnp.float32, smallest / len(pieces), high / len(pieces)))
        level = level * jnp.repeat(draws, extent[dim] // parts).reshape([-1 if axis == dim else 1 for axis in range(len(extent))])
    return level


def normal_values(rng, shape, scale, limit, cuts=(), dtype=jnp.bfloat16):
    array = jax.random.normal(rng, shape, jnp.float32) * scale
    if len(cuts) > 0:
        array = block_scale(rng, shape, cuts, -0.22, 0.18) * array
    return jnp.clip(array, min=-limit, max=limit).astype(dtype)


def setup_inputs(seed: int = 0) -> dict:
    streams_of = jax.random.split(jax.random.key(seed), 22)
    return {
        "latents": normal_values(streams_of[0], (LEN, LATENTS, D), 1.0, 6.0, ((0, 4), (1, 8))),
        "skips": normal_values(streams_of[1], (LEN, LATENTS, D), 1.0, 6.0, ((0, 4), (1, 8))),
        "text_states": normal_values(streams_of[2], (LATENTS, TXT, TXT_D), 1.0, 6.0, ((0, 8),)),
        "time_embedding": normal_values(streams_of[3], (LATENTS, D), 1.0, 6.0, ((0, 8),)),
        "merger": normal_values(streams_of[4], (2 * D, D), (2 * D) ** -0.5, 0.109375, ((0, 32),)),
        "modulator": normal_values(streams_of[5], (D, D), D ** -0.5, 0.15625, ((0, 32),)),
        "norm_gains": jnp.clip(1.0 + 0.18 * jax.random.normal(streams_of[6], (5, D), jnp.float32), 0.1, 1.9),
        "norm_biases": normal_values(streams_of[7], (9, D), 0.3, 1.75, ((1, 32),), jnp.float32),
        "output_bias": normal_values(streams_of[8], (D,), 1.5, 8.0, ((0, 32),), jnp.float32),
        "projector": normal_values(streams_of[9], (D, 3, D), D ** -0.5, 0.15625, ((0, 8), (2, 4))),
        "combiner": normal_values(streams_of[10], (D, D), (D // 64) ** -0.5, 1.25, ((0, 4), (1, 8))),
        "cross_query": normal_values(streams_of[11], (D, D), D ** -0.5, 0.15625, ((0, 8), (1, 4))),
        "cross_memory": normal_values(streams_of[12], (TXT_D, 2, D), TXT_D ** -0.5, 0.1875, ((0, 8), (2, 4))),
        "blender": normal_values(streams_of[13], (D, D), (D // 64) ** -0.5, 1.25, ((0, 4), (1, 8))),
        "expander": normal_values(streams_of[14], (D, FF), D ** -0.5, 0.15625, ((0, 8), (1, 4))),
        "reducer": normal_values(streams_of[15], (FF, D), FF ** -0.5, 0.078125, ((0, 4), (1, 8))),
        "column_biases": normal_values(streams_of[16], (6, D), 0.3, 1.75, ((1, 32),), jnp.float32),
        "hidden_bias": normal_values(streams_of[17], (FF,), 0.3, 1.75, ((0, 32),), jnp.float32),
        "per_head_norm_gains": jnp.clip(1.0 + 0.18 * jax.random.normal(streams_of[18], (4, HD), jnp.float32), 0.1, 1.9),
        "head_shifts": normal_values(streams_of[19], (3, HD), 0.3, 1.75, (), jnp.float32),
        "cotangent": normal_values(streams_of[20], (LEN, LATENTS, D), 1.0, 6.0, ((0, 4), (1, 8))),
    }


EPSILON = 1e-06
THETA = 10000.0

@jax.custom_vjp
def low(v):
    return lax.optimization_barrier(v.astype(jnp.bfloat16)).astype(jnp.float32)

@jax.custom_vjp
def low_back(v):
    return v

def low_keep(v):
    return (low(v), None)

def low_pass(kept, grad):
    return (grad,)

def back_keep(v):
    return (v, None)

def back_low(kept, grad):
    return (low(grad),)
low.defvjp(low_keep, low_pass)
low_back.defvjp(back_keep, back_low)

def product(left, right):
    return jnp.dot(left, right, precision=lax.Precision.HIGHEST)

def layer_norm(values, gain, offset):
    centred = values - lax.optimization_barrier(jnp.mean(values, axis=-1, keepdims=True))
    inverse = lax.rsqrt(lax.optimization_barrier(jnp.mean(centred * centred, axis=-1, keepdims=True)) + EPSILON)
    return centred * inverse * gain + offset

def rope_tables(length, head_size):
    quarter = head_size // 4
    position = jnp.arange(length)
    row_index = (position // GRID_W).astype(jnp.float32)
    col_index = (position % GRID_W).astype(jnp.float32)
    inverse = THETA ** (-2.0 * jnp.arange(quarter).astype(jnp.float32) / (head_size // 2))
    angles = jnp.stack([row_index[:, None] * inverse, col_index[:, None] * inverse], axis=1)
    return (jnp.cos(angles)[:, :, None, :], jnp.sin(angles)[:, :, None, :])

def apply_rotary_embedding(values, rotary_cosine_values, rotary_sine_values, direction):
    value_shape = values.shape
    quarter = value_shape[-1] // 4
    halves = values.reshape(value_shape[:-1] + (2, 2, quarter))
    spread = (value_shape[0],) + (1,) * (len(value_shape) - 2) + (2, 1, quarter)
    swapped = jnp.stack([-halves[..., 1, :], halves[..., 0, :]], axis=-2)
    turned = halves * rotary_cosine_values.reshape(spread) + direction * swapped * rotary_sine_values.reshape(spread)
    return turned.reshape(value_shape)

def attend(query, keys, values):
    scores = low_back(jnp.einsum('qhd,khd->hqk', query, keys, precision=lax.Precision.HIGHEST))
    row_max = lax.optimization_barrier(jnp.max(scores, axis=-1, keepdims=True))
    exponent = jnp.exp(scores - row_max)
    shares = low(exponent / lax.optimization_barrier(jnp.sum(exponent, axis=-1, keepdims=True)))
    mixture = jnp.einsum('hqk,khd->qhd', shares, values, precision=lax.Precision.HIGHEST)
    return low(low_back(mixture))

def block(latent_rows, skip_rows, text_rows, embedding, merger, modulator, gains, biases, output_bias, projector, combiner, cross_query, cross_memory, blender, expander, reducer, column_biases, hidden_bias, per_head_norm_gains, head_shifts):
    length, model_width = latent_rows.shape
    text_width = text_rows.shape[1]
    heads = model_width // HD
    softmax_scale = HD ** (-0.5)
    rotary_cosine_values, rotary_sine_values = rope_tables(length, HD)
    joined = jnp.concatenate([latent_rows, skip_rows], axis=1)
    merge_in = low(layer_norm(joined, jnp.concatenate([gains[0], gains[1]]), jnp.concatenate([biases[0], biases[1]])))
    first = low_back(product(merge_in, merger) + biases[5])
    modulation = product(low(jax.nn.silu(embedding))[None, :], modulator) + biases[6]
    self_in = low(layer_norm(first, gains[2], biases[2]) + modulation)
    packed = low_back(product(self_in, projector.reshape(model_width, 3 * model_width)).reshape(length, 3, model_width) + column_biases[None, 0:3])
    query = layer_norm(packed[:, 0].reshape(length, heads, HD), per_head_norm_gains[0], head_shifts[0])
    keys = layer_norm(packed[:, 1].reshape(length, heads, HD), per_head_norm_gains[1], head_shifts[1])
    query = low(apply_rotary_embedding(query, rotary_cosine_values, rotary_sine_values, 1.0) * softmax_scale)
    keys = low(apply_rotary_embedding(keys, rotary_cosine_values, rotary_sine_values, 1.0))
    values = low(packed[:, 2].reshape(length, heads, HD))
    attended = attend(query, keys, values).reshape(length, model_width)
    second = first + low_back(product(attended, combiner) + biases[7])
    cross_in = low(layer_norm(second, gains[3], biases[3]))
    cross_pre = low_back(product(cross_in, cross_query) + column_biases[3])
    cross_q = low(layer_norm(cross_pre.reshape(length, heads, HD), per_head_norm_gains[2], head_shifts[2]) * softmax_scale)
    text_len = text_rows.shape[0]
    memory = low_back(product(text_rows, cross_memory.reshape(text_width, 2 * model_width)).reshape(text_len, 2, model_width) + column_biases[None, 4:6])
    memory_keys = low(layer_norm(memory[:, 0].reshape(text_len, heads, HD), per_head_norm_gains[3], 0.0))
    memory_values = low(memory[:, 1].reshape(text_len, heads, HD))
    crossed = attend(cross_q, memory_keys, memory_values).reshape(length, model_width)
    third = second + low_back(product(crossed, blender) + biases[8])
    ffn_in = low(layer_norm(third, gains[4], biases[4]))
    hidden = low_back(product(ffn_in, expander) + hidden_bias)
    active = low(jax.nn.gelu(hidden, approximate=True))
    return third + product(active, reducer) + output_bias

def reference(latents, skips, text_states, time_embedding, merger, modulator, norm_gains, norm_biases, output_bias, projector, combiner, cross_query, cross_memory, blender, expander, reducer, column_biases, hidden_bias, per_head_norm_gains, head_shifts, cotangent):
    weights = tuple((weight.astype(jnp.float32) for weight in (merger, modulator, norm_gains, norm_biases, output_bias, projector, combiner, cross_query, cross_memory, blender, expander, reducer, column_biases, hidden_bias, per_head_norm_gains, head_shifts)))
    scan_items = (jnp.transpose(latents, (1, 0, 2)).astype(jnp.float32), jnp.transpose(skips, (1, 0, 2)).astype(jnp.float32), text_states.astype(jnp.float32), time_embedding.astype(jnp.float32), jnp.transpose(cotangent, (1, 0, 2)).astype(jnp.float32))

    def one_latent(totals, scan_item):
        latent_rows, skip_rows, text_rows, embedding, grad_out = scan_item
        result, pull = jax.vjp(block, latent_rows, skip_rows, text_rows, embedding, *weights)
        gradients = pull(grad_out)
        totals = tuple((running + update for running, update in zip(totals, gradients[4:])))
        return (totals, (result, gradients[0], gradients[1], gradients[2], gradients[3]))
    starting = tuple((jnp.zeros(weight.shape, jnp.float32) for weight in weights))
    totals, (result, row_grads, skip_grads, text_grads, time_grads) = lax.scan(one_latent, starting, scan_items)
    return (jnp.transpose(result, (1, 0, 2)), jnp.transpose(row_grads, (1, 0, 2)), jnp.transpose(skip_grads, (1, 0, 2)), text_grads, time_grads, totals[0], totals[1], totals[2], totals[3], totals[4], totals[5], totals[6], totals[7], totals[8], totals[9], totals[10], totals[11], totals[12], totals[13], totals[14], totals[15])
```

```python
import functools

import jax
import jax.numpy as jnp
from jax import lax
from jax.experimental import pallas as pl
from jax.experimental.pallas import tpu as pltpu
from jax.sharding import Mesh, PartitionSpec as P

GRID_W = 32
EPSILON = 1e-06
THETA = 10000.0
F32 = jnp.float32
BF16 = jnp.bfloat16
VMEM_LIMIT = 62 * 1024 * 1024
MLP_CHUNKS = 3
QUERY_BLOCK = 512


def bits_of(size):
    return [1 << i for i in range(size.bit_length() - 1)]


def swap(value, axis, size, mask):
    return lax.ppermute(value, axis, [(i, i ^ mask) for i in range(size)])


def dot(left, right, left_dim, right_dim):
    return lax.dot_general(
        left, right, (((left_dim,), (right_dim,)), ((), ())), preferred_element_type=F32
    )


def params(count=1):
    return pltpu.CompilerParams(
        dimension_semantics=("arbitrary",) * count, vmem_limit_bytes=VMEM_LIMIT
    )


def whole(shape):
    zeros = (0,) * len(shape)
    return pl.BlockSpec(shape, lambda *_: zeros, pipeline_mode=pl.Buffered(1))


def per_step(shape):
    rest = (0,) * (len(shape) - 1)
    return pl.BlockSpec((1,) + tuple(shape[1:]), lambda i, *_: (i,) + rest)


def shape_of(shape, dtype):
    return jax.ShapeDtypeStruct(shape, dtype)


def head_norm(values):
    width = values.shape[-1]
    centred = values - jnp.sum(values, axis=-1, keepdims=True) * (1.0 / width)
    inverse = lax.rsqrt(
        jnp.sum(centred * centred, axis=-1, keepdims=True) * (1.0 / width) + EPSILON
    )
    return centred * inverse, inverse


def head_norm_back(grad, hat, inverse, gain):
    scale = 1.0 / grad.shape[-1]
    scaled = grad * gain
    first = jnp.sum(scaled, axis=-1, keepdims=True) * scale
    second = jnp.sum(scaled * hat, axis=-1, keepdims=True) * scale
    return inverse * (scaled - first - hat * second)


def half_turn(values):
    quarter = values.shape[-1] // 4
    part = [values[:, i * quarter : (i + 1) * quarter] for i in range(4)]
    return jnp.concatenate([part[1], part[0], part[3], part[2]], axis=1)


def assemble(target, pieces, chip, rows):
    for k, piece in enumerate(pieces):
        start = pl.multiple_of((chip ^ k) * rows, 16)
        target[pl.ds(start, rows), :] = piece[0]


def scatter_pieces(source, pieces, chip, rows):
    for k, piece in enumerate(pieces):
        start = pl.multiple_of((chip ^ k) * rows, 16)
        piece[0] = source[pl.ds(start, rows), :]


def column_sum(values):
    return jnp.sum(values, axis=0, keepdims=True)


def self_forward_kernel(counts, chip_ref, *refs):
    chips, heads, size, own = counts
    refs = list(refs)
    take = lambda n: [refs.pop(0) for _ in range(n)]
    (x_ref,) = take(1)
    proj = take(chips)
    (bias_ref,) = take(1)
    comb = take(chips)
    gains, shifts, cosine, sine = take(4)
    low_ref, pre_ref, att_ref, lse_ref, own_ref, other_ref = take(6)
    wp, wc, acc = take(3)
    step = pl.program_id(0)
    chip = chip_ref[0]
    assemble(wp, proj, chip, proj[0].shape[1])
    assemble(wc, comb, chip, comb[0].shape[1])
    width = heads * size
    packed = dot(x_ref[...], wp[...], 1, 0) + bias_ref[0]
    pre_ref[0] = packed[:, : 2 * width].astype(BF16)
    value_low = packed[:, 2 * width :].astype(BF16)
    length = packed.shape[0]
    block = min(QUERY_BLOCK, length)
    cos, sin = cosine[...], sine[...]
    queries, keys, mixes, logs = [], [], [], []
    for h in range(heads):
        part = packed[:, h * size : (h + 1) * size]
        hat, _ = head_norm(part)
        turned = hat * gains[0:1, :] + shifts[0:1, :]
        query = ((turned * cos + half_turn(turned) * sin) * (size**-0.5)).astype(BF16)
        part = packed[:, width + h * size : width + (h + 1) * size]
        hat, _ = head_norm(part)
        turned = hat * gains[1:2, :] + shifts[1:2, :]
        key = (turned * cos + half_turn(turned) * sin).astype(BF16)
        value = value_low[:, h * size : (h + 1) * size]
        queries.append(query)
        keys.append(key)
        parts, sums = [], []
        for b in range(length // block):
            scores = dot(key, query[b * block : (b + 1) * block], 1, 1)
            top = jnp.max(scores, axis=0, keepdims=True)
            power = jnp.exp(scores - top)
            total = jnp.sum(power, axis=0, keepdims=True)
            shares = (power * (1.0 / total)).astype(BF16)
            parts.append(jnp.transpose(dot(value, shares, 0, 0)))
            sums.append(top + jnp.log(total))
        mixes.append(jnp.concatenate(parts, axis=0))
        logs.append(jnp.concatenate(sums, axis=1))
    low_ref[0] = jnp.concatenate(queries + keys + [value_low], axis=1)
    att = jnp.concatenate(mixes, axis=1).astype(BF16)
    att_ref[0] = att
    lse_ref[0] = jnp.concatenate(logs, axis=0)
    term = dot(att, wc[...], 1, 1)

    @pl.when(step == 0)
    def _():
        acc[...] = term

    @pl.when(step > 0)
    def _():
        acc[...] += term

    @pl.when(step == pl.num_programs(0) - 1)
    def _():
        own_ref[...] = acc[:own, :]
        other_ref[...] = acc[own:, :].astype(BF16)


def self_forward(chip, x, proj, bias, comb, gains, shifts, cosine, sine, own):
    length, width = x.shape
    groups, rows, cols = proj[0].shape
    size = gains.shape[1]
    heads = cols // (3 * size)
    chips = len(proj)
    small = heads * size
    return pl.pallas_call(
        functools.partial(self_forward_kernel, (chips, heads, size, own)),
        grid_spec=pltpu.PrefetchScalarGridSpec(
            num_scalar_prefetch=1,
            grid=(groups,),
            in_specs=[whole(x.shape)]
            + [per_step(p.shape) for p in proj]
            + [per_step(bias.shape)]
            + [per_step(p.shape) for p in comb]
            + [whole(gains.shape), whole(shifts.shape), whole(cosine.shape), whole(sine.shape)],
            out_specs=[
                per_step((groups, length, cols)),
                per_step((groups, length, 2 * small)),
                per_step((groups, length, small)),
                per_step((groups, heads, length)),
                whole((own, width)),
                whole((length - own, width)),
            ],
            scratch_shapes=[
                pltpu.VMEM((rows * chips, cols), BF16),
                pltpu.VMEM((rows * chips, small), BF16),
                pltpu.VMEM((length, width), F32),
            ],
        ),
        out_shape=[
            shape_of((groups, length, cols), BF16),
            shape_of((groups, length, 2 * small), BF16),
            shape_of((groups, length, small), BF16),
            shape_of((groups, heads, length), F32),
            shape_of((own, width), F32),
            shape_of((length - own, width), BF16),
        ],
        compiler_params=params(),
        name="self_forward",
    )(chip, x, *proj, bias, *comb, gains, shifts, cosine, sine)


def attention_back(query, key, value, out_grad, logs, block, limit=None):
    length = query.shape[0]
    key_grad, value_grad, query_parts = None, None, []
    for b in range(length // block):
        rows = slice(b * block, (b + 1) * block)
        query_part, grad_part = query[rows], out_grad[rows]
        scores = dot(key, query_part, 1, 1)
        shares = jnp.exp(scores - logs[:, rows])
        if limit is not None:
            index = lax.broadcasted_iota(jnp.int32, shares.shape, 0)
            shares = jnp.where(index < limit, shares, 0.0)
        share_grad = dot(value, grad_part, 1, 1)
        inner = jnp.sum(shares * share_grad, axis=0, keepdims=True)
        score_grad = (shares * (share_grad - inner)).astype(BF16)
        query_parts.append(jnp.transpose(dot(key, score_grad, 0, 0)))
        key_term = dot(score_grad, query_part, 1, 0)
        value_term = dot(shares.astype(BF16), grad_part, 1, 0)
        key_grad = key_term if b == 0 else key_grad + key_term
        value_grad = value_term if b == 0 else value_grad + value_term
    return jnp.concatenate(query_parts, axis=0), key_grad, value_grad


def self_backward_kernel(counts, chip_ref, *refs):
    chips, heads, size, own = counts
    refs = list(refs)
    take = lambda n: [refs.pop(0) for _ in range(n)]
    x_ref, grad_ref = take(2)
    proj = take(chips)
    comb = take(chips)
    low_ref, pre_ref, att_ref, lse_ref = take(4)
    gains, cosine, sine = take(3)
    proj_out = take(chips)
    comb_out = take(chips)
    own_ref, other_ref, column_ref, head_ref = take(4)
    wp, wc, acc, grad_t, x_t = take(5)
    step = pl.program_id(0)
    chip = chip_ref[0]
    rows = proj[0].shape[1]
    assemble(wp, proj, chip, rows)
    assemble(wc, comb, chip, rows)
    width = heads * size
    scale = size**-0.5

    @pl.when(step == 0)
    def _():
        grad_t[...] = jnp.transpose(grad_ref[...])
        x_t[...] = jnp.transpose(x_ref[...])

    out_grad = dot(grad_ref[...], wc[...], 1, 0).astype(BF16)
    wc[...] = dot(grad_t[...], att_ref[0], 1, 0).astype(BF16)
    scatter_pieces(wc, comb_out, chip, rows)
    cos, sin = cosine[...], sine[...]
    block = min(QUERY_BLOCK, out_grad.shape[0])
    query_grads, key_grads, value_grads = [], [], []
    sums = [None] * 4
    for h in range(heads):
        cut = lambda ref, part: ref[0, :, part * width + h * size : part * width + (h + 1) * size]
        query, key, value = cut(low_ref, 0), cut(low_ref, 1), cut(low_ref, 2)
        dq, dk, dv = attention_back(
            query, key, value, out_grad[:, h * size : (h + 1) * size], lse_ref[0, h : h + 1, :], block
        )
        dq = dq * scale
        dq = dq * cos - half_turn(dq) * sin
        dk = dk * cos - half_turn(dk) * sin
        q_hat, q_inverse = head_norm(cut(pre_ref, 0).astype(F32))
        k_hat, k_inverse = head_norm(cut(pre_ref, 1).astype(F32))
        terms = [column_sum(dq * q_hat), column_sum(dk * k_hat), column_sum(dq), column_sum(dk)]
        sums = terms if h == 0 else [s + t for s, t in zip(sums, terms)]
        query_grads.append(head_norm_back(dq, q_hat, q_inverse, gains[0:1, :]))
        key_grads.append(head_norm_back(dk, k_hat, k_inverse, gains[1:2, :]))
        value_grads.append(dv)
    packed = jnp.concatenate(query_grads + key_grads + value_grads, axis=1).astype(BF16)
    column_ref[0] = column_sum(packed.astype(F32))
    term = dot(packed, wp[...], 1, 1)
    wp[...] = dot(x_t[...], packed, 1, 0).astype(BF16)
    scatter_pieces(wp, proj_out, chip, rows)
    head_sums = jnp.concatenate(sums, axis=0)

    @pl.when(step == 0)
    def _():
        acc[...] = term
        head_ref[...] = head_sums

    @pl.when(step > 0)
    def _():
        acc[...] += term
        head_ref[...] += head_sums

    @pl.when(step == pl.num_programs(0) - 1)
    def _():
        own_ref[...] = acc[:own, :]
        other_ref[...] = acc[own:, :].astype(BF16)


def self_backward(chip, x, grad, proj, comb, low, pre, att, lse, gains, cosine, sine, own):
    length, width = x.shape
    groups, rows, cols = proj[0].shape
    size = gains.shape[1]
    heads = cols // (3 * size)
    chips = len(proj)
    small = heads * size
    out = pl.pallas_call(
        functools.partial(self_backward_kernel, (chips, heads, size, own)),
        grid_spec=pltpu.PrefetchScalarGridSpec(
            num_scalar_prefetch=1,
            grid=(groups,),
            in_specs=[whole(x.shape), whole(grad.shape)]
            + [per_step(p.shape) for p in proj]
            + [per_step(p.shape) for p in comb]
            + [per_step(v.shape) for v in (low, pre, att, lse)]
            + [whole(gains.shape), whole(cosine.shape), whole(sine.shape)],
            out_specs=[per_step(p.shape) for p in proj]
            + [per_step(p.shape) for p in comb]
            + [
                whole((own, width)),
                whole((length - own, width)),
                per_step((groups, 1, cols)),
                whole((4, size)),
            ],
            scratch_shapes=[
                pltpu.VMEM((rows * chips, cols), BF16),
                pltpu.VMEM((rows * chips, small), BF16),
                pltpu.VMEM((length, width), F32),
                pltpu.VMEM((width, length), BF16),
                pltpu.VMEM((width, length), BF16),
            ],
        ),
        out_shape=[shape_of(p.shape, BF16) for p in proj]
        + [shape_of(p.shape, BF16) for p in comb]
        + [
            shape_of((own, width), F32),
            shape_of((length - own, width), BF16),
            shape_of((groups, 1, cols), F32),
            shape_of((4, size), F32),
        ],
        compiler_params=params(),
        name="self_backward",
    )(chip, x, grad, *proj, *comb, low, pre, att, lse, gains, cosine, sine)
    return out[:chips], out[chips : 2 * chips], *out[2 * chips :]


def cross_forward_kernel(counts, chip_ref, *refs):
    chips, heads, size, own, limit = counts
    refs = list(refs)
    take = lambda n: [refs.pop(0) for _ in range(n)]
    x_ref, text_ref = take(2)
    query_w = take(chips)
    memory_w = take(chips)
    blend = take(chips)
    bias_ref, memory_bias, gains, shifts = take(4)
    low_ref, pre_ref, memory_ref, memory_pre, att_ref, lse_ref, own_ref, other_ref = take(8)
    wq, wm, wb, acc = take(4)
    step = pl.program_id(0)
    chip = chip_ref[0]
    assemble(wq, query_w, chip, query_w[0].shape[1])
    assemble(wm, memory_w, chip, memory_w[0].shape[1])
    assemble(wb, blend, chip, blend[0].shape[1])
    width = heads * size
    pre = dot(x_ref[...], wq[...], 1, 0) + bias_ref[0]
    memory = dot(text_ref[...], wm[...], 1, 0) + memory_bias[0]
    pre_ref[0] = pre.astype(BF16)
    memory_pre[0] = memory[:, :width].astype(BF16)
    value_low = memory[:, width:].astype(BF16)
    length = pre.shape[0]
    block = min(QUERY_BLOCK, length)
    queries, keys, mixes, logs = [], [], [], []
    for h in range(heads):
        cols = slice(h * size, (h + 1) * size)
        hat, _ = head_norm(pre[:, cols])
        query = ((hat * gains[2:3, :] + shifts[2:3, :]) * (size**-0.5)).astype(BF16)
        hat, _ = head_norm(memory[:, cols])
        key = (hat * gains[3:4, :]).astype(BF16)
        value = value_low[:, cols]
        queries.append(query)
        keys.append(key)
        parts, sums = [], []
        for b in range(length // block):
            scores = dot(key, query[b * block : (b + 1) * block], 1, 1)
            index = lax.broadcasted_iota(jnp.int32, scores.shape, 0)
            scores = jnp.where(index < limit, scores, -jnp.inf)
            top = jnp.max(scores, axis=0, keepdims=True)
            power = jnp.exp(scores - top)
            total = jnp.sum(power, axis=0, keepdims=True)
            shares = (power * (1.0 / total)).astype(BF16)
            parts.append(jnp.transpose(dot(value, shares, 0, 0)))
            sums.append(top + jnp.log(total))
        mixes.append(jnp.concatenate(parts, axis=0))
        logs.append(jnp.concatenate(sums, axis=1))
    low_ref[0] = jnp.concatenate(queries, axis=1)
    memory_ref[0] = jnp.concatenate(keys + [value_low], axis=1)
    att = jnp.concatenate(mixes, axis=1).astype(BF16)
    att_ref[0] = att
    lse_ref[0] = jnp.concatenate(logs, axis=0)
    term = dot(att, wb[...], 1, 1)

    @pl.when(step == 0)
    def _():
        acc[...] = term

    @pl.when(step > 0)
    def _():
        acc[...] += term

    @pl.when(step == pl.num_programs(0) - 1)
    def _():
        own_ref[...] = acc[:own, :]
        other_ref[...] = acc[own:, :].astype(BF16)


def cross_forward(chip, x, text, query_w, memory_w, blend, bias, memory_bias, gains, shifts, own, limit):
    length, width = x.shape
    groups, rows, small = query_w[0].shape
    text_rows = text.shape[0]
    memory_rows = memory_w[0].shape[1]
    size = gains.shape[1]
    heads = small // size
    chips = len(query_w)
    saved = [
        ((groups, length, small), BF16),
        ((groups, length, small), BF16),
        ((groups, text_rows, 2 * small), BF16),
        ((groups, text_rows, small), BF16),
        ((groups, length, small), BF16),
        ((groups, heads, length), F32),
    ]
    return pl.pallas_call(
        functools.partial(cross_forward_kernel, (chips, heads, size, own, limit)),
        grid_spec=pltpu.PrefetchScalarGridSpec(
            num_scalar_prefetch=1,
            grid=(groups,),
            in_specs=[whole(x.shape), whole(text.shape)]
            + [per_step(p.shape) for p in (*query_w, *memory_w, *blend)]
            + [per_step(bias.shape), per_step(memory_bias.shape), whole(gains.shape), whole(shifts.shape)],
            out_specs=[per_step(s) for s, _ in saved]
            + [whole((own, width)), whole((length - own, width))],
            scratch_shapes=[
                pltpu.VMEM((rows * chips, small), BF16),
                pltpu.VMEM((memory_rows * chips, 2 * small), BF16),
                pltpu.VMEM((rows * chips, small), BF16),
                pltpu.VMEM((length, width), F32),
            ],
        ),
        out_shape=[shape_of(*s) for s in saved]
        + [shape_of((own, width), F32), shape_of((length - own, width), BF16)],
        compiler_params=params(),
        name="cross_forward",
    )(chip, x, text, *query_w, *memory_w, *blend, bias, memory_bias, gains, shifts)


def cross_backward_kernel(counts, chip_ref, *refs):
    chips, heads, size, own, limit = counts
    refs = list(refs)
    take = lambda n: [refs.pop(0) for _ in range(n)]
    x_ref, grad_ref, text_ref = take(3)
    query_w = take(chips)
    memory_w = take(chips)
    blend = take(chips)
    low_ref, pre_ref, memory_ref, memory_pre, att_ref, lse_ref = take(6)
    (gains,) = take(1)
    query_out = take(chips)
    memory_out = take(chips)
    blend_out = take(chips)
    own_ref, other_ref, text_out, column_ref, memory_column, head_ref = take(6)
    wq, wm, wb, acc, grad_t, x_t, text_t = take(7)
    step = pl.program_id(0)
    chip = chip_ref[0]
    rows, memory_rows = query_w[0].shape[1], memory_w[0].shape[1]
    assemble(wq, query_w, chip, rows)
    assemble(wm, memory_w, chip, memory_rows)
    assemble(wb, blend, chip, rows)
    width = heads * size
    scale = size**-0.5

    @pl.when(step == 0)
    def _():
        grad_t[...] = jnp.transpose(grad_ref[...])
        x_t[...] = jnp.transpose(x_ref[...])
        text_t[...] = jnp.transpose(text_ref[...])

    out_grad = dot(grad_ref[...], wb[...], 1, 0).astype(BF16)
    wb[...] = dot(grad_t[...], att_ref[0], 1, 0).astype(BF16)
    scatter_pieces(wb, blend_out, chip, rows)
    block = min(QUERY_BLOCK, out_grad.shape[0])
    query_grads, key_grads, value_grads = [], [], []
    sums = [None] * 3
    for h in range(heads):
        cols = slice(h * size, (h + 1) * size)
        query = low_ref[0, :, cols]
        key = memory_ref[0, :, cols]
        value = memory_ref[0, :, width + h * size : width + (h + 1) * size]
        dq, dk, dv = attention_back(
            query, key, value, out_grad[:, cols], lse_ref[0, h : h + 1, :], block, limit
        )
        dq = dq * scale
        q_hat, q_inverse = head_norm(pre_ref[0, :, cols].astype(F32))
        k_hat, k_inverse = head_norm(memory_pre[0, :, cols].astype(F32))
        terms = [column_sum(dq * q_hat), column_sum(dk * k_hat), column_sum(dq)]
        sums = terms if h == 0 else [s + t for s, t in zip(sums, terms)]
        query_grads.append(head_norm_back(dq, q_hat, q_inverse, gains[2:3, :]))
        key_grads.append(head_norm_back(dk, k_hat, k_inverse, gains[3:4, :]))
        value_grads.append(dv)
    packed = jnp.concatenate(query_grads, axis=1).astype(BF16)
    memory_grad = jnp.concatenate(key_grads + value_grads, axis=1).astype(BF16)
    column_ref[0] = column_sum(packed.astype(F32))
    memory_column[0] = column_sum(memory_grad.astype(F32))
    term = dot(packed, wq[...], 1, 1)
    text_term = dot(memory_grad, wm[...], 1, 1)
    wq[...] = dot(x_t[...], packed, 1, 0).astype(BF16)
    scatter_pieces(wq, query_out, chip, rows)
    wm[...] = dot(text_t[...], memory_grad, 1, 0).astype(BF16)
    scatter_pieces(wm, memory_out, chip, memory_rows)
    head_sums = jnp.concatenate(sums, axis=0)

    @pl.when(step == 0)
    def _():
        acc[...] = term
        text_out[...] = text_term
        head_ref[...] = head_sums

    @pl.when(step > 0)
    def _():
        acc[...] += term
        text_out[...] += text_term
        head_ref[...] += head_sums

    @pl.when(step == pl.num_programs(0) - 1)
    def _():
        own_ref[...] = acc[:own, :]
        other_ref[...] = acc[own:, :].astype(BF16)


def cross_backward(
    chip, x, grad, text, query_w, memory_w, blend, low, pre, memory, memory_pre, att, lse, gains, own, limit
):
    length, width = x.shape
    groups, rows, small = query_w[0].shape
    memory_rows = memory_w[0].shape[1]
    size = gains.shape[1]
    heads = small // size
    chips = len(query_w)
    pieces = (*query_w, *memory_w, *blend)
    tail = [
        ((own, width), F32, False),
        ((length - own, width), BF16, False),
        (text.shape, F32, False),
        ((groups, 1, small), F32, True),
        ((groups, 1, 2 * small), F32, True),
        ((3, size), F32, False),
    ]
    out = pl.pallas_call(
        functools.partial(cross_backward_kernel, (chips, heads, size, own, limit)),
        grid_spec=pltpu.PrefetchScalarGridSpec(
            num_scalar_prefetch=1,
            grid=(groups,),
            in_specs=[whole(x.shape), whole(grad.shape), whole(text.shape)]
            + [per_step(p.shape) for p in pieces]
            + [per_step(v.shape) for v in (low, pre, memory, memory_pre, att, lse)]
            + [whole(gains.shape)],
            out_specs=[per_step(p.shape) for p in pieces]
            + [per_step(s) if stepped else whole(s) for s, _, stepped in tail],
            scratch_shapes=[
                pltpu.VMEM((rows * chips, small), BF16),
                pltpu.VMEM((memory_rows * chips, 2 * small), BF16),
                pltpu.VMEM((rows * chips, small), BF16),
                pltpu.VMEM((length, width), F32),
                pltpu.VMEM((width, length), BF16),
                pltpu.VMEM((width, length), BF16),
                pltpu.VMEM((text.shape[1], text.shape[0]), BF16),
            ],
        ),
        out_shape=[shape_of(p.shape, BF16) for p in pieces] + [shape_of(s, d) for s, d, _ in tail],
        compiler_params=params(),
        name="cross_backward",
    )(chip, x, grad, text, *pieces, low, pre, memory, memory_pre, att, lse, gains)
    return out[:chips], out[chips : 2 * chips], out[2 * chips : 3 * chips], *out[3 * chips :]


def mlp_kernel(counts, chip_ref, *refs):
    chips, own = counts
    refs = list(refs)
    take = lambda n: [refs.pop(0) for _ in range(n)]
    x_ref, cot_ref, x_t, cot_t = take(4)
    weights = take(chips)
    (bias_ref,) = take(1)
    grads = take(chips)
    out_own, out_other, back_own, back_other, hidden_ref = take(5)
    w, acc, back = take(3)
    step = pl.program_id(0)
    chip = chip_ref[0]
    rows = weights[0].shape[1]
    assemble(w, weights, chip, rows)
    tile = w.shape[1] // 2
    hidden = dot(x_ref[...], w[:, :tile], 1, 0) + bias_ref[0]
    square = hidden * hidden
    inner = 0.7978845608028654 * hidden * (1.0 + 0.044715 * square)
    curve = jnp.tanh(inner)
    active = (0.5 * hidden * (1.0 + curve)).astype(BF16)
    slope = 0.5 * (1.0 + curve) + 0.5 * hidden * (1.0 - curve * curve) * (
        0.7978845608028654 * (1.0 + 3 * 0.044715 * square)
    )
    hidden_grad = dot(cot_ref[...], w[:, tile:], 1, 0) * slope
    hidden_grad = hidden_grad.astype(BF16)
    hidden_ref[0] = column_sum(hidden_grad.astype(F32))
    out_term = dot(active, w[:, tile:], 1, 1)
    back_term = dot(hidden_grad, w[:, :tile], 1, 1)

    @pl.when(step == 0)
    def _():
        acc[...] = out_term
        back[...] = back_term

    @pl.when(step > 0)
    def _():
        acc[...] += out_term
        back[...] += back_term

    w[:, :tile] = dot(x_t[...], hidden_grad, 1, 0).astype(BF16)
    w[:, tile:] = dot(cot_t[...], active, 1, 0).astype(BF16)
    scatter_pieces(w, grads, chip, rows)

    @pl.when(step == pl.num_programs(0) - 1)
    def _():
        out_own[...] = acc[:own, :]
        out_other[...] = acc[own:, :].astype(BF16)
        back_own[...] = back[:own, :]
        back_other[...] = back[own:, :].astype(BF16)


def mlp(chip, x, cot, x_t, cot_t, weights, bias, own):
    length, width = x.shape
    groups, rows, cols = weights[0].shape
    chips = len(weights)
    tail = [((own, width), F32), ((length - own, width), BF16)] * 2
    out = pl.pallas_call(
        functools.partial(mlp_kernel, (chips, own)),
        grid_spec=pltpu.PrefetchScalarGridSpec(
            num_scalar_prefetch=1,
            grid=(groups,),
            in_specs=[whole(v.shape) for v in (x, cot, x_t, cot_t)]
            + [per_step(p.shape) for p in weights]
            + [per_step(bias.shape)],
            out_specs=[per_step(p.shape) for p in weights]
            + [whole(s) for s, _ in tail]
            + [per_step(bias.shape)],
            scratch_shapes=[
                pltpu.VMEM((rows * chips, cols), BF16),
                pltpu.VMEM((length, width), F32),
                pltpu.VMEM((length, width), F32),
            ],
        ),
        out_shape=[shape_of(p.shape, BF16) for p in weights]
        + [shape_of(*s) for s in tail]
        + [shape_of(bias.shape, F32)],
        compiler_params=params(),
        name="mlp",
    )(chip, x, cot, x_t, cot_t, *weights, bias)
    return out[:chips], *out[chips:]


def row_spec(block, width):
    return pl.BlockSpec((block, width), lambda i, *_: (i, 0))


def merge_kernel(count, index_ref, *refs):
    refs = list(refs)
    take = lambda n: [refs.pop(0) for _ in range(n)]
    latent_ref, skip_ref = take(2)
    pieces = take(count)
    gains, biases = take(2)
    out_ref, merger_ref = take(2)

    @pl.when(pl.program_id(0) == 0)
    def _():
        rows = pieces[0].shape[0]
        for k, piece in enumerate(pieces):
            start = pl.multiple_of((index_ref[0] ^ k) * rows, 16)
            merger_ref[pl.ds(start, rows), :] = piece[...]

    left, right, _ = joined_norm(latent_ref, skip_ref)
    width = left.shape[1]
    left = (left * gains[0:1, :] + biases[0:1, :]).astype(BF16)
    right = (right * gains[1:2, :] + biases[1:2, :]).astype(BF16)
    total = dot(left, merger_ref[:width, :], 1, 0) + dot(right, merger_ref[width:, :], 1, 0)
    out_ref[...] = (total + biases[5:6, :]).astype(BF16)


def joined_norm(latent_ref, skip_ref):
    left, right = latent_ref[...].astype(F32), skip_ref[...].astype(F32)
    scale = 0.5 / left.shape[1]
    mean = (jnp.sum(left, axis=-1, keepdims=True) + jnp.sum(right, axis=-1, keepdims=True)) * scale
    left, right = left - mean, right - mean
    spread = jnp.sum(left * left, axis=-1, keepdims=True) + jnp.sum(right * right, axis=-1, keepdims=True)
    inverse = lax.rsqrt(spread * scale + EPSILON)
    return left * inverse, right * inverse, inverse


def merge(index, latents, skips, pieces, gains, biases, block=128):
    rows, width = latents.shape
    return pl.pallas_call(
        functools.partial(merge_kernel, len(pieces)),
        grid_spec=pltpu.PrefetchScalarGridSpec(
            num_scalar_prefetch=1,
            grid=(rows // block,),
            in_specs=[row_spec(block, width)] * 2
            + [whole(p.shape) for p in pieces]
            + [whole(gains.shape), whole(biases.shape)],
            out_specs=[row_spec(block, width), whole((2 * width, width))],
        ),
        out_shape=[shape_of((rows, width), BF16), shape_of((2 * width, width), BF16)],
        compiler_params=params(),
        name="merge",
    )(index, latents, skips, *pieces, gains, biases)


def merge_back_kernel(latent_ref, skip_ref, low_ref, merger, gains, biases, left_out, right_out, merge_in, sums):
    left, right, inverse = joined_norm(latent_ref, skip_ref)
    width = left.shape[1]
    low = low_ref[...]
    scale = 0.5 / width
    left_grad = dot(low, merger[:width, :], 1, 1)
    right_grad = dot(low, merger[width:, :], 1, 1)
    merge_in[:, :width] = (left * gains[0:1, :] + biases[0:1, :]).astype(BF16)
    merge_in[:, width:] = (right * gains[1:2, :] + biases[1:2, :]).astype(BF16)
    terms = jnp.concatenate(
        [
            column_sum(left_grad * left),
            column_sum(right_grad * right),
            column_sum(left_grad),
            column_sum(right_grad),
            column_sum(low.astype(F32)),
        ],
        axis=0,
    )
    left_grad, right_grad = left_grad * gains[0:1, :], right_grad * gains[1:2, :]
    first = jnp.sum(left_grad, axis=-1, keepdims=True) + jnp.sum(right_grad, axis=-1, keepdims=True)
    second = jnp.sum(left_grad * left, axis=-1, keepdims=True) + jnp.sum(
        right_grad * right, axis=-1, keepdims=True
    )
    first, second = first * scale, second * scale
    left_out[...] = inverse * (left_grad - first - left * second)
    right_out[...] = inverse * (right_grad - first - right * second)

    @pl.when(pl.program_id(0) == 0)
    def _():
        sums[...] = terms

    @pl.when(pl.program_id(0) > 0)
    def _():
        sums[...] += terms


def merge_back(latents, skips, low, merger, gains, biases, block=128):
    rows, width = latents.shape
    return pl.pallas_call(
        merge_back_kernel,
        grid=(rows // block,),
        in_specs=[row_spec(block, width)] * 3
        + [whole(merger.shape), whole(gains.shape), whole(biases.shape)],
        out_specs=[row_spec(block, width)] * 2 + [row_spec(block, 2 * width), whole((5, width))],
        out_shape=[
            shape_of((rows, width), F32),
            shape_of((rows, width), F32),
            shape_of((rows, 2 * width), BF16),
            shape_of((5, width), F32),
        ],
        compiler_params=params(),
        name="merge_back",
    )(latents, skips, low, merger, gains, biases)


def norm_kernel(count, keep, *refs):
    parts, rows, outs = refs[:count], refs[count], refs[count + 1 :]
    total = parts[0][...].astype(F32)
    for part in parts[1:]:
        total = total + part[...].astype(F32)
    total = total + rows[0:1, :]
    hat, _ = head_norm(total)
    outs[0][...] = (hat * rows[1:2, :] + rows[2:3, :]).astype(BF16)
    if keep:
        outs[1][...] = total


def norm(parts, rows, keep=True, block=128):
    length, width = parts[0].shape
    out = pl.pallas_call(
        functools.partial(norm_kernel, len(parts), keep),
        grid=(length // block,),
        in_specs=[row_spec(block, width)] * len(parts) + [whole(rows.shape)],
        out_specs=[row_spec(block, width)] * (1 + keep),
        out_shape=[shape_of((length, width), BF16)] + [shape_of((length, width), F32)] * keep,
        compiler_params=params(),
        name="norm",
    )(*parts, rows)
    return out if keep else out[0]


def norm_back_kernel(count, keep, *refs):
    parts, value_ref, carried, gain = refs[:count], refs[count], refs[count + 1], refs[count + 2]
    outs = refs[count + 3 :]
    grad = parts[0][...].astype(F32)
    for part in parts[1:]:
        grad = grad + part[...].astype(F32)
    hat, inverse = head_norm(value_ref[...].astype(F32))
    total = carried[...].astype(F32) + head_norm_back(grad, hat, inverse, gain[...])
    low = total.astype(BF16)
    outs[0][...] = low
    if keep:
        outs[2][...] = total
    terms = jnp.concatenate(
        [column_sum(grad * hat), column_sum(grad), column_sum(low.astype(F32))], axis=0
    )
    sums = outs[1]

    @pl.when(pl.program_id(0) == 0)
    def _():
        sums[...] = terms

    @pl.when(pl.program_id(0) > 0)
    def _():
        sums[...] += terms


def norm_back(parts, value, carried, gain, keep=True, block=128):
    length, width = value.shape
    return pl.pallas_call(
        functools.partial(norm_back_kernel, len(parts), keep),
        grid=(length // block,),
        in_specs=[row_spec(block, width)] * (len(parts) + 2) + [whole(gain.shape)],
        out_specs=[row_spec(block, width), whole((3, width))] + [row_spec(block, width)] * keep,
        out_shape=[shape_of((length, width), BF16), shape_of((3, width), F32)]
        + [shape_of((length, width), F32)] * keep,
        compiler_params=params(),
        name="norm_back",
    )(*parts, value, carried, gain)


class Links:
    def __init__(self, depth):
        self.depth = depth
        self.sent = {}

    def swap(self, value, axis, size, mask):
        sent = self.sent.setdefault((axis, mask if axis == "chip" else 0), [])
        if len(sent) >= self.depth:
            value, _ = lax.optimization_barrier((value, sent[-self.depth]))
        value = swap(value, axis, size, mask)
        sent.append(value)
        return value


def body(sizes, latents, skips, text_states, time_embedding, merger, modulator, norm_gains, norm_biases,
         output_bias, projector, combiner, cross_query, cross_memory, blender, expander, reducer,
         column_biases, hidden_bias, per_head_norm_gains, head_shifts, cotangent):
    chips, wide, deep = sizes
    chip_index, core, lane, side = (lax.axis_index(n) for n in ("chip", "core", "ta", "tb"))
    shard_len, local, width = latents.shape
    size = per_head_norm_gains.shape[1]
    text_len, text_width = text_states.shape[1:]
    own_len = shard_len * local
    seq_len = shard_len * wide * deep
    devices = chips * 2 * wide * deep
    latent_total = chips * 2 * local
    half_len = shard_len // 2
    tensor_cols = projector.shape[2]
    head_cols = tensor_cols // 2
    hidden_cols = expander.shape[1] // 2
    links = Links(2)
    chip_bits, wide_bits, deep_bits = bits_of(chips), bits_of(wide)[::-1], bits_of(deep)
    chip = chip_index.astype(jnp.int32).reshape(1)

    everywhere = [("ta", wide, b) for b in bits_of(wide)] + [("tb", deep, b) for b in deep_bits]
    everywhere = [("core", 2, 1)] + everywhere + [("chip", chips, b) for b in chip_bits]
    index_of = {"chip": chip_index, "core": core, "ta": lane, "tb": side}

    def at(value, index, axis=0):
        return lax.dynamic_index_in_dim(value, index, axis, keepdims=False)

    def gather_all(value):
        value = value[None, None, None, None]
        dims = {"chip": 0, "core": 1, "ta": 2, "tb": 3}
        shape = [1, 1, 1, 1]
        for axis, extent, mask in everywhere:
            value = value.reshape((*shape, *value.shape[4:]))
            other = swap(value, axis, extent, mask)
            high = (index_of[axis] & mask) > 0
            low_part = jnp.where(high, other, value)
            high_part = jnp.where(high, value, other)
            value = jnp.concatenate([low_part, high_part], axis=dims[axis])
            shape[dims[axis]] *= 2
        return value

    def sum_scatter_all(value):
        dims = {"chip": 0, "core": 1, "ta": 2, "tb": 3}
        for axis, extent, mask in everywhere[::-1]:
            dim = dims[axis]
            rows = value.shape[dim] // 2
            high = (index_of[axis] & mask) > 0
            low_part = lax.slice_in_dim(value, 0, rows, axis=dim)
            high_part = lax.slice_in_dim(value, rows, 2 * rows, axis=dim)
            kept = jnp.where(high, high_part, low_part)
            value = kept + swap(jnp.where(high, low_part, high_part), axis, extent, mask)
        return value.reshape(value.shape[4:])

    def halves(value):
        mine, other = at(value, core, 1), at(value, 1 - core, 1)
        other = swap(other, "core", 2, 1)
        pair = jnp.where(core == 0, jnp.stack([mine, other]), jnp.stack([other, mine]))
        return pair.reshape((-1,) + pair.shape[2:])

    def unhalves(value):
        value = value.reshape((2, -1) + value.shape[1:])
        mine, other = at(value, core), at(value, 1 - core)
        other = swap(other, "core", 2, 1)
        return jnp.where(core == 0, jnp.stack([mine, other], 1), jnp.stack([other, mine], 1))

    def gather_weight(value, order):
        value = value[None]
        count = 1
        value = value.reshape((1,) + value.shape)
        for mask in wide_bits:
            other = links.swap(value, "ta", wide, mask)
            value = jnp.stack([value, other], axis=2)
            count *= 2
            value = value.reshape((1, count) + value.shape[3:])
        pieces = {0: value[0]}
        for mask in order:
            for k in list(pieces):
                pieces[k ^ mask] = links.swap(pieces[k], "chip", chips, mask)
        return [pieces[k] for k in range(chips)]

    def scatter_weight(pieces, order):
        pieces = dict(enumerate(pieces))
        for mask in order[::-1]:
            for k in [k for k in pieces if k & mask]:
                received = swap(pieces.pop(k), "chip", chips, mask).astype(F32)
                near = pieces[k ^ mask].astype(F32) + received
                pieces[k ^ mask] = near if k == mask else near.astype(BF16)
        value = pieces[0].astype(F32)
        for mask in wide_bits[::-1]:
            value = value.reshape((value.shape[0] // 2, 2) + value.shape[1:])
            value = value[:, 0] + swap(value[:, 1].astype(BF16), "ta", wide, mask).astype(F32)
        return value[0]

    forth, back = chip_bits, chip_bits[::-1]

    small = jnp.concatenate(
        [v.reshape(-1) for v in (norm_gains, norm_biases, output_bias, column_biases, hidden_bias)]
    )
    small_all = gather_all(small).reshape(devices, -1)
    part = norm_gains.shape[1]
    hidden_part = hidden_bias.shape[0]
    table = jnp.transpose(small_all[:, : 21 * part].reshape(devices, 21, part), (1, 0, 2)).reshape(21, width)
    gains, biases, out_bias, columns = table[:5], table[5:14], table[14:15], table[15:21]
    hidden_all = small_all[:, 21 * part :].reshape(wide, deep, 2, hidden_cols)

    def own_columns(value):
        value = value.reshape(value.shape[0], wide, deep, 2, -1)
        value = at(at(value, side, 2), core, 2)
        return jnp.stack([at(value, lane ^ i, 1) for i in range(wide)])

    def all_columns(value):
        value = jnp.stack([at(value, lane ^ i) for i in range(wide)], axis=1)
        there = (jnp.arange(deep) == side)[:, None] & (jnp.arange(2) == core)[None, :]
        value = jnp.where(there[None, None, :, :, None], value[:, :, None, None, :], 0.0)
        return value.reshape(value.shape[0], -1)

    own_biases = own_columns(columns)

    rows = projector.shape[0]
    merger_z = merger[None]
    for mask in bits_of(wide):
        other = links.swap(merger_z, "ta", wide, mask)
        high = (lane & mask) > 0
        merger_z = jnp.concatenate(
            [jnp.where(high, other, merger_z), jnp.where(high, merger_z, other)], axis=0
        )
    merger_z = merger_z.reshape(wide, 1, *merger.shape)
    for mask in deep_bits:
        other = swap(merger_z, "tb", deep, mask)
        high = (side & mask) > 0
        merger_z = jnp.concatenate(
            [jnp.where(high, other, merger_z), jnp.where(high, merger_z, other)], axis=1
        )
    merger_z = merger_z.reshape(-1, width)
    merger_pieces = {0: merger_z}
    for mask in forth:
        for k in list(merger_pieces):
            merger_pieces[k ^ mask] = links.swap(merger_pieces[k], "chip", chips, mask)
    merger_list = []
    for k in range(chips):
        merger_list += [merger_pieces[k], swap(merger_pieces[k], "core", 2, 1)]

    projector_in = halves(projector.reshape(rows, 3, 2, head_cols).transpose(0, 2, 1, 3))
    projector_w = gather_weight(projector_in.reshape(2 * rows, 3 * head_cols), back)
    combiner_w = gather_weight(halves(combiner.T.reshape(rows, 2, head_cols)), forth)
    text_rows_w = cross_memory.shape[0]
    memory_in = halves(cross_memory.reshape(text_rows_w, 2, 2, head_cols).transpose(0, 2, 1, 3))
    memory_w = gather_weight(memory_in.reshape(2 * text_rows_w, 2 * head_cols), back)
    query_w = gather_weight(halves(cross_query.reshape(rows, 2, head_cols)), forth)
    blender_w = gather_weight(halves(blender.T.reshape(rows, 2, head_cols)), back)
    tile = hidden_cols // MLP_CHUNKS
    mlp_in = jnp.stack(
        [
            halves(expander.reshape(rows, 2, hidden_cols)),
            halves(reducer.T.reshape(rows, 2, hidden_cols)),
        ],
        axis=1,
    ).reshape(2 * rows, 2, MLP_CHUNKS, tile)
    mlp_orders = [forth if j % 2 == 0 else back for j in range(MLP_CHUNKS)]

    times = time_embedding
    silu_own = jax.nn.silu(times.astype(F32)).astype(BF16)
    silu_all = silu_own[None, None]
    silu_all = jnp.concatenate([silu_all, swap(silu_all, "core", 2, 1)], axis=1)
    silu_all = jnp.where(core == 0, silu_all, silu_all[:, ::-1])
    for mask in chip_bits:
        other = swap(silu_all, "chip", chips, mask)
        high = (chip_index & mask) > 0
        silu_all = jnp.concatenate(
            [jnp.where(high, other, silu_all), jnp.where(high, silu_all, other)], axis=0
        )
    silu_all = silu_all.reshape(latent_total, width)
    mod_rows = modulator.shape[0]
    device = ((chip_index * 2 + core) * wide + lane) * deep + side
    silu_cols = at(silu_all.reshape(latent_total, devices, mod_rows), device, 1)
    mod = jnp.dot(silu_cols, modulator, preferred_element_type=F32).reshape(chips, wide, width)
    for axis, extent, mask in [("chip", chips, b) for b in chip_bits[::-1]]:
        high = (chip_index & mask) > 0
        low_part, high_part = jnp.split(mod, 2, axis=0)
        mod = jnp.where(high, high_part, low_part) + swap(
            jnp.where(high, low_part, high_part), axis, extent, mask
        )
    for axis, extent, mask in [("ta", wide, b) for b in bits_of(wide)[::-1]]:
        high = (lane & mask) > 0
        low_part, high_part = jnp.split(mod, 2, axis=1)
        mod = jnp.where(high, high_part, low_part) + swap(
            jnp.where(high, low_part, high_part), axis, extent, mask
        )
    mod = mod.reshape(1, width)
    for axis, extent, mask in [("tb", deep, b) for b in deep_bits] + [("core", 2, 1)]:
        mod = mod + swap(mod, axis, extent, mask)

    def to_latent(value):
        value = value.reshape(local, 2, half_len, width)
        mine, other = at(value, core, 1), at(value, 1 - core, 1)
        other = swap(other, "core", 2, 1)
        pair = jnp.where(core == 0, jnp.stack([mine, other]), jnp.stack([other, mine]))
        return exchange(pair.reshape(wide, half_len, width)).reshape(own_len, width)

    def from_latent(value):
        pair = exchange(value.reshape(wide, half_len, width)).reshape(2, local, half_len, width)
        mine, other = at(pair, core), at(pair, 1 - core)
        other = swap(other, "core", 2, 1)
        value = jnp.where(core == 0, jnp.stack([mine, other], 1), jnp.stack([other, mine], 1))
        return value.reshape(own_len, width)

    def exchange(value):
        own = at(value, lane)
        parts = [own] + [
            swap(at(value, lane ^ mask), "ta", wide, mask) for mask in range(1, wide)
        ]
        parts = jnp.stack(parts)
        return jnp.stack([at(parts, lane ^ i) for i in range(wide)])

    def gather_tokens(value):
        value = jnp.concatenate([value, swap(value, "core", 2, 1)], axis=0)
        for mask in deep_bits:
            value = jnp.concatenate([value, swap(value, "tb", deep, mask)], axis=0)
        return value

    def scatter_tokens(other):
        terms = []
        rest = other
        for mask in deep_bits[::-1]:
            rows_sent = (own_len * 2 * deep) // 2
            kept = rest.shape[0] - rows_sent
            received = swap(rest[kept:], "tb", deep, mask)
            terms.append(received[:own_len])
            rest = (rest[:kept].astype(F32) + received[own_len:].astype(F32)).astype(BF16)
        terms.append(swap(rest, "core", 2, 1))
        return terms

    latents_flat = jnp.transpose(latents, (1, 0, 2)).reshape(own_len, width)
    skips_flat = jnp.transpose(skips, (1, 0, 2)).reshape(own_len, width)
    merge_index = (chip_index * 2 + core).astype(jnp.int32).reshape(1)
    first_local, merger_full = merge(merge_index, latents_flat, skips_flat, merger_list, gains, biases)
    first = to_latent(first_local)
    cot = to_latent(jnp.transpose(cotangent, (1, 0, 2)))
    cot_all = gather_tokens(cot)

    block_index = jnp.arange(wide)[:, None]
    inside = jnp.arange(half_len)[None, :]
    places = []
    for b in range(deep):
        for c in range(2):
            slot = (block_index * deep + (side ^ b)) * 2 + (core ^ c)
            places.append((slot * half_len + inside).reshape(-1))
    places = jnp.concatenate(places)
    quarter = size // 4
    frequency = THETA ** (-2.0 * jnp.arange(quarter).astype(F32) / (size // 2))
    row_angle = (places // GRID_W).astype(F32)[:, None] * frequency
    column_angle = (places % GRID_W).astype(F32)[:, None] * frequency
    angles = jnp.concatenate([row_angle, row_angle, column_angle, column_angle], axis=1)
    sign = jnp.where((jnp.arange(size) // quarter) % 2 == 0, -1.0, 1.0)
    cosine, sine = jnp.cos(angles), jnp.sin(angles) * sign

    zero_row = jnp.zeros((1, width), F32)
    rows_of = lambda *parts: jnp.concatenate(parts, axis=0)
    x_self = gather_tokens(
        norm([first], rows_of(zero_row, gains[2:3], biases[2:3] + biases[6:7] + mod), keep=False)
    )
    self_bias = own_biases[:, 0:3].reshape(wide, 1, 3 * head_cols)
    self_low, self_pre, self_att, self_lse, part_own, part_other = self_forward(
        chip, x_self, projector_w, self_bias, combiner_w, per_head_norm_gains, head_shifts, cosine, sine, own_len
    )
    x_cross, second = norm(
        [first, part_own, *scatter_tokens(part_other)], rows_of(biases[7:8], gains[3:4], biases[3:4])
    )
    x_cross = gather_tokens(x_cross)

    text_pad = -text_len % 16
    text_mine = at(text_states, lane % local)
    text_other = swap(text_mine, "core", 2, 1)
    text = jnp.where(core == lane // local, text_mine, text_other)
    text = jnp.pad(text, ((0, text_pad), (0, 0)))
    cross_bias = own_biases[:, 3:4]
    memory_bias = own_biases[:, 4:6].reshape(wide, 1, 2 * head_cols)
    cross_low, cross_pre, memory_low, memory_pre, cross_att, cross_lse, part_own, part_other = cross_forward(
        chip, x_cross, text, query_w, memory_w, blender_w, cross_bias, memory_bias,
        per_head_norm_gains, head_shifts, own_len, text_len,
    )
    x_mlp, third = norm(
        [second, part_own, *scatter_tokens(part_other)], rows_of(biases[8:9], gains[4:5], biases[4:5])
    )
    x_mlp = gather_tokens(x_mlp)

    own_hidden = at(at(hidden_all, side, 1), core, 1)
    own_hidden = jnp.stack([at(own_hidden, lane ^ i) for i in range(wide)]).reshape(wide, 1, MLP_CHUNKS, tile)
    x_t, cot_t = x_mlp.T, cot_all.T
    outs, backs, hidden_sums, mlp_grads = [third], [], [], []
    for j in range(MLP_CHUNKS):
        weights = gather_weight(mlp_in[:, :, j].reshape(2 * rows, 2 * tile), mlp_orders[j])
        grads, out_own, out_other, back_own, back_other, hidden_sum = mlp(
            chip, x_mlp, cot_all, x_t, cot_t, weights, own_hidden[:, :, j], own_len
        )
        mlp_grads.append(scatter_weight(grads, mlp_orders[j]))
        outs += [out_own, *scatter_tokens(out_other)]
        backs += [back_own, *scatter_tokens(back_other)]
        hidden_sums.append(hidden_sum)
    block_total = sum(v.astype(F32) for v in outs) + out_bias
    block_out = from_latent(block_total.astype(BF16))

    third_low, mlp_sums, third_grad = norm_back(backs, third, cot, gains[4:5])
    blender_g_in = gather_tokens(third_low)
    query_g, memory_g, blender_g, part_own, part_other, text_part, query_col, memory_col, cross_heads = (
        cross_backward(
            chip, x_cross, blender_g_in, text, query_w, memory_w, blender_w, cross_low, cross_pre,
            memory_low, memory_pre, cross_att, cross_lse, per_head_norm_gains, own_len, text_len,
        )
    )
    blender_grads = unhalves(scatter_weight(blender_g, back)).reshape(rows, tensor_cols).T
    query_grads = unhalves(scatter_weight(query_g, forth)).reshape(rows, tensor_cols)
    memory_grads = unhalves(
        scatter_weight(memory_g, back).reshape(2 * text_rows_w, 2, head_cols)
    )
    memory_grads = memory_grads.transpose(0, 2, 1, 3).reshape(text_rows_w, 2, tensor_cols)
    second_low, cross_sums, second_grad = norm_back(
        [part_own, *scatter_tokens(part_other)], second, third_grad, gains[3:4]
    )
    proj_g, comb_g, part_own, part_other, self_col, self_heads = self_backward(
        chip, x_self, gather_tokens(second_low), projector_w, combiner_w, self_low, self_pre, self_att,
        self_lse, per_head_norm_gains, cosine, sine, own_len,
    )
    first_low, self_sums = norm_back(
        [part_own, *scatter_tokens(part_other)], first, second_grad, gains[2:3], keep=False
    )
    low_local = from_latent(first_low)
    projector_grads = unhalves(scatter_weight(proj_g, back).reshape(2 * rows, 3, head_cols))
    projector_grads = projector_grads.transpose(0, 2, 1, 3).reshape(rows, 3, tensor_cols)
    combiner_grads = unhalves(scatter_weight(comb_g, forth)).reshape(rows, tensor_cols).T
    left, right, merge_in, merge_sums = merge_back(
        latents_flat, skips_flat, low_local, merger_full, gains, biases
    )
    merger_g = dot(merge_in, low_local, 0, 0).astype(BF16).reshape(chips, 2, -1, width)
    mine, other = [], []
    for k in range(chips):
        block = at(merger_g, chip_index ^ k)
        mine.append(at(block, core))
        other.append(at(block, 1 - core))
    received = [swap(o, "core", 2, 1) for o in other]
    merger_p = {
        k: (m.astype(F32) + r.astype(F32)).astype(BF16) for k, (m, r) in enumerate(zip(mine, received))
    }
    for mask in forth[::-1]:
        for k in [k for k in merger_p if k & mask]:
            received = swap(merger_p.pop(k), "chip", chips, mask)
            merger_p[k ^ mask] = (merger_p[k ^ mask].astype(F32) + received.astype(F32)).astype(BF16)
    value = merger_p[0].reshape(wide, deep, -1, width).astype(F32)
    for axis, dim, extent, index, mask in [("tb", 1, deep, side, b) for b in deep_bits[::-1]] + [
        ("ta", 0, wide, lane, b) for b in bits_of(wide)[::-1]
    ]:
        low_part, high_part = jnp.split(value, 2, axis=dim)
        high = (index & mask) > 0
        sent = jnp.where(high, low_part, high_part).astype(BF16)
        value = jnp.where(high, high_part, low_part) + swap(sent, axis, extent, mask).astype(F32)
    merger_grads = value.reshape(merger.shape)

    mlp_grad = jnp.stack([g.reshape(2 * rows, 2, tile) for g in mlp_grads], axis=2)
    expander_grads = unhalves(mlp_grad[:, 0].reshape(2 * rows, hidden_cols)).reshape(rows, 2 * hidden_cols)
    reducer_grads = unhalves(mlp_grad[:, 1].reshape(2 * rows, hidden_cols)).reshape(rows, 2 * hidden_cols).T

    text_sum = text_part
    for axis, extent, mask in [("core", 2, 1)] + [("tb", deep, b) for b in deep_bits]:
        text_sum = text_sum + swap(text_sum.astype(BF16), axis, extent, mask).astype(F32)
    text_sum = text_sum[:text_len].astype(BF16).reshape(text_len, wide, deep, -1)
    text_sum = at(text_sum, side, 2).transpose(1, 0, 2)
    text_got = exchange(text_sum)
    text_grads = lax.dynamic_slice_in_dim(text_got, core * local, local, 0).astype(F32)

    mod_grad = self_sums[1:2]
    for axis, extent, mask in [("core", 2, 1)] + [("tb", deep, b) for b in deep_bits]:
        mod_grad = mod_grad + swap(mod_grad, axis, extent, mask)
    mod_all = mod_grad[None]
    for mask in bits_of(wide):
        other = swap(mod_all, "ta", wide, mask)
        high = (lane & mask) > 0
        mod_all = jnp.concatenate([jnp.where(high, other, mod_all), jnp.where(high, mod_all, other)], axis=1)
    for mask in chip_bits:
        other = swap(mod_all, "chip", chips, mask)
        high = (chip_index & mask) > 0
        mod_all = jnp.concatenate([jnp.where(high, other, mod_all), jnp.where(high, mod_all, other)], axis=0)
    mod_all = mod_all.reshape(latent_total, width)
    exact = lax.Precision.HIGHEST
    modulator_grads = lax.dot_general(
        silu_cols.astype(F32), mod_all, (((0,), (0,)), ((), ())), precision=exact
    )
    time_part = lax.dot_general(
        mod_all, modulator.astype(F32), (((1,), (1,)), ((), ())), precision=exact
    )
    time_all = gather_all(time_part)
    time_all = jnp.moveaxis(time_all.reshape(devices, latent_total, mod_rows), 0, 1)
    time_all = time_all.reshape(chips * 2, local, wide * deep, -1)
    time_own = at(at(time_all, chip_index * 2 + core), lane * deep + side, 1)
    times_own = at(times.reshape(local, wide * deep, -1), lane * deep + side, 1).astype(F32)
    _, silu_pull = jax.vjp(jax.nn.silu, times_own)
    time_grads = silu_pull(time_own)[0]

    output_sum = jnp.sum(cotangent.astype(F32), axis=(0, 1))[None]
    columns_own = jnp.concatenate(
        [self_col.reshape(wide, 3, head_cols), query_col, memory_col.reshape(wide, 2, head_cols)], axis=1
    )
    sums = jnp.concatenate(
        [
            merge_sums[0:2], self_sums[0:1], cross_sums[0:1], mlp_sums[0:1],
            merge_sums[2:4], self_sums[1:2], cross_sums[1:2], mlp_sums[1:2],
            merge_sums[4:5], self_sums[1:2], cross_sums[2:3], mlp_sums[2:3],
            output_sum, all_columns(columns_own),
        ],
        axis=0,
    )
    hidden_sum = jnp.stack(hidden_sums, axis=2).reshape(wide, 1, hidden_cols)
    hidden_sum = all_columns(hidden_sum)
    sums = jnp.transpose(sums.reshape(21, devices, part), (1, 0, 2)).reshape(devices, -1)
    both = jnp.concatenate([sums, hidden_sum.reshape(devices, hidden_part)], axis=1)
    both = sum_scatter_all(both.reshape(chips, 2, wide, deep, -1))
    table = both[: 21 * part].reshape(21, part)
    hidden_grads = both[21 * part :]
    head_sums = jnp.concatenate(
        [self_heads[0:2], cross_heads[0:2], self_heads[2:4], cross_heads[2:3]], axis=0
    )
    for axis, extent, mask in everywhere:
        head_sums = head_sums + swap(head_sums, axis, extent, mask)

    def to_local(value):
        return jnp.transpose(value.reshape(local, shard_len, width), (1, 0, 2)).astype(F32)

    return (
        to_local(block_out), to_local(left), to_local(right), text_grads, time_grads, merger_grads,
        modulator_grads, table[0:5], table[5:14], table[14], projector_grads, combiner_grads, query_grads,
        memory_grads, blender_grads, expander_grads, reducer_grads, table[15:21], hidden_grads,
        head_sums[0:4], head_sums[4:7],
    )


def solution(mesh):
    data, tensor = mesh.shape["dp"], mesh.shape["tensor"]

    def run(*arrays):
        local = arrays[0].shape[1] // data
        wide = min(tensor, 2 * local)
        deep = tensor // wide
        grid = Mesh(
            mesh.devices.reshape(data // 2, 2, wide, deep), ("chip", "core", "ta", "tb")
        )
        dp, tp = ("chip", "core"), ("ta", "tb")
        both = dp + tp
        tokens = P(tp, dp, None)
        in_specs = (
            tokens, tokens, P(dp, None, None), P(dp, None), P(both, None), P(both, None), P(None, both),
            P(None, both), P(both), P(dp, None, tp), P(tp, dp), P(dp, tp), P(dp, None, tp), P(tp, dp),
            P(dp, tp), P(tp, dp), P(None, both), P(both), P(), P(), tokens,
        )
        out_specs = (
            tokens, tokens, tokens, P(dp, None, tp), P(dp, tp), P(both, None), P(both, None),
            P(None, both), P(None, both), P(both), P(dp, None, tp), P(tp, dp), P(dp, tp),
            P(dp, None, tp), P(tp, dp), P(dp, tp), P(tp, dp), P(None, both), P(both), P(), P(),
        )
        return jax.shard_map(
            functools.partial(body, (data // 2, wide, deep)),
            mesh=grid, in_specs=in_specs, out_specs=out_specs, check_vma=False,
        )(*arrays)

    return run
```

```python
import functools

import jax
import jax.numpy as jnp
from jax import lax
from jax.experimental import pallas as pl
from jax.experimental.pallas import tpu as pltpu
from jax.sharding import Mesh, PartitionSpec as P

GRID_W = 32
EPSILON = 1e-06
THETA = 10000.0
F32 = jnp.float32
BF16 = jnp.bfloat16
VMEM_LIMIT = 62 * 1024 * 1024
MLP_CHUNKS = 3
QUERY_BLOCK = 512
MESH = pl.DeviceIdType.MESH


def bits_of(size):
    return [1 << i for i in range(size.bit_length() - 1)]


def swap(value, axis, size, mask):
    return lax.ppermute(value, axis, [(i, i ^ mask) for i in range(size)])


def dot(left, right, left_dim, right_dim):
    return lax.dot_general(
        left, right, (((left_dim,), (right_dim,)), ((), ())), preferred_element_type=F32
    )


def params(count=1):
    return pltpu.CompilerParams(
        dimension_semantics=("arbitrary",) * count, vmem_limit_bytes=VMEM_LIMIT
    )


def whole(shape):
    zeros = (0,) * len(shape)
    return pl.BlockSpec(shape, lambda *_: zeros, pipeline_mode=pl.Buffered(1))


def per_step(shape):
    rest = (0,) * (len(shape) - 1)
    return pl.BlockSpec((1,) + tuple(shape[1:]), lambda i, *_: (i,) + rest)


def shape_of(shape, dtype):
    return jax.ShapeDtypeStruct(shape, dtype)


def head_norm(values):
    width = values.shape[-1]
    centred = values - jnp.sum(values, axis=-1, keepdims=True) * (1.0 / width)
    inverse = lax.rsqrt(
        jnp.sum(centred * centred, axis=-1, keepdims=True) * (1.0 / width) + EPSILON
    )
    return centred * inverse, inverse


def head_norm_back(grad, hat, inverse, gain):
    scale = 1.0 / grad.shape[-1]
    scaled = grad * gain
    first = jnp.sum(scaled, axis=-1, keepdims=True) * scale
    second = jnp.sum(scaled * hat, axis=-1, keepdims=True) * scale
    return inverse * (scaled - first - hat * second)


def half_turn(values):
    quarter = values.shape[-1] // 4
    part = [values[:, i * quarter : (i + 1) * quarter] for i in range(4)]
    return jnp.concatenate([part[1], part[0], part[3], part[2]], axis=1)


def of_chips(width, shape):
    return pl.BlockSpec(shape[:1] + (1,) + shape[2:3] + (width,), lambda i, *_: (0, i, 0, 0))


def flat(ref):
    chips, _, rows, cols = ref.shape
    return ref[...].reshape(chips * rows, cols)


def flip(index, mask):
    for bit in bits_of(2 * mask + 1):
        if mask & bit:
            index = index + bit - 2 * bit * (index // bit % 2)
    return index


def link_of(k, slot):
    bits = [b for b in bits_of(2 * k + 1) if k & b]
    return bits[-1] if slot % 2 == 0 else bits[0]


def by_distance(chips):
    return sorted(range(1, chips), key=lambda k: (bin(k).count("1"), k))


def greet(chips, wide, with_core):
    chip, core, lane = (lax.axis_index(n) for n in ("chip", "core", "ta"))
    barrier = pltpu.get_barrier_semaphore()
    partners = [{"ta": flip(lane, i)} for i in range(1, wide)]
    partners += [{"chip": flip(chip, b)} for b in bits_of(chips)]
    if with_core:
        partners.append({"core": 1 - core})
    for partner in partners:
        pl.semaphore_signal(barrier, inc=1, device_id=partner, device_id_type=MESH)
    pl.semaphore_wait(barrier, len(partners))


def gather_kernel(sizes, full, *refs):
    chips, wide = sizes
    n = len(full)
    shards, outs = refs[:n], refs[n : 2 * n]
    local_sem, z_send, z_recv, x_send, x_recv, c_send, c_recv = refs[2 * n :]
    chip, core, lane = (lax.axis_index(name) for name in ("chip", "core", "ta"))
    greet(chips, wide, any(full))
    sends, arrived = [], set()

    def place(w, k, i):
        if full[w]:
            return outs[w].at[flip(chip, k), core, flip(lane, i)]
        return outs[w].at[flip(chip, k), i]

    def send(source, target, device, send_sem, recv_sem):
        copy = pltpu.make_async_remote_copy(
            src_ref=source, dst_ref=target, send_sem=send_sem, recv_sem=recv_sem,
            device_id=device, device_id_type=MESH,
        )
        copy.start()
        sends.append(copy)

    def take(w, k, i):
        if k == 0 and i == 0 or (w, k, i) in arrived:
            return
        arrived.add((w, k, i))
        piece = place(w, k, i)
        sem = z_recv.at[w, i - 1] if k == 0 else x_recv.at[w, i, k - 1]
        pltpu.make_async_copy(piece, piece, sem).wait()

    def near(w, i):
        take(w, 0, i)
        source = shards[w] if i == 0 else place(w, 0, i)
        for bit in bits_of(chips):
            send(source, place(w, 0, i), {"chip": flip(chip, bit)},
                 x_send.at[w, i, bit - 1], x_recv.at[w, i, bit - 1])

    def far(w, i):
        for k in by_distance(chips):
            bit = link_of(k, i)
            held = k ^ bit
            if held:
                take(w, held, i)
                piece = place(w, held, i)
                send(piece, piece, {"chip": flip(chip, bit)}, x_send.at[w, i, k - 1], x_recv.at[w, i, k - 1])

    locals_ = []
    for w in range(n):
        copy = pltpu.make_async_copy(shards[w], place(w, 0, 0), local_sem.at[w])
        copy.start()
        locals_.append(copy)
        for i in range(1, wide):
            target = outs[w].at[chip, core, lane] if full[w] else outs[w].at[chip, i]
            send(shards[w], target, {"ta": flip(lane, i)}, z_send.at[w, i - 1], z_recv.at[w, i - 1])
    order = [(w, 0) for w in range(n)] + [(w, i) for w in range(n) for i in range(1, wide)]
    for t, (w, i) in enumerate(order):
        near(w, i)
        if t >= 2:
            far(*order[t - 2])
    for w, i in order[-2:]:
        far(w, i)
    for copy in locals_:
        copy.wait()
    for w in range(n):
        if full[w]:
            for k in range(chips):
                for i in range(wide):
                    take(w, k, i)
                send(outs[w].at[flip(chip, k), core], outs[w].at[flip(chip, k), core], {"core": 1 - core},
                     c_send.at[w, k], c_recv.at[w, k])
    for w in range(n):
        for i in range(wide):
            for k in range(chips):
                take(w, k, i)
        if full[w]:
            for k in range(chips):
                piece = outs[w].at[flip(chip, k), 1 - core]
                pltpu.make_async_copy(piece, piece, c_recv.at[w, k]).wait()
    for copy in sends:
        copy.wait_send()


def gather(sizes, shards, full, number):
    chips, wide = sizes
    n = len(shards)
    shapes = [
        ((chips, 2, wide) if f else (chips, wide)) + tuple(s.shape) for s, f in zip(shards, full)
    ]
    dma = pltpu.SemaphoreType.DMA
    return pl.pallas_call(
        functools.partial(gather_kernel, sizes, full),
        in_specs=[pl.BlockSpec(memory_space=pltpu.VMEM)] * n,
        out_specs=[pl.BlockSpec(memory_space=pl.ANY)] * n,
        out_shape=[shape_of(shape, s.dtype) for shape, s in zip(shapes, shards)],
        scratch_shapes=[
            dma((n,)), dma((n, wide - 1)), dma((n, wide - 1)), dma((n, wide, chips - 1)),
            dma((n, wide, chips - 1)), dma((n, chips)), dma((n, chips)),
        ],
        compiler_params=pltpu.CompilerParams(
            collective_id=number, has_side_effects=True, vmem_limit_bytes=VMEM_LIMIT
        ),
        name="gather",
    )(*shards)


def scatter_kernel(sizes, absolute, *refs):
    chips, wide = sizes
    n = len(absolute)
    sources, outs, nearby, along = (refs[j * n : (j + 1) * n] for j in range(4))
    x_send, x_recv, z_send, z_recv = refs[4 * n :]
    chip, lane = lax.axis_index("chip"), lax.axis_index("ta")
    greet(chips, wide, False)
    sends = []

    def send(source, target, device, send_sem, recv_sem):
        copy = pltpu.make_async_remote_copy(
            src_ref=source, dst_ref=target, send_sem=send_sem, recv_sem=recv_sem,
            device_id=device, device_id_type=MESH,
        )
        copy.start()
        sends.append(copy)

    def own(w, k, i):
        return sources[w].at[flip(chip, k), flip(lane, i) if absolute[w] else i]

    def children(q, i):
        return [k for k in by_distance(chips) if k ^ link_of(k, i) == q]

    def total(w, q, i):
        value = own(w, q, i)[...].astype(F32)
        for k in children(q, i):
            piece = nearby[w].at[i, k - 1]
            pltpu.make_async_copy(piece, piece, x_recv.at[w, i, k - 1]).wait()
            value = value + piece[...].astype(F32)
        return value

    def pass_on(source, w, k, i):
        send(source, nearby[w].at[i, k - 1], {"chip": flip(chip, link_of(k, i))},
             x_send.at[w, i, k - 1], x_recv.at[w, i, k - 1])

    order = [(w, i) for w in range(n) for i in (*range(1, wide), 0)]
    for w, i in order:
        for k in by_distance(chips)[::-1]:
            if not children(k, i):
                pass_on(own(w, k, i), w, k, i)
    for w, i in order:
        for k in by_distance(chips)[::-1]:
            if children(k, i):
                place = nearby[w].at[i, children(k, i)[0] - 1]
                place[...] = total(w, k, i).astype(BF16)
                pass_on(place, w, k, i)
    for w, i in order:
        value = total(w, 0, i)
        if i == 0:
            outs[w][...] = value
        else:
            place = nearby[w].at[i, children(0, i)[0] - 1]
            place[...] = value.astype(BF16)
            send(place, along[w].at[i - 1], {"ta": flip(lane, i)}, z_send.at[w, i - 1], z_recv.at[w, i - 1])
    for w in range(n):
        value = outs[w][...]
        for i in range(1, wide):
            piece = along[w].at[i - 1]
            pltpu.make_async_copy(piece, piece, z_recv.at[w, i - 1]).wait()
            value = value + piece[...].astype(F32)
        outs[w][...] = value
    for copy in sends:
        copy.wait_send()


def scatter(sizes, parts, absolute, number):
    chips, wide = sizes
    n = len(parts)
    ends = [tuple(p.shape[2:]) for p in parts]
    dma = pltpu.SemaphoreType.DMA
    return pl.pallas_call(
        functools.partial(scatter_kernel, sizes, absolute),
        in_specs=[pl.BlockSpec(memory_space=pltpu.VMEM)] * n,
        out_specs=[pl.BlockSpec(memory_space=pltpu.VMEM)] * n,
        out_shape=[shape_of(e, F32) for e in ends],
        scratch_shapes=[pltpu.VMEM((wide, chips - 1) + e, BF16) for e in ends]
        + [pltpu.VMEM((wide - 1,) + e, BF16) for e in ends]
        + [
            dma((n, wide, chips - 1)), dma((n, wide, chips - 1)), dma((n, wide - 1)), dma((n, wide - 1)),
        ],
        compiler_params=pltpu.CompilerParams(
            collective_id=number, has_side_effects=True, vmem_limit_bytes=VMEM_LIMIT
        ),
        name="scatter",
    )(*parts)


def column_sum(values):
    return jnp.sum(values, axis=0, keepdims=True)


def self_forward_kernel(counts, x_ref, w_ref, bias_ref, gains, shifts, cosine, sine, low_ref, pre_ref, att_ref,
                        lse_ref, own_ref, other_ref, acc):
    heads, size, own = counts
    step = pl.program_id(0)
    width = heads * size
    weights = flat(w_ref)
    packed = dot(x_ref[...], weights[:, : 3 * width], 1, 0) + bias_ref[0]
    pre_ref[0] = packed[:, : 2 * width].astype(BF16)
    value_low = packed[:, 2 * width :].astype(BF16)
    length = packed.shape[0]
    block = min(QUERY_BLOCK, length)
    cos, sin = cosine[...], sine[...]
    queries, keys, mixes, logs = [], [], [], []
    for h in range(heads):
        part = packed[:, h * size : (h + 1) * size]
        hat, _ = head_norm(part)
        turned = hat * gains[0:1, :] + shifts[0:1, :]
        query = ((turned * cos + half_turn(turned) * sin) * (size**-0.5)).astype(BF16)
        part = packed[:, width + h * size : width + (h + 1) * size]
        hat, _ = head_norm(part)
        turned = hat * gains[1:2, :] + shifts[1:2, :]
        key = (turned * cos + half_turn(turned) * sin).astype(BF16)
        value = value_low[:, h * size : (h + 1) * size]
        queries.append(query)
        keys.append(key)
        parts, sums = [], []
        for b in range(length // block):
            scores = dot(key, query[b * block : (b + 1) * block], 1, 1)
            top = jnp.max(scores, axis=0, keepdims=True)
            power = jnp.exp(scores - top)
            total = jnp.sum(power, axis=0, keepdims=True)
            shares = (power * (1.0 / total)).astype(BF16)
            parts.append(jnp.transpose(dot(value, shares, 0, 0)))
            sums.append(top + jnp.log(total))
        mixes.append(jnp.concatenate(parts, axis=0))
        logs.append(jnp.concatenate(sums, axis=1))
    low_ref[0] = jnp.concatenate(queries + keys + [value_low], axis=1)
    att = jnp.concatenate(mixes, axis=1).astype(BF16)
    att_ref[0] = att
    lse_ref[0] = jnp.concatenate(logs, axis=0)
    term = dot(att, weights[:, 3 * width :], 1, 1)

    @pl.when(step == 0)
    def _():
        acc[...] = term

    @pl.when(step > 0)
    def _():
        acc[...] += term

    @pl.when(step == pl.num_programs(0) - 1)
    def _():
        own_ref[...] = acc[:own, :]
        other_ref[...] = acc[own:, :].astype(BF16)


def self_forward(x, weights, bias, gains, shifts, cosine, sine, own):
    length, width = x.shape
    chips, groups, rows, all_cols = weights.shape
    size = gains.shape[1]
    small = all_cols // 4
    cols = 3 * small
    heads = small // size
    return pl.pallas_call(
        functools.partial(self_forward_kernel, (heads, size, own)),
        grid=(groups,),
        in_specs=[whole(x.shape), of_chips(all_cols, weights.shape), per_step(bias.shape)]
        + [whole(gains.shape), whole(shifts.shape), whole(cosine.shape), whole(sine.shape)],
        out_specs=[
            per_step((groups, length, cols)),
            per_step((groups, length, 2 * small)),
            per_step((groups, length, small)),
            per_step((groups, heads, length)),
            whole((own, width)),
            whole((length - own, width)),
        ],
        scratch_shapes=[pltpu.VMEM((length, width), F32)],
        out_shape=[
            shape_of((groups, length, cols), BF16),
            shape_of((groups, length, 2 * small), BF16),
            shape_of((groups, length, small), BF16),
            shape_of((groups, heads, length), F32),
            shape_of((own, width), F32),
            shape_of((length - own, width), BF16),
        ],
        compiler_params=params(),
        name="self_forward",
    )(x, weights, bias, gains, shifts, cosine, sine)


def attention_back(query, key, value, out_grad, logs, block, limit=None):
    length = query.shape[0]
    key_grad, value_grad, query_parts = None, None, []
    for b in range(length // block):
        rows = slice(b * block, (b + 1) * block)
        query_part, grad_part = query[rows], out_grad[rows]
        scores = dot(key, query_part, 1, 1)
        shares = jnp.exp(scores - logs[:, rows])
        if limit is not None:
            index = lax.broadcasted_iota(jnp.int32, shares.shape, 0)
            shares = jnp.where(index < limit, shares, 0.0)
        share_grad = dot(value, grad_part, 1, 1)
        inner = jnp.sum(shares * share_grad, axis=0, keepdims=True)
        score_grad = (shares * (share_grad - inner)).astype(BF16)
        query_parts.append(jnp.transpose(dot(key, score_grad, 0, 0)))
        key_term = dot(score_grad, query_part, 1, 0)
        value_term = dot(shares.astype(BF16), grad_part, 1, 0)
        key_grad = key_term if b == 0 else key_grad + key_term
        value_grad = value_term if b == 0 else value_grad + value_term
    return jnp.concatenate(query_parts, axis=0), key_grad, value_grad


def self_backward_kernel(counts, x_ref, grad_ref, w_ref, low_ref, pre_ref, att_ref, lse_ref, gains, cosine, sine,
                         w_out, own_ref, other_ref, column_ref, head_ref, acc, grad_t, x_t):
    heads, size, own = counts
    step = pl.program_id(0)
    width = heads * size
    scale = size**-0.5
    weights = flat(w_ref)
    chips, _, rows, _ = w_ref.shape

    @pl.when(step == 0)
    def _():
        grad_t[...] = jnp.transpose(grad_ref[...])
        x_t[...] = jnp.transpose(x_ref[...])

    out_grad = dot(grad_ref[...], weights[:, 3 * width :], 1, 0).astype(BF16)
    comb_grad = dot(grad_t[...], att_ref[0], 1, 0).astype(BF16)
    cos, sin = cosine[...], sine[...]
    block = min(QUERY_BLOCK, out_grad.shape[0])
    query_grads, key_grads, value_grads = [], [], []
    sums = [None] * 4
    for h in range(heads):
        cut = lambda ref, part: ref[0, :, part * width + h * size : part * width + (h + 1) * size]
        query, key, value = cut(low_ref, 0), cut(low_ref, 1), cut(low_ref, 2)
        dq, dk, dv = attention_back(
            query, key, value, out_grad[:, h * size : (h + 1) * size], lse_ref[0, h : h + 1, :], block
        )
        dq = dq * scale
        dq = dq * cos - half_turn(dq) * sin
        dk = dk * cos - half_turn(dk) * sin
        q_hat, q_inverse = head_norm(cut(pre_ref, 0).astype(F32))
        k_hat, k_inverse = head_norm(cut(pre_ref, 1).astype(F32))
        terms = [column_sum(dq * q_hat), column_sum(dk * k_hat), column_sum(dq), column_sum(dk)]
        sums = terms if h == 0 else [s + t for s, t in zip(sums, terms)]
        query_grads.append(head_norm_back(dq, q_hat, q_inverse, gains[0:1, :]))
        key_grads.append(head_norm_back(dk, k_hat, k_inverse, gains[1:2, :]))
        value_grads.append(dv)
    packed = jnp.concatenate(query_grads + key_grads + value_grads, axis=1).astype(BF16)
    column_ref[0] = column_sum(packed.astype(F32))
    term = dot(packed, weights[:, : 3 * width], 1, 1)
    proj_grad = dot(x_t[...], packed, 1, 0).astype(BF16)
    w_out[:, 0] = jnp.concatenate([proj_grad, comb_grad], axis=1).reshape(chips, rows, 4 * width)
    head_sums = jnp.concatenate(sums, axis=0)

    @pl.when(step == 0)
    def _():
        acc[...] = term
        head_ref[...] = head_sums

    @pl.when(step > 0)
    def _():
        acc[...] += term
        head_ref[...] += head_sums

    @pl.when(step == pl.num_programs(0) - 1)
    def _():
        own_ref[...] = acc[:own, :]
        other_ref[...] = acc[own:, :].astype(BF16)


def self_backward(x, grad, weights, low, pre, att, lse, gains, cosine, sine, own):
    length, width = x.shape
    chips, groups, rows, all_cols = weights.shape
    size = gains.shape[1]
    small = all_cols // 4
    cols = 3 * small
    heads = small // size
    return pl.pallas_call(
        functools.partial(self_backward_kernel, (heads, size, own)),
        grid=(groups,),
        in_specs=[whole(x.shape), whole(grad.shape), of_chips(all_cols, weights.shape)]
        + [per_step(v.shape) for v in (low, pre, att, lse)]
        + [whole(gains.shape), whole(cosine.shape), whole(sine.shape)],
        out_specs=[
            of_chips(all_cols, weights.shape),
            whole((own, width)),
            whole((length - own, width)),
            per_step((groups, 1, cols)),
            whole((4, size)),
        ],
        scratch_shapes=[
            pltpu.VMEM((length, width), F32),
            pltpu.VMEM((width, length), BF16),
            pltpu.VMEM((width, length), BF16),
        ],
        out_shape=[
            shape_of(weights.shape, BF16),
            shape_of((own, width), F32),
            shape_of((length - own, width), BF16),
            shape_of((groups, 1, cols), F32),
            shape_of((4, size), F32),
        ],
        compiler_params=params(),
        name="self_backward",
    )(x, grad, weights, low, pre, att, lse, gains, cosine, sine)


def cross_forward_kernel(counts, x_ref, text_ref, w_ref, memory_w, bias_ref, memory_bias, gains, shifts, low_ref,
                         pre_ref, memory_ref, memory_pre, att_ref, lse_ref, own_ref, other_ref, acc):
    heads, size, own, limit = counts
    step = pl.program_id(0)
    width = heads * size
    weights = flat(w_ref)
    pre = dot(x_ref[...], weights[:, :width], 1, 0) + bias_ref[0]
    memory = dot(text_ref[...], flat(memory_w), 1, 0) + memory_bias[0]
    pre_ref[0] = pre.astype(BF16)
    memory_pre[0] = memory[:, :width].astype(BF16)
    value_low = memory[:, width:].astype(BF16)
    length = pre.shape[0]
    block = min(QUERY_BLOCK, length)
    queries, keys, mixes, logs = [], [], [], []
    for h in range(heads):
        cols = slice(h * size, (h + 1) * size)
        hat, _ = head_norm(pre[:, cols])
        query = ((hat * gains[2:3, :] + shifts[2:3, :]) * (size**-0.5)).astype(BF16)
        hat, _ = head_norm(memory[:, cols])
        key = (hat * gains[3:4, :]).astype(BF16)
        value = value_low[:, cols]
        queries.append(query)
        keys.append(key)
        parts, sums = [], []
        for b in range(length // block):
            scores = dot(key, query[b * block : (b + 1) * block], 1, 1)
            index = lax.broadcasted_iota(jnp.int32, scores.shape, 0)
            scores = jnp.where(index < limit, scores, -jnp.inf)
            top = jnp.max(scores, axis=0, keepdims=True)
            power = jnp.exp(scores - top)
            total = jnp.sum(power, axis=0, keepdims=True)
            shares = (power * (1.0 / total)).astype(BF16)
            parts.append(jnp.transpose(dot(value, shares, 0, 0)))
            sums.append(top + jnp.log(total))
        mixes.append(jnp.concatenate(parts, axis=0))
        logs.append(jnp.concatenate(sums, axis=1))
    low_ref[0] = jnp.concatenate(queries, axis=1)
    memory_ref[0] = jnp.concatenate(keys + [value_low], axis=1)
    att = jnp.concatenate(mixes, axis=1).astype(BF16)
    att_ref[0] = att
    lse_ref[0] = jnp.concatenate(logs, axis=0)
    term = dot(att, weights[:, width:], 1, 1)

    @pl.when(step == 0)
    def _():
        acc[...] = term

    @pl.when(step > 0)
    def _():
        acc[...] += term

    @pl.when(step == pl.num_programs(0) - 1)
    def _():
        own_ref[...] = acc[:own, :]
        other_ref[...] = acc[own:, :].astype(BF16)


def cross_forward(x, text, weights, memory_w, bias, memory_bias, gains, shifts, own, limit):
    length, width = x.shape
    groups, small = weights.shape[1], weights.shape[3] // 2
    text_rows = text.shape[0]
    size = gains.shape[1]
    heads = small // size
    saved = [
        ((groups, length, small), BF16),
        ((groups, length, small), BF16),
        ((groups, text_rows, 2 * small), BF16),
        ((groups, text_rows, small), BF16),
        ((groups, length, small), BF16),
        ((groups, heads, length), F32),
    ]
    return pl.pallas_call(
        functools.partial(cross_forward_kernel, (heads, size, own, limit)),
        grid=(groups,),
        in_specs=[whole(x.shape), whole(text.shape)]
        + [of_chips(v.shape[3], v.shape) for v in (weights, memory_w)]
        + [per_step(bias.shape), per_step(memory_bias.shape), whole(gains.shape), whole(shifts.shape)],
        out_specs=[per_step(s) for s, _ in saved] + [whole((own, width)), whole((length - own, width))],
        scratch_shapes=[pltpu.VMEM((length, width), F32)],
        out_shape=[shape_of(*s) for s in saved]
        + [shape_of((own, width), F32), shape_of((length - own, width), BF16)],
        compiler_params=params(),
        name="cross_forward",
    )(x, text, weights, memory_w, bias, memory_bias, gains, shifts)


def cross_backward_kernel(counts, x_ref, grad_ref, text_ref, w_ref, memory_w, low_ref, pre_ref, memory_ref,
                          memory_pre, att_ref, lse_ref, gains, w_out, memory_out, own_ref, other_ref, text_out,
                          column_ref, memory_column, head_ref, acc, grad_t, x_t, text_t):
    heads, size, own, limit = counts
    step = pl.program_id(0)
    width = heads * size
    scale = size**-0.5
    weights = flat(w_ref)
    chips, _, rows, _ = w_ref.shape

    @pl.when(step == 0)
    def _():
        grad_t[...] = jnp.transpose(grad_ref[...])
        x_t[...] = jnp.transpose(x_ref[...])
        text_t[...] = jnp.transpose(text_ref[...])

    out_grad = dot(grad_ref[...], weights[:, width:], 1, 0).astype(BF16)
    blend_grad = dot(grad_t[...], att_ref[0], 1, 0).astype(BF16)
    block = min(QUERY_BLOCK, out_grad.shape[0])
    query_grads, key_grads, value_grads = [], [], []
    sums = [None] * 3
    for h in range(heads):
        cols = slice(h * size, (h + 1) * size)
        query = low_ref[0, :, cols]
        key = memory_ref[0, :, cols]
        value = memory_ref[0, :, width + h * size : width + (h + 1) * size]
        dq, dk, dv = attention_back(
            query, key, value, out_grad[:, cols], lse_ref[0, h : h + 1, :], block, limit
        )
        dq = dq * scale
        q_hat, q_inverse = head_norm(pre_ref[0, :, cols].astype(F32))
        k_hat, k_inverse = head_norm(memory_pre[0, :, cols].astype(F32))
        terms = [column_sum(dq * q_hat), column_sum(dk * k_hat), column_sum(dq)]
        sums = terms if h == 0 else [s + t for s, t in zip(sums, terms)]
        query_grads.append(head_norm_back(dq, q_hat, q_inverse, gains[2:3, :]))
        key_grads.append(head_norm_back(dk, k_hat, k_inverse, gains[3:4, :]))
        value_grads.append(dv)
    packed = jnp.concatenate(query_grads, axis=1).astype(BF16)
    memory_grad = jnp.concatenate(key_grads + value_grads, axis=1).astype(BF16)
    column_ref[0] = column_sum(packed.astype(F32))
    memory_column[0] = column_sum(memory_grad.astype(F32))
    term = dot(packed, weights[:, :width], 1, 1)
    text_term = dot(memory_grad, flat(memory_w), 1, 1)
    query_grad = dot(x_t[...], packed, 1, 0).astype(BF16)
    w_out[:, 0] = jnp.concatenate([query_grad, blend_grad], axis=1).reshape(chips, rows, 2 * width)
    memory_out[:, 0] = dot(text_t[...], memory_grad, 1, 0).astype(BF16).reshape(chips, -1, 2 * width)
    head_sums = jnp.concatenate(sums, axis=0)

    @pl.when(step == 0)
    def _():
        acc[...] = term
        text_out[...] = text_term
        head_ref[...] = head_sums

    @pl.when(step > 0)
    def _():
        acc[...] += term
        text_out[...] += text_term
        head_ref[...] += head_sums

    @pl.when(step == pl.num_programs(0) - 1)
    def _():
        own_ref[...] = acc[:own, :]
        other_ref[...] = acc[own:, :].astype(BF16)


def cross_backward(x, grad, text, weights, memory_w, low, pre, memory, memory_pre, att, lse, gains, own, limit):
    length, width = x.shape
    groups, small = weights.shape[1], weights.shape[3] // 2
    size = gains.shape[1]
    heads = small // size
    pieces = (weights, memory_w)
    tail = [
        ((own, width), F32, False),
        ((length - own, width), BF16, False),
        (text.shape, F32, False),
        ((groups, 1, small), F32, True),
        ((groups, 1, 2 * small), F32, True),
        ((3, size), F32, False),
    ]
    return pl.pallas_call(
        functools.partial(cross_backward_kernel, (heads, size, own, limit)),
        grid=(groups,),
        in_specs=[whole(x.shape), whole(grad.shape), whole(text.shape)]
        + [of_chips(p.shape[3], p.shape) for p in pieces]
        + [per_step(v.shape) for v in (low, pre, memory, memory_pre, att, lse)]
        + [whole(gains.shape)],
        out_specs=[of_chips(p.shape[3], p.shape) for p in pieces]
        + [per_step(s) if stepped else whole(s) for s, _, stepped in tail],
        scratch_shapes=[
            pltpu.VMEM((length, width), F32),
            pltpu.VMEM((width, length), BF16),
            pltpu.VMEM((width, length), BF16),
            pltpu.VMEM((text.shape[1], text.shape[0]), BF16),
        ],
        out_shape=[shape_of(p.shape, BF16) for p in pieces] + [shape_of(s, d) for s, d, _ in tail],
        compiler_params=params(),
        name="cross_backward",
    )(x, grad, text, *pieces, low, pre, memory, memory_pre, att, lse, gains)


def mlp_kernel(own, x_ref, cot_ref, x_t, cot_t, w_ref, bias_ref, w_out, out_own, out_other, back_own, back_other,
               hidden_ref, acc, back):
    step = pl.program_id(0)
    chips, _, rows, cols = w_ref.shape
    tile = cols // 2
    w = flat(w_ref)
    hidden = dot(x_ref[...], w[:, :tile], 1, 0) + bias_ref[0]
    square = hidden * hidden
    inner = 0.7978845608028654 * hidden * (1.0 + 0.044715 * square)
    curve = jnp.tanh(inner)
    active = (0.5 * hidden * (1.0 + curve)).astype(BF16)
    slope = 0.5 * (1.0 + curve) + 0.5 * hidden * (1.0 - curve * curve) * (
        0.7978845608028654 * (1.0 + 3 * 0.044715 * square)
    )
    hidden_grad = dot(cot_ref[...], w[:, tile:], 1, 0) * slope
    hidden_grad = hidden_grad.astype(BF16)
    hidden_ref[0] = column_sum(hidden_grad.astype(F32))
    out_term = dot(active, w[:, tile:], 1, 1)
    back_term = dot(hidden_grad, w[:, :tile], 1, 1)

    @pl.when(step == 0)
    def _():
        acc[...] = out_term
        back[...] = back_term

    @pl.when(step > 0)
    def _():
        acc[...] += out_term
        back[...] += back_term

    w_out[:, 0, :, :tile] = dot(x_t[...], hidden_grad, 1, 0).astype(BF16).reshape(chips, rows, tile)
    w_out[:, 0, :, tile:] = dot(cot_t[...], active, 1, 0).astype(BF16).reshape(chips, rows, tile)

    @pl.when(step == pl.num_programs(0) - 1)
    def _():
        out_own[...] = acc[:own, :]
        out_other[...] = acc[own:, :].astype(BF16)
        back_own[...] = back[:own, :]
        back_other[...] = back[own:, :].astype(BF16)


def mlp(x, cot, x_t, cot_t, weights, bias, own):
    length, width = x.shape
    chips, groups, rows, cols = weights.shape
    part = pl.BlockSpec(
        (chips, 1, rows, cols // MLP_CHUNKS), lambda i: (0, i // MLP_CHUNKS, 0, i % MLP_CHUNKS)
    )
    tail = [((own, width), F32), ((length - own, width), BF16)] * 2
    return pl.pallas_call(
        functools.partial(mlp_kernel, own),
        grid=(groups * MLP_CHUNKS,),
        in_specs=[whole(v.shape) for v in (x, cot, x_t, cot_t)] + [part, per_step(bias.shape)],
        out_specs=[part] + [whole(s) for s, _ in tail] + [per_step(bias.shape)],
        scratch_shapes=[pltpu.VMEM((length, width), F32), pltpu.VMEM((length, width), F32)],
        out_shape=[shape_of(weights.shape, BF16)]
        + [shape_of(*s) for s in tail]
        + [shape_of(bias.shape, F32)],
        compiler_params=params(),
        name="mlp",
    )(x, cot, x_t, cot_t, weights, bias)


def row_spec(block, width):
    return pl.BlockSpec((block, width), lambda i, *_: (i, 0))


def merge_kernel(latent_ref, skip_ref, merger_ref, gains, biases, out_ref):
    left, right, _ = joined_norm(latent_ref, skip_ref)
    width = left.shape[1]
    left = (left * gains[0:1, :] + biases[0:1, :]).astype(BF16)
    right = (right * gains[1:2, :] + biases[1:2, :]).astype(BF16)
    total = dot(left, merger_ref[:width, :], 1, 0) + dot(right, merger_ref[width:, :], 1, 0)
    out_ref[...] = (total + biases[5:6, :]).astype(BF16)


def joined_norm(latent_ref, skip_ref):
    left, right = latent_ref[...].astype(F32), skip_ref[...].astype(F32)
    scale = 0.5 / left.shape[1]
    mean = (jnp.sum(left, axis=-1, keepdims=True) + jnp.sum(right, axis=-1, keepdims=True)) * scale
    left, right = left - mean, right - mean
    spread = jnp.sum(left * left, axis=-1, keepdims=True) + jnp.sum(right * right, axis=-1, keepdims=True)
    inverse = lax.rsqrt(spread * scale + EPSILON)
    return left * inverse, right * inverse, inverse


def merge(latents, skips, merger, gains, biases, block=128):
    rows, width = latents.shape
    return pl.pallas_call(
        merge_kernel,
        grid=(rows // block,),
        in_specs=[row_spec(block, width)] * 2
        + [whole(merger.shape), whole(gains.shape), whole(biases.shape)],
        out_specs=row_spec(block, width),
        out_shape=shape_of((rows, width), BF16),
        compiler_params=params(),
        name="merge",
    )(latents, skips, merger, gains, biases)


def merge_back_kernel(latent_ref, skip_ref, low_ref, merger, gains, biases, left_out, right_out, merge_in, sums):
    left, right, inverse = joined_norm(latent_ref, skip_ref)
    width = left.shape[1]
    low = low_ref[...]
    scale = 0.5 / width
    left_grad = dot(low, merger[:width, :], 1, 1)
    right_grad = dot(low, merger[width:, :], 1, 1)
    merge_in[:, :width] = (left * gains[0:1, :] + biases[0:1, :]).astype(BF16)
    merge_in[:, width:] = (right * gains[1:2, :] + biases[1:2, :]).astype(BF16)
    terms = jnp.concatenate(
        [
            column_sum(left_grad * left),
            column_sum(right_grad * right),
            column_sum(left_grad),
            column_sum(right_grad),
            column_sum(low.astype(F32)),
        ],
        axis=0,
    )
    left_grad, right_grad = left_grad * gains[0:1, :], right_grad * gains[1:2, :]
    first = jnp.sum(left_grad, axis=-1, keepdims=True) + jnp.sum(right_grad, axis=-1, keepdims=True)
    second = jnp.sum(left_grad * left, axis=-1, keepdims=True) + jnp.sum(
        right_grad * right, axis=-1, keepdims=True
    )
    first, second = first * scale, second * scale
    left_out[...] = inverse * (left_grad - first - left * second)
    right_out[...] = inverse * (right_grad - first - right * second)

    @pl.when(pl.program_id(0) == 0)
    def _():
        sums[...] = terms

    @pl.when(pl.program_id(0) > 0)
    def _():
        sums[...] += terms


def merge_back(latents, skips, low, merger, gains, biases, block=128):
    rows, width = latents.shape
    return pl.pallas_call(
        merge_back_kernel,
        grid=(rows // block,),
        in_specs=[row_spec(block, width)] * 3
        + [whole(merger.shape), whole(gains.shape), whole(biases.shape)],
        out_specs=[row_spec(block, width)] * 2 + [row_spec(block, 2 * width), whole((5, width))],
        out_shape=[
            shape_of((rows, width), F32),
            shape_of((rows, width), F32),
            shape_of((rows, 2 * width), BF16),
            shape_of((5, width), F32),
        ],
        compiler_params=params(),
        name="merge_back",
    )(latents, skips, low, merger, gains, biases)


def norm_kernel(count, keep, *refs):
    parts, rows, outs = refs[:count], refs[count], refs[count + 1 :]
    total = parts[0][...].astype(F32)
    for part in parts[1:]:
        total = total + part[...].astype(F32)
    total = total + rows[0:1, :]
    hat, _ = head_norm(total)
    outs[0][...] = (hat * rows[1:2, :] + rows[2:3, :]).astype(BF16)
    if keep:
        outs[1][...] = total


def norm(parts, rows, keep=True, block=128):
    length, width = parts[0].shape
    out = pl.pallas_call(
        functools.partial(norm_kernel, len(parts), keep),
        grid=(length // block,),
        in_specs=[row_spec(block, width)] * len(parts) + [whole(rows.shape)],
        out_specs=[row_spec(block, width)] * (1 + keep),
        out_shape=[shape_of((length, width), BF16)] + [shape_of((length, width), F32)] * keep,
        compiler_params=params(),
        name="norm",
    )(*parts, rows)
    return out if keep else out[0]


def norm_back_kernel(count, keep, *refs):
    parts, value_ref, carried, gain = refs[:count], refs[count], refs[count + 1], refs[count + 2]
    outs = refs[count + 3 :]
    grad = parts[0][...].astype(F32)
    for part in parts[1:]:
        grad = grad + part[...].astype(F32)
    hat, inverse = head_norm(value_ref[...].astype(F32))
    total = carried[...].astype(F32) + head_norm_back(grad, hat, inverse, gain[...])
    low = total.astype(BF16)
    outs[0][...] = low
    if keep:
        outs[2][...] = total
    terms = jnp.concatenate(
        [column_sum(grad * hat), column_sum(grad), column_sum(low.astype(F32))], axis=0
    )
    sums = outs[1]

    @pl.when(pl.program_id(0) == 0)
    def _():
        sums[...] = terms

    @pl.when(pl.program_id(0) > 0)
    def _():
        sums[...] += terms


def norm_back(parts, value, carried, gain, keep=True, block=128):
    length, width = value.shape
    return pl.pallas_call(
        functools.partial(norm_back_kernel, len(parts), keep),
        grid=(length // block,),
        in_specs=[row_spec(block, width)] * (len(parts) + 2) + [whole(gain.shape)],
        out_specs=[row_spec(block, width), whole((3, width))] + [row_spec(block, width)] * keep,
        out_shape=[shape_of((length, width), BF16), shape_of((3, width), F32)]
        + [shape_of((length, width), F32)] * keep,
        compiler_params=params(),
        name="norm_back",
    )(*parts, value, carried, gain)


def body(sizes, latents, skips, text_states, time_embedding, merger, modulator, norm_gains, norm_biases,
         output_bias, projector, combiner, cross_query, cross_memory, blender, expander, reducer,
         column_biases, hidden_bias, per_head_norm_gains, head_shifts, cotangent):
    chips, wide, deep = sizes
    chip_index, core, lane, side = (lax.axis_index(n) for n in ("chip", "core", "ta", "tb"))
    shard_len, local, width = latents.shape
    size = per_head_norm_gains.shape[1]
    text_len, text_width = text_states.shape[1:]
    own_len = shard_len * local
    seq_len = shard_len * wide * deep
    devices = chips * 2 * wide * deep
    latent_total = chips * 2 * local
    half_len = shard_len // 2
    tensor_cols = projector.shape[2]
    head_cols = tensor_cols // 2
    hidden_cols = expander.shape[1] // 2
    chip_bits, wide_bits, deep_bits = bits_of(chips), bits_of(wide)[::-1], bits_of(deep)

    everywhere = [("ta", wide, b) for b in bits_of(wide)] + [("tb", deep, b) for b in deep_bits]
    everywhere = [("core", 2, 1)] + everywhere + [("chip", chips, b) for b in chip_bits]
    index_of = {"chip": chip_index, "core": core, "ta": lane, "tb": side}

    def at(value, index, axis=0):
        return lax.dynamic_index_in_dim(value, index, axis, keepdims=False)

    def gather_all(value):
        value = value[None, None, None, None]
        dims = {"chip": 0, "core": 1, "ta": 2, "tb": 3}
        shape = [1, 1, 1, 1]
        for axis, extent, mask in everywhere:
            value = value.reshape((*shape, *value.shape[4:]))
            other = swap(value, axis, extent, mask)
            high = (index_of[axis] & mask) > 0
            low_part = jnp.where(high, other, value)
            high_part = jnp.where(high, value, other)
            value = jnp.concatenate([low_part, high_part], axis=dims[axis])
            shape[dims[axis]] *= 2
        return value

    def sum_scatter_all(value):
        dims = {"chip": 0, "core": 1, "ta": 2, "tb": 3}
        for axis, extent, mask in everywhere[::-1]:
            dim = dims[axis]
            rows = value.shape[dim] // 2
            high = (index_of[axis] & mask) > 0
            low_part = lax.slice_in_dim(value, 0, rows, axis=dim)
            high_part = lax.slice_in_dim(value, rows, 2 * rows, axis=dim)
            kept = jnp.where(high, high_part, low_part)
            value = kept + swap(jnp.where(high, low_part, high_part), axis, extent, mask)
        return value.reshape(value.shape[4:])

    def halves(value):
        mine, other = at(value, core, 1), at(value, 1 - core, 1)
        other = swap(other, "core", 2, 1)
        pair = jnp.where(core == 0, jnp.stack([mine, other]), jnp.stack([other, mine]))
        return pair.reshape((-1,) + pair.shape[2:])

    def unhalves(value):
        value = value.reshape((2, -1) + value.shape[1:])
        mine, other = at(value, core), at(value, 1 - core)
        other = swap(other, "core", 2, 1)
        return jnp.where(core == 0, jnp.stack([mine, other], 1), jnp.stack([other, mine], 1))

    small = jnp.concatenate(
        [v.reshape(-1) for v in (norm_gains, norm_biases, output_bias, column_biases, hidden_bias)]
    )
    times = time_embedding
    silu_own = jax.nn.silu(times.astype(F32)).astype(BF16)
    small = jnp.concatenate([small, silu_own.astype(F32).reshape(-1)])[None]
    rows, tile = projector.shape[0], hidden_cols // MLP_CHUNKS

    def with_tb(value):
        value = value[None]
        for mask in deep_bits:
            other = swap(value, "tb", deep, mask)
            high = (side & mask) > 0
            value = jnp.concatenate(
                [jnp.where(high, other, value), jnp.where(high, value, other)], axis=0
            )
        return value.reshape((-1,) + value.shape[2:])

    self_in = jnp.concatenate([projector, combiner.T[:, None]], axis=1)
    self_in = halves(self_in.reshape(rows, 4, 2, head_cols).transpose(0, 2, 1, 3)).reshape(2 * rows, -1)
    small_all, merger_full, modulator_full, self_w = gather(
        (chips, wide), [with_tb(small), with_tb(merger), with_tb(modulator), self_in], (True, True, True, False), 1
    )
    merger_full = merger_full.reshape(2 * width, width)
    modulator_full = modulator_full.reshape(width, width)
    small_all = small_all.reshape(devices, -1)
    part = norm_gains.shape[1]
    hidden_part = hidden_bias.shape[0]
    table = jnp.transpose(small_all[:, : 21 * part].reshape(devices, 21, part), (1, 0, 2)).reshape(21, width)
    gains, biases, out_bias, columns = table[:5], table[5:14], table[14:15], table[15:21]
    silu_at = 21 * part + hidden_part
    hidden_all = small_all[:, 21 * part : silu_at].reshape(wide, deep, 2, hidden_cols)
    silu_all = small_all[:, silu_at:].reshape(chips * 2, wide * deep, local, width)[:, 0]
    silu_all = silu_all.reshape(latent_total, width).astype(BF16)

    def own_columns(value):
        value = value.reshape(value.shape[0], wide, deep, 2, -1)
        value = at(at(value, side, 2), core, 2)
        return jnp.stack([at(value, lane ^ i, 1) for i in range(wide)])

    def all_columns(value):
        value = jnp.stack([at(value, lane ^ i) for i in range(wide)], axis=1)
        there = (jnp.arange(deep) == side)[:, None] & (jnp.arange(2) == core)[None, :]
        value = jnp.where(there[None, None, :, :, None], value[:, :, None, None, :], 0.0)
        return value.reshape(value.shape[0], -1)

    own_biases = own_columns(columns)

    text_rows_w = cross_memory.shape[0]
    cross_in = jnp.stack([cross_query, blender.T], axis=1)
    cross_in = halves(cross_in.reshape(rows, 2, 2, head_cols).transpose(0, 2, 1, 3)).reshape(2 * rows, -1)
    memory_in = halves(cross_memory.reshape(text_rows_w, 2, 2, head_cols).transpose(0, 2, 1, 3))
    memory_in = memory_in.reshape(2 * text_rows_w, 2 * head_cols)
    mlp_in = jnp.stack([expander, reducer.T], axis=1).reshape(rows, 2, 2, MLP_CHUNKS, tile)
    mlp_in = halves(mlp_in.transpose(0, 2, 3, 1, 4)).reshape(2 * rows, 2 * hidden_cols)
    cross_w, memory_w, mlp_w = gather((chips, wide), [cross_in, memory_in, mlp_in], (False,) * 3, 2)

    mod_rows = modulator.shape[0]
    device = ((chip_index * 2 + core) * wide + lane) * deep + side
    silu_cols = at(silu_all.reshape(latent_total, devices, mod_rows), device, 1)
    silu_mine = lax.dynamic_slice_in_dim(silu_all, chip_index * 2 * local + lane, 1, 0)
    mod = jnp.dot(silu_mine, modulator_full, preferred_element_type=F32)

    def to_latent(value):
        value = value.reshape(local, 2, half_len, width)
        mine, other = at(value, core, 1), at(value, 1 - core, 1)
        other = swap(other, "core", 2, 1)
        pair = jnp.where(core == 0, jnp.stack([mine, other]), jnp.stack([other, mine]))
        return exchange(pair.reshape(wide, half_len, width)).reshape(own_len, width)

    def from_latent(value):
        pair = exchange(value.reshape(wide, half_len, width)).reshape(2, local, half_len, width)
        mine, other = at(pair, core), at(pair, 1 - core)
        other = swap(other, "core", 2, 1)
        value = jnp.where(core == 0, jnp.stack([mine, other], 1), jnp.stack([other, mine], 1))
        return value.reshape(own_len, width)

    def exchange(value):
        own = at(value, lane)
        parts = [own] + [
            swap(at(value, lane ^ mask), "ta", wide, mask) for mask in range(1, wide)
        ]
        parts = jnp.stack(parts)
        return jnp.stack([at(parts, lane ^ i) for i in range(wide)])

    def gather_tokens(value):
        value = jnp.concatenate([value, swap(value, "core", 2, 1)], axis=0)
        for mask in deep_bits:
            value = jnp.concatenate([value, swap(value, "tb", deep, mask)], axis=0)
        return value

    def scatter_tokens(other):
        terms = []
        rest = other
        for mask in deep_bits[::-1]:
            rows_sent = (own_len * 2 * deep) // 2
            kept = rest.shape[0] - rows_sent
            received = swap(rest[kept:], "tb", deep, mask)
            terms.append(received[:own_len])
            rest = (rest[:kept].astype(F32) + received[own_len:].astype(F32)).astype(BF16)
        terms.append(swap(rest, "core", 2, 1))
        return terms

    latents_flat = jnp.transpose(latents, (1, 0, 2)).reshape(own_len, width)
    skips_flat = jnp.transpose(skips, (1, 0, 2)).reshape(own_len, width)
    first_local = merge(latents_flat, skips_flat, merger_full, gains, biases)
    first = to_latent(first_local)
    cot = to_latent(jnp.transpose(cotangent, (1, 0, 2)))
    cot_all = gather_tokens(cot)

    block_index = jnp.arange(wide)[:, None]
    inside = jnp.arange(half_len)[None, :]
    places = []
    for b in range(deep):
        for c in range(2):
            slot = (block_index * deep + (side ^ b)) * 2 + (core ^ c)
            places.append((slot * half_len + inside).reshape(-1))
    places = jnp.concatenate(places)
    quarter = size // 4
    frequency = THETA ** (-2.0 * jnp.arange(quarter).astype(F32) / (size // 2))
    row_angle = (places // GRID_W).astype(F32)[:, None] * frequency
    column_angle = (places % GRID_W).astype(F32)[:, None] * frequency
    angles = jnp.concatenate([row_angle, row_angle, column_angle, column_angle], axis=1)
    sign = jnp.where((jnp.arange(size) // quarter) % 2 == 0, -1.0, 1.0)
    cosine, sine = jnp.cos(angles), jnp.sin(angles) * sign

    zero_row = jnp.zeros((1, width), F32)
    rows_of = lambda *parts: jnp.concatenate(parts, axis=0)
    x_self = gather_tokens(
        norm([first], rows_of(zero_row, gains[2:3], biases[2:3] + biases[6:7] + mod), keep=False)
    )
    self_bias = own_biases[:, 0:3].reshape(wide, 1, 3 * head_cols)
    self_low, self_pre, self_att, self_lse, part_own, part_other = self_forward(
        x_self, self_w, self_bias, per_head_norm_gains, head_shifts, cosine, sine, own_len
    )
    x_cross, second = norm(
        [first, part_own, *scatter_tokens(part_other)], rows_of(biases[7:8], gains[3:4], biases[3:4])
    )
    x_cross = gather_tokens(x_cross)

    text_pad = -text_len % 16
    text_mine = at(text_states, lane % local)
    text_other = swap(text_mine, "core", 2, 1)
    text = jnp.where(core == lane // local, text_mine, text_other)
    text = jnp.pad(text, ((0, text_pad), (0, 0)))
    cross_bias = own_biases[:, 3:4]
    memory_bias = own_biases[:, 4:6].reshape(wide, 1, 2 * head_cols)
    cross_low, cross_pre, memory_low, memory_pre, cross_att, cross_lse, part_own, part_other = cross_forward(
        x_cross, text, cross_w, memory_w, cross_bias, memory_bias,
        per_head_norm_gains, head_shifts, own_len, text_len,
    )
    x_mlp, third = norm(
        [second, part_own, *scatter_tokens(part_other)], rows_of(biases[8:9], gains[4:5], biases[4:5])
    )
    x_mlp = gather_tokens(x_mlp)

    own_hidden = at(at(hidden_all, side, 1), core, 1)
    own_hidden = jnp.stack([at(own_hidden, lane ^ i) for i in range(wide)]).reshape(wide * MLP_CHUNKS, 1, tile)
    mlp_g, out_own, out_other, back_own, back_other, hidden_sum = mlp(
        x_mlp, cot_all, x_mlp.T, cot_all.T, mlp_w, own_hidden, own_len
    )
    (mlp_grad,) = scatter((chips, wide), [mlp_g], (False,), 3)
    outs = [third, out_own, *scatter_tokens(out_other)]
    backs = [back_own, *scatter_tokens(back_other)]
    block_total = sum(v.astype(F32) for v in outs) + out_bias
    block_out = from_latent(block_total.astype(BF16))

    third_low, mlp_sums, third_grad = norm_back(backs, third, cot, gains[4:5])
    blender_g_in = gather_tokens(third_low)
    cross_g, memory_g, part_own, part_other, text_part, query_col, memory_col, cross_heads = cross_backward(
        x_cross, blender_g_in, text, cross_w, memory_w, cross_low, cross_pre,
        memory_low, memory_pre, cross_att, cross_lse, per_head_norm_gains, own_len, text_len,
    )
    cross_grad, memory_grads = scatter((chips, wide), [cross_g, memory_g], (False, False), 4)
    cross_grad = unhalves(cross_grad.reshape(2 * rows, 2, head_cols)).transpose(2, 0, 1, 3)
    query_grads = cross_grad[0].reshape(rows, tensor_cols)
    blender_grads = cross_grad[1].reshape(rows, tensor_cols).T
    memory_grads = unhalves(memory_grads.reshape(2 * text_rows_w, 2, head_cols))
    memory_grads = memory_grads.transpose(0, 2, 1, 3).reshape(text_rows_w, 2, tensor_cols)
    second_low, cross_sums, second_grad = norm_back(
        [part_own, *scatter_tokens(part_other)], second, third_grad, gains[3:4]
    )
    self_g, part_own, part_other, self_col, self_heads = self_backward(
        x_self, gather_tokens(second_low), self_w, self_low, self_pre, self_att,
        self_lse, per_head_norm_gains, cosine, sine, own_len,
    )
    first_low, self_sums = norm_back(
        [part_own, *scatter_tokens(part_other)], first, second_grad, gains[2:3], keep=False
    )
    low_local = from_latent(first_low)
    left, right, merge_in, merge_sums = merge_back(
        latents_flat, skips_flat, low_local, merger_full, gains, biases
    )
    merger_g = dot(merge_in, low_local, 0, 0).astype(BF16).reshape(chips, 2, -1, width)
    mine, other = at(merger_g, core, 1), at(merger_g, 1 - core, 1)
    value = mine.astype(F32) + swap(other, "core", 2, 1).astype(F32)
    value = value.reshape(chips, wide, deep, -1, width)
    for mask in deep_bits[::-1]:
        low_part, high_part = jnp.split(value, 2, axis=2)
        high = (side & mask) > 0
        sent = jnp.where(high, low_part, high_part).astype(BF16)
        value = jnp.where(high, high_part, low_part) + swap(sent, "tb", deep, mask).astype(F32)
    merger_g = value.astype(BF16).reshape(chips, wide, -1, width)
    self_grad, merger_grads = scatter((chips, wide), [self_g, merger_g], (False, True), 5)
    self_grad = unhalves(self_grad.reshape(2 * rows, 4, head_cols)).transpose(0, 2, 1, 3)
    projector_grads = self_grad[:, :3].reshape(rows, 3, tensor_cols)
    combiner_grads = self_grad[:, 3].reshape(rows, tensor_cols).T

    mlp_grad = unhalves(mlp_grad.reshape(2 * rows, MLP_CHUNKS, 2, tile)).transpose(3, 0, 1, 2, 4)
    expander_grads = mlp_grad[0].reshape(rows, 2 * hidden_cols)
    reducer_grads = mlp_grad[1].reshape(rows, 2 * hidden_cols).T

    text_sum = text_part
    for axis, extent, mask in [("core", 2, 1)] + [("tb", deep, b) for b in deep_bits]:
        text_sum = text_sum + swap(text_sum.astype(BF16), axis, extent, mask).astype(F32)
    text_sum = text_sum[:text_len].astype(BF16).reshape(text_len, wide, deep, -1)
    text_sum = at(text_sum, side, 2).transpose(1, 0, 2)
    text_got = exchange(text_sum)
    text_grads = lax.dynamic_slice_in_dim(text_got, core * local, local, 0).astype(F32)

    mod_grad = self_sums[1:2]
    for axis, extent, mask in [("core", 2, 1)] + [("tb", deep, b) for b in deep_bits]:
        mod_grad = mod_grad + swap(mod_grad, axis, extent, mask)
    mod_all = mod_grad[None]
    for mask in bits_of(wide):
        other = swap(mod_all, "ta", wide, mask)
        high = (lane & mask) > 0
        mod_all = jnp.concatenate([jnp.where(high, other, mod_all), jnp.where(high, mod_all, other)], axis=1)
    for mask in chip_bits:
        other = swap(mod_all, "chip", chips, mask)
        high = (chip_index & mask) > 0
        mod_all = jnp.concatenate([jnp.where(high, other, mod_all), jnp.where(high, mod_all, other)], axis=0)
    mod_all = mod_all.reshape(latent_total, width)
    exact = lax.Precision.HIGHEST
    modulator_grads = lax.dot_general(
        silu_cols.astype(F32), mod_all, (((0,), (0,)), ((), ())), precision=exact
    )
    mod_own = lax.dynamic_slice_in_dim(mod_all, (chip_index * 2 + core) * local, local, 0)
    cols_own = width // (wide * deep)
    tensor_index = lane * deep + side
    modulator_own = lax.dynamic_slice_in_dim(modulator_full, tensor_index * cols_own, cols_own, 0)
    time_own = lax.dot_general(
        mod_own, modulator_own.astype(F32), (((1,), (1,)), ((), ())), precision=exact
    )
    times_own = lax.dynamic_slice_in_dim(times, tensor_index * cols_own, cols_own, 1).astype(F32)
    _, silu_pull = jax.vjp(jax.nn.silu, times_own)
    time_grads = silu_pull(time_own)[0]

    output_sum = jnp.sum(cotangent.astype(F32), axis=(0, 1))[None]
    columns_own = jnp.concatenate(
        [self_col.reshape(wide, 3, head_cols), query_col, memory_col.reshape(wide, 2, head_cols)], axis=1
    )
    sums = jnp.concatenate(
        [
            merge_sums[0:2], self_sums[0:1], cross_sums[0:1], mlp_sums[0:1],
            merge_sums[2:4], self_sums[1:2], cross_sums[1:2], mlp_sums[1:2],
            merge_sums[4:5], self_sums[1:2], cross_sums[2:3], mlp_sums[2:3],
            output_sum, all_columns(columns_own),
        ],
        axis=0,
    )
    hidden_sum = hidden_sum.reshape(wide, 1, hidden_cols)
    hidden_sum = all_columns(hidden_sum)
    sums = jnp.transpose(sums.reshape(21, devices, part), (1, 0, 2)).reshape(devices, -1)
    both = jnp.concatenate([sums, hidden_sum.reshape(devices, hidden_part)], axis=1)
    both = sum_scatter_all(both.reshape(chips, 2, wide, deep, -1))
    table = both[: 21 * part].reshape(21, part)
    hidden_grads = both[21 * part :]
    head_sums = jnp.concatenate(
        [self_heads[0:2], cross_heads[0:2], self_heads[2:4], cross_heads[2:3]], axis=0
    )
    for axis, extent, mask in everywhere:
        head_sums = head_sums + swap(head_sums, axis, extent, mask)

    def to_local(value):
        return jnp.transpose(value.reshape(local, shard_len, width), (1, 0, 2)).astype(F32)

    return (
        to_local(block_out), to_local(left), to_local(right), text_grads, time_grads, merger_grads,
        modulator_grads, table[0:5], table[5:14], table[14], projector_grads, combiner_grads, query_grads,
        memory_grads, blender_grads, expander_grads, reducer_grads, table[15:21], hidden_grads,
        head_sums[0:4], head_sums[4:7],
    )


def solution(mesh):
    data, tensor = mesh.shape["dp"], mesh.shape["tensor"]

    def run(*arrays):
        local = arrays[0].shape[1] // data
        wide = min(tensor, 2 * local)
        deep = tensor // wide
        grid = Mesh(
            mesh.devices.reshape(data // 2, 2, wide, deep), ("chip", "core", "ta", "tb")
        )
        dp, tp = ("chip", "core"), ("ta", "tb")
        both = dp + tp
        tokens = P(tp, dp, None)
        in_specs = (
            tokens, tokens, P(dp, None, None), P(dp, None), P(both, None), P(both, None), P(None, both),
            P(None, both), P(both), P(dp, None, tp), P(tp, dp), P(dp, tp), P(dp, None, tp), P(tp, dp),
            P(dp, tp), P(tp, dp), P(None, both), P(both), P(), P(), tokens,
        )
        out_specs = (
            tokens, tokens, tokens, P(dp, None, tp), P(dp, tp), P(both, None), P(both, None),
            P(None, both), P(None, both), P(both), P(dp, None, tp), P(tp, dp), P(dp, tp),
            P(dp, None, tp), P(tp, dp), P(dp, tp), P(tp, dp), P(None, both), P(both), P(), P(),
        )
        return jax.shard_map(
            functools.partial(body, (data // 2, wide, deep)),
            mesh=grid, in_specs=in_specs, out_specs=out_specs, check_vma=False,
        )(*arrays)

    return run
```

```python
import functools

import jax
import jax.numpy as jnp
from jax import lax
from jax.experimental import pallas as pl
from jax.experimental.pallas import tpu as pltpu
from jax.sharding import Mesh, PartitionSpec as P

GRID_W = 32
EPSILON = 1e-06
THETA = 10000.0
F32 = jnp.float32
BF16 = jnp.bfloat16
VMEM_LIMIT = 62 * 1024 * 1024
MLP_CHUNKS = 3
PACES = (0.7, 0.4, 0.8, 0.8)
QUERY_BLOCK = 512
MESH = pl.DeviceIdType.MESH


def bits_of(size):
    return [1 << i for i in range(size.bit_length() - 1)]


def swap(value, axis, size, mask):
    return lax.ppermute(value, axis, [(i, i ^ mask) for i in range(size)])


def dot(left, right, left_dim, right_dim):
    return lax.dot_general(
        left, right, (((left_dim,), (right_dim,)), ((), ())), preferred_element_type=F32
    )


def params(count=1):
    return pltpu.CompilerParams(
        dimension_semantics=("arbitrary",) * count, vmem_limit_bytes=VMEM_LIMIT
    )


def whole(shape):
    zeros = (0,) * len(shape)
    return pl.BlockSpec(shape, lambda *_: zeros, pipeline_mode=pl.Buffered(1))


def per_step(shape):
    rest = (0,) * (len(shape) - 1)
    return pl.BlockSpec((1,) + tuple(shape[1:]), lambda i, *_: (i,) + rest)


def shape_of(shape, dtype):
    return jax.ShapeDtypeStruct(shape, dtype)


def head_norm(values):
    width = values.shape[-1]
    centred = values - jnp.sum(values, axis=-1, keepdims=True) * (1.0 / width)
    inverse = lax.rsqrt(
        jnp.sum(centred * centred, axis=-1, keepdims=True) * (1.0 / width) + EPSILON
    )
    return centred * inverse, inverse


def head_norm_back(grad, hat, inverse, gain):
    scale = 1.0 / grad.shape[-1]
    scaled = grad * gain
    first = jnp.sum(scaled, axis=-1, keepdims=True) * scale
    second = jnp.sum(scaled * hat, axis=-1, keepdims=True) * scale
    return inverse * (scaled - first - hat * second)


def half_turn(values):
    quarter = values.shape[-1] // 4
    part = [values[:, i * quarter : (i + 1) * quarter] for i in range(4)]
    return jnp.concatenate([part[1], part[0], part[3], part[2]], axis=1)


def of_chips(width, shape):
    return pl.BlockSpec(shape[:1] + (1,) + shape[2:3] + (width,), lambda i, *_: (0, i, 0, 0))


def flat(ref):
    chips, _, rows, cols = ref.shape
    return ref[...].reshape(chips * rows, cols)


def flip(index, mask):
    for bit in bits_of(2 * mask + 1):
        if mask & bit:
            index = index + bit - 2 * bit * (index // bit % 2)
    return index


def link_of(k, slot):
    bits = [b for b in bits_of(2 * k + 1) if k & b]
    return bits[-1] if slot % 2 == 0 else bits[0]


def by_distance(chips):
    return sorted(range(1, chips), key=lambda k: (bin(k).count("1"), k))


def greet(chips, wide, with_core):
    chip, core, lane = (lax.axis_index(n) for n in ("chip", "core", "ta"))
    barrier = pltpu.get_barrier_semaphore()
    partners = [{"ta": flip(lane, i)} for i in range(1, wide)]
    partners += [{"chip": flip(chip, b)} for b in bits_of(chips)]
    if with_core:
        partners.append({"core": 1 - core})
    for partner in partners:
        pl.semaphore_signal(barrier, inc=1, device_id=partner, device_id_type=MESH)
    pl.semaphore_wait(barrier, len(partners))


def remote(source, target, device, send_sem, recv_sem, sent):
    copy = pltpu.make_async_remote_copy(
        src_ref=source, dst_ref=target, send_sem=send_sem, recv_sem=recv_sem,
        device_id=device, device_id_type=MESH,
    )
    if sent:
        copy.wait_send()
    else:
        copy.start()


def await_bytes(ref, sem):
    pltpu.make_async_copy(ref, ref, sem).wait()


def here():
    return tuple(lax.axis_index(name) for name in ("chip", "core", "ta"))


class Gather:
    def __init__(self, sizes, shards, full, number, pace=1.0):
        chips, wide = sizes
        n = len(shards)
        dma = pltpu.SemaphoreType.DMA
        self.sizes, self.full, self.number, self.pace = sizes, full, number, pace
        self.args = list(shards)
        self.in_specs = [pl.BlockSpec(memory_space=pltpu.VMEM)] * n
        self.out_specs = [pl.BlockSpec(memory_space=pl.ANY)] * n
        self.out_shape = [
            shape_of(((chips, 2, wide) if f else (chips, wide)) + tuple(v.shape), v.dtype)
            for v, f in zip(shards, full)
        ]
        self.scratch = [
            dma((n,)), dma((n, wide - 1)), dma((n, wide - 1)), dma((n, wide, chips - 1)),
            dma((n, wide, chips - 1)), dma((n, chips)), dma((n, chips)),
        ]

    def plan(self, shards, outs, scratch):
        chips, wide = self.sizes
        full, n = self.full, len(shards)
        local_sem, z_send, z_recv, x_send, x_recv, c_send, c_recv = scratch
        steps, ends, placed, arrived = [], [], [], set()

        def place(w, k, i):
            chip, core, lane = here()
            if full[w]:
                return outs[w].at[flip(chip, k), core, flip(lane, i)]
            return outs[w].at[flip(chip, k), i]

        def take(w, k, i):
            if k == 0 and i == 0 or (w, k, i) in arrived:
                return
            arrived.add((w, k, i))
            sem = z_recv.at[w, i - 1] if k == 0 else x_recv.at[w, i, k - 1]
            steps.append(lambda: await_bytes(place(w, k, i), sem))

        def pass_on(w, k, i, bit, source, sent=False):
            chip = here()[0]
            target = place(w, k ^ bit, i)
            remote(source() if source else target, target, {"chip": flip(chip, bit)},
                   x_send.at[w, i, k - 1], x_recv.at[w, i, k - 1], sent)

        def near(w, i):
            take(w, 0, i)
            for bit in bits_of(chips):
                source = (lambda: shards[w]) if i == 0 else None
                steps.append(lambda bit=bit: pass_on(w, bit, i, bit, source))
                ends.append(lambda bit=bit: pass_on(w, bit, i, bit, source, True))

        def far(w, i):
            for k in by_distance(chips):
                bit = link_of(k, i)
                if k ^ bit:
                    take(w, k ^ bit, i)
                    steps.append(lambda k=k, bit=bit: pass_on(w, k, i, bit, None))
                    ends.append(lambda k=k, bit=bit: pass_on(w, k, i, bit, None, True))

        def along(w, i, sent=False):
            chip, core, lane = here()
            target = outs[w].at[chip, core, lane] if full[w] else outs[w].at[chip, i]
            remote(shards[w], target, {"ta": flip(lane, i)}, z_send.at[w, i - 1], z_recv.at[w, i - 1], sent)

        def over(w, k, sent=False):
            chip, core, _ = here()
            piece = outs[w].at[flip(chip, k), core]
            remote(piece, piece, {"core": 1 - core}, c_send.at[w, k], c_recv.at[w, k], sent)

        def got(w, k):
            chip, core, _ = here()
            await_bytes(outs[w].at[flip(chip, k), 1 - core], c_recv.at[w, k])

        steps.append(lambda: greet(chips, wide, any(full)))
        for w in range(n):
            steps.append(lambda w=w: pltpu.make_async_copy(shards[w], place(w, 0, 0), local_sem.at[w]).start())
            placed.append(len(ends))
            ends.append(lambda w=w: pltpu.make_async_copy(shards[w], place(w, 0, 0), local_sem.at[w]).wait())
            for i in range(1, wide):
                steps.append(lambda w=w, i=i: along(w, i))
                ends.append(lambda w=w, i=i: along(w, i, True))
        for w in range(n):
            near(w, 0)
        first = len(steps)
        order = [(w, 0) for w in range(n)] + [(w, i) for w in range(n) for i in range(1, wide)]
        for t, (w, i) in enumerate(order):
            if t >= n:
                near(w, i)
            if t >= 2:
                far(*order[t - 2])
        for w, i in order[-2:]:
            far(w, i)
        for w in range(n):
            if full[w]:
                steps.append(ends[placed[w]])
                ends[placed[w]] = lambda: None
                for k in range(chips):
                    for i in range(wide):
                        take(w, k, i)
                    steps.append(lambda w=w, k=k: over(w, k))
        for w in range(n):
            for i in range(wide):
                for k in range(chips):
                    take(w, k, i)
            if full[w]:
                for k in range(chips):
                    steps.append(lambda w=w, k=k: got(w, k))
                    ends.append(lambda w=w, k=k: over(w, k, True))
        return steps + ends, first


class Scatter:
    def __init__(self, sizes, entries, absolute, number, pace=1.0):
        chips, wide = sizes
        n = len(entries)
        dma = pltpu.SemaphoreType.DMA
        self.sizes, self.absolute, self.number, self.pace = sizes, absolute, number, pace
        self.args, self.where = [], []
        for array, start, cols in entries:
            known = [j for j, a in enumerate(self.args) if a is array]
            if not known:
                self.args.append(array)
            self.where.append((known[0] if known else len(self.args) - 1, start, cols))
        ends = [(array.shape[2], cols) for array, _, cols in entries]
        self.in_specs = [pl.BlockSpec(memory_space=pl.ANY)] * len(self.args)
        self.out_specs = [pl.BlockSpec(memory_space=pltpu.VMEM)] * n
        self.out_shape = [shape_of(e, F32) for e in ends]
        self.scratch = (
            [pltpu.VMEM((wide, chips - 1) + e, BF16) for e in ends]
            + [pltpu.VMEM((wide - 1,) + e, BF16) for e in ends]
            + [pltpu.VMEM((2,) + e, BF16) for e in ends]
            + [
                dma((n, wide, chips - 1)), dma((n, wide, chips - 1)), dma((n, wide - 1)),
                dma((n, wide - 1)), dma((n, 2)),
            ]
        )

    def plan(self, arrays, outs, scratch):
        chips, wide = self.sizes
        absolute, n = self.absolute, len(outs)
        nearby, along, stage = scratch[:n], scratch[n : 2 * n], scratch[2 * n : 3 * n]
        x_send, x_recv, z_send, z_recv, stage_sem = scratch[3 * n :]
        steps, ends = [], []

        def own(w, k, i):
            chip, _, lane = here()
            j, start, cols = self.where[w]
            slot = flip(lane, i) if absolute[w] else i
            if cols == arrays[j].shape[3]:
                return arrays[j].at[flip(chip, k), slot]
            return arrays[j].at[flip(chip, k), slot, :, pl.ds(start, cols)]

        def children(q, i):
            return [k for k in by_distance(chips) if k ^ link_of(k, i) == q]

        def load(w, q, i, turn):
            pltpu.make_async_copy(own(w, q, i), stage[w].at[turn], stage_sem.at[w, turn]).start()

        def total(w, q, i, turn):
            pltpu.make_async_copy(own(w, q, i), stage[w].at[turn], stage_sem.at[w, turn]).wait()
            value = stage[w][turn].astype(F32)
            for k in children(q, i):
                await_bytes(nearby[w].at[i, k - 1], x_recv.at[w, i, k - 1])
                value = value + nearby[w][i, k - 1].astype(F32)
            return value

        def pass_on(source, w, k, i, sent=False):
            chip = here()[0]
            remote(source, nearby[w].at[i, k - 1], {"chip": flip(chip, link_of(k, i))},
                   x_send.at[w, i, k - 1], x_recv.at[w, i, k - 1], sent)

        def relay(w, k, i, turn):
            place = children(k, i)[0] - 1
            nearby[w][i, place] = total(w, k, i, turn).astype(BF16)
            pass_on(nearby[w].at[i, place], w, k, i)

        def onward(w, i, sent=False):
            lane = here()[2]
            remote(nearby[w].at[i, children(0, i)[0] - 1], along[w].at[i - 1], {"ta": flip(lane, i)},
                   z_send.at[w, i - 1], z_recv.at[w, i - 1], sent)

        def finish(w, i, turn):
            value = total(w, 0, i, turn)
            if i == 0:
                outs[w][...] = value
                return
            nearby[w][i, children(0, i)[0] - 1] = value.astype(BF16)
            onward(w, i)

        def last(w):
            value = outs[w][...]
            for i in range(1, wide):
                await_bytes(along[w].at[i - 1], z_recv.at[w, i - 1])
                value = value + along[w][i - 1].astype(F32)
            outs[w][...] = value

        slots = (*range(1, wide), 0)
        sums = []
        raw = {w: [] for w in range(n)}
        for w in range(n):
            for i in slots:
                for k in by_distance(chips)[::-1]:
                    if not children(k, i):
                        raw[w].append(lambda w=w, k=k, i=i: pass_on(own(w, k, i), w, k, i))
                    if children(k, i):
                        ends.append(lambda w=w, k=k, i=i: pass_on(
                            nearby[w].at[i, children(k, i)[0] - 1], w, k, i, True))
                    else:
                        ends.append(lambda w=w, k=k, i=i: pass_on(own(w, k, i), w, k, i, True))
            mine = [(w, k, i) for i in slots for k in by_distance(chips)[::-1] if children(k, i)]
            mine += [(w, 0, i) for i in slots]
            for turn, (_, k, i) in enumerate(mine):
                sums.append((w, k, i, turn % 2))
            for i in range(1, wide):
                ends.append(lambda w=w, i=i: onward(w, i, True))
        steps.append(lambda: greet(chips, wide, False))
        steps += raw[0]
        steps += raw[1] if n > 1 else []
        first = len(steps)
        for w in range(n):
            mine = [t for t in sums if t[0] == w]
            steps.append(lambda t=mine[0]: load(*t))
            for j, (_, k, i, turn) in enumerate(mine):
                if j + 1 < len(mine):
                    steps.append(lambda t=mine[j + 1]: load(*t))
                if k:
                    steps.append(lambda w=w, k=k, i=i, turn=turn: relay(w, k, i, turn))
                else:
                    steps.append(lambda w=w, i=i, turn=turn: finish(w, i, turn))
            if w + 2 < n:
                steps += raw[w + 2]
        for w in range(n):
            steps.append(lambda w=w: last(w))
        return steps + ends, first


def alone(work, name):
    a, o = len(work.args), len(work.out_shape)

    def kernel(*refs):
        for step in work.plan(refs[:a], refs[a : a + o], refs[a + o :])[0]:
            step()

    return pl.pallas_call(
        kernel,
        in_specs=work.in_specs,
        out_specs=work.out_specs,
        out_shape=work.out_shape,
        scratch_shapes=work.scratch,
        compiler_params=pltpu.CompilerParams(
            collective_id=work.number, has_side_effects=True, vmem_limit_bytes=VMEM_LIMIT
        ),
        name=name,
    )(*work.args)


def beside(kernel, args, groups, in_specs, out_specs, out_shape, scratch, name, points, work=None):
    if work is None:
        return pl.pallas_call(
            lambda *refs: kernel(lambda point: None, *refs),
            grid=(groups,), in_specs=in_specs, out_specs=out_specs, out_shape=out_shape,
            scratch_shapes=scratch, compiler_params=params(), name=name,
        )(*args), ()
    a, o, s = len(in_specs), len(out_specs), len(scratch)
    b, p = len(work.args), len(work.out_shape)

    def mixed(*refs):
        ins, refs = refs[:a], refs[a:]
        work_ins, refs = refs[:b], refs[b:]
        outs, refs = refs[:o], refs[o:]
        work_outs, refs = refs[:p], refs[p:]
        steps, first = work.plan(work_ins, work_outs, refs[s:])
        slots = groups * points
        table = [[] for _ in range(slots)]
        table[0] = steps[:first]
        rest = steps[first:]
        until = int(len(rest) * work.pace)
        for j, step in enumerate(rest):
            slot = 1 + j * (slots - 2) // until if j < until else slots - 1
            table[slot].append(step)

        def pulse(point):
            for group in range(groups):
                part = table[group * points + point]
                if part:

                    @pl.when(pl.program_id(0) == group)
                    def _():
                        for step in part:
                            step()

        kernel(pulse, *ins, *outs, *refs[:s])

    out = pl.pallas_call(
        mixed,
        grid=(groups,),
        in_specs=list(in_specs) + work.in_specs,
        out_specs=list(out_specs) + work.out_specs,
        out_shape=list(out_shape) + work.out_shape,
        scratch_shapes=list(scratch) + work.scratch,
        compiler_params=pltpu.CompilerParams(
            dimension_semantics=("arbitrary",), vmem_limit_bytes=VMEM_LIMIT,
            collective_id=work.number, has_side_effects=True,
        ),
        name=name,
    )(*args, *work.args)
    return out[:o], out[o:]


def column_sum(values):
    return jnp.sum(values, axis=0, keepdims=True)


def self_forward_kernel(counts, pulse, x_ref, w_ref, bias_ref, gains, shifts, cosine, sine, low_ref, pre_ref, att_ref,
                        lse_ref, own_ref, other_ref, acc):
    heads, size, own = counts
    step = pl.program_id(0)
    pulse(0)
    width = heads * size
    weights = flat(w_ref)
    packed = dot(x_ref[...], weights[:, : 3 * width], 1, 0) + bias_ref[0]
    pre_ref[0] = packed[:, : 2 * width].astype(BF16)
    value_low = packed[:, 2 * width :].astype(BF16)
    length = packed.shape[0]
    block = min(QUERY_BLOCK, length)
    cos, sin = cosine[...], sine[...]
    queries, keys, mixes, logs = [], [], [], []
    for h in range(heads):
        part = packed[:, h * size : (h + 1) * size]
        hat, _ = head_norm(part)
        turned = hat * gains[0:1, :] + shifts[0:1, :]
        query = ((turned * cos + half_turn(turned) * sin) * (size**-0.5)).astype(BF16)
        part = packed[:, width + h * size : width + (h + 1) * size]
        hat, _ = head_norm(part)
        turned = hat * gains[1:2, :] + shifts[1:2, :]
        key = (turned * cos + half_turn(turned) * sin).astype(BF16)
        value = value_low[:, h * size : (h + 1) * size]
        queries.append(query)
        keys.append(key)
        parts, sums = [], []
        for b in range(length // block):
            scores = dot(key, query[b * block : (b + 1) * block], 1, 1)
            top = jnp.max(scores, axis=0, keepdims=True)
            power = jnp.exp(scores - top)
            total = jnp.sum(power, axis=0, keepdims=True)
            shares = (power * (1.0 / total)).astype(BF16)
            parts.append(jnp.transpose(dot(value, shares, 0, 0)))
            sums.append(top + jnp.log(total))
        mixes.append(jnp.concatenate(parts, axis=0))
        logs.append(jnp.concatenate(sums, axis=1))
    low_ref[0] = jnp.concatenate(queries + keys + [value_low], axis=1)
    att = jnp.concatenate(mixes, axis=1).astype(BF16)
    att_ref[0] = att
    lse_ref[0] = jnp.concatenate(logs, axis=0)
    term = dot(att, weights[:, 3 * width :], 1, 1)

    @pl.when(step == 0)
    def _():
        acc[...] = term

    @pl.when(step > 0)
    def _():
        acc[...] += term

    @pl.when(step == pl.num_programs(0) - 1)
    def _():
        own_ref[...] = acc[:own, :]
        other_ref[...] = acc[own:, :].astype(BF16)
    pulse(1)


def self_forward(x, weights, bias, gains, shifts, cosine, sine, own, work=None):
    length, width = x.shape
    chips, groups, rows, all_cols = weights.shape
    size = gains.shape[1]
    small = all_cols // 4
    cols = 3 * small
    heads = small // size
    return beside(
        functools.partial(self_forward_kernel, (heads, size, own)), (x, weights, bias, gains, shifts, cosine, sine), groups,
        in_specs=[whole(x.shape), of_chips(all_cols, weights.shape), per_step(bias.shape)]
        + [whole(gains.shape), whole(shifts.shape), whole(cosine.shape), whole(sine.shape)],
        out_specs=[
            per_step((groups, length, cols)),
            per_step((groups, length, 2 * small)),
            per_step((groups, length, small)),
            per_step((groups, heads, length)),
            whole((own, width)),
            whole((length - own, width)),
        ],
        scratch=[pltpu.VMEM((length, width), F32)],
        out_shape=[
            shape_of((groups, length, cols), BF16),
            shape_of((groups, length, 2 * small), BF16),
            shape_of((groups, length, small), BF16),
            shape_of((groups, heads, length), F32),
            shape_of((own, width), F32),
            shape_of((length - own, width), BF16),
        ],
        name="self_forward", points=2, work=work,
    )


def attention_back(query, key, value, out_grad, logs, block, limit=None):
    length = query.shape[0]
    key_grad, value_grad, query_parts = None, None, []
    for b in range(length // block):
        rows = slice(b * block, (b + 1) * block)
        query_part, grad_part = query[rows], out_grad[rows]
        scores = dot(key, query_part, 1, 1)
        shares = jnp.exp(scores - logs[:, rows])
        if limit is not None:
            index = lax.broadcasted_iota(jnp.int32, shares.shape, 0)
            shares = jnp.where(index < limit, shares, 0.0)
        share_grad = dot(value, grad_part, 1, 1)
        inner = jnp.sum(shares * share_grad, axis=0, keepdims=True)
        score_grad = (shares * (share_grad - inner)).astype(BF16)
        query_parts.append(jnp.transpose(dot(key, score_grad, 0, 0)))
        key_term = dot(score_grad, query_part, 1, 0)
        value_term = dot(shares.astype(BF16), grad_part, 1, 0)
        key_grad = key_term if b == 0 else key_grad + key_term
        value_grad = value_term if b == 0 else value_grad + value_term
    return jnp.concatenate(query_parts, axis=0), key_grad, value_grad


def self_backward_kernel(counts, pulse, x_t, grad_ref, w_ref, low_ref, pre_ref, att_ref, lse_ref, gains, cosine, sine,
                         w_out, own_ref, other_ref, column_ref, head_ref, acc, grad_t):
    heads, size, own = counts
    step = pl.program_id(0)
    pulse(0)
    width = heads * size
    scale = size**-0.5
    weights = flat(w_ref)
    chips, _, rows, _ = w_ref.shape

    @pl.when(step == 0)
    def _():
        grad_t[...] = jnp.transpose(grad_ref[...])

    out_grad = dot(grad_ref[...], weights[:, 3 * width :], 1, 0).astype(BF16)
    comb_grad = dot(grad_t[...], att_ref[0], 1, 0).astype(BF16)
    cos, sin = cosine[...], sine[...]
    block = min(QUERY_BLOCK, out_grad.shape[0])
    query_grads, key_grads, value_grads = [], [], []
    sums = [None] * 4
    for h in range(heads):
        cut = lambda ref, part: ref[0, :, part * width + h * size : part * width + (h + 1) * size]
        query, key, value = cut(low_ref, 0), cut(low_ref, 1), cut(low_ref, 2)
        dq, dk, dv = attention_back(
            query, key, value, out_grad[:, h * size : (h + 1) * size], lse_ref[0, h : h + 1, :], block
        )
        dq = dq * scale
        dq = dq * cos - half_turn(dq) * sin
        dk = dk * cos - half_turn(dk) * sin
        q_hat, q_inverse = head_norm(cut(pre_ref, 0).astype(F32))
        k_hat, k_inverse = head_norm(cut(pre_ref, 1).astype(F32))
        terms = [column_sum(dq * q_hat), column_sum(dk * k_hat), column_sum(dq), column_sum(dk)]
        sums = terms if h == 0 else [s + t for s, t in zip(sums, terms)]
        query_grads.append(head_norm_back(dq, q_hat, q_inverse, gains[0:1, :]))
        key_grads.append(head_norm_back(dk, k_hat, k_inverse, gains[1:2, :]))
        value_grads.append(dv)
        pulse(h + 1)
    packed = jnp.concatenate(query_grads + key_grads + value_grads, axis=1).astype(BF16)
    column_ref[0] = column_sum(packed.astype(F32))
    term = dot(packed, weights[:, : 3 * width], 1, 1)
    proj_grad = dot(x_t[...], packed, 1, 0).astype(BF16)
    w_out[:, 0] = jnp.concatenate([proj_grad, comb_grad], axis=1).reshape(chips, rows, 4 * width)
    head_sums = jnp.concatenate(sums, axis=0)

    @pl.when(step == 0)
    def _():
        acc[...] = term
        head_ref[...] = head_sums

    @pl.when(step > 0)
    def _():
        acc[...] += term
        head_ref[...] += head_sums

    @pl.when(step == pl.num_programs(0) - 1)
    def _():
        own_ref[...] = acc[:own, :]
        other_ref[...] = acc[own:, :].astype(BF16)
    pulse(heads + 1)


def self_backward(x_t, grad, weights, low, pre, att, lse, gains, cosine, sine, own, work=None):
    width, length = x_t.shape
    chips, groups, rows, all_cols = weights.shape
    size = gains.shape[1]
    small = all_cols // 4
    cols = 3 * small
    heads = small // size
    return beside(
        functools.partial(self_backward_kernel, (heads, size, own)), (x_t, grad, weights, low, pre, att, lse, gains, cosine, sine), groups,
        in_specs=[whole(x_t.shape), whole(grad.shape), of_chips(all_cols, weights.shape)]
        + [per_step(v.shape) for v in (low, pre, att, lse)]
        + [whole(gains.shape), whole(cosine.shape), whole(sine.shape)],
        out_specs=[
            of_chips(all_cols, weights.shape),
            whole((own, width)),
            whole((length - own, width)),
            per_step((groups, 1, cols)),
            whole((4, size)),
        ],
        scratch=[
            pltpu.VMEM((length, width), F32),
            pltpu.VMEM((width, length), BF16),
        ],
        out_shape=[
            shape_of(weights.shape, BF16),
            shape_of((own, width), F32),
            shape_of((length - own, width), BF16),
            shape_of((groups, 1, cols), F32),
            shape_of((4, size), F32),
        ],
        name="self_backward", points=heads + 2, work=work,
    )


def cross_forward_kernel(counts, pulse, x_ref, text_ref, w_ref, memory_w, bias_ref, memory_bias, gains, shifts, low_ref,
                         pre_ref, memory_ref, memory_pre, att_ref, lse_ref, own_ref, other_ref, acc):
    heads, size, own, limit = counts
    step = pl.program_id(0)
    pulse(0)
    width = heads * size
    weights = flat(w_ref)
    pre = dot(x_ref[...], weights[:, :width], 1, 0) + bias_ref[0]
    memory = dot(text_ref[...], flat(memory_w), 1, 0) + memory_bias[0]
    pre_ref[0] = pre.astype(BF16)
    memory_pre[0] = memory[:, :width].astype(BF16)
    value_low = memory[:, width:].astype(BF16)
    length = pre.shape[0]
    block = min(QUERY_BLOCK, length)
    queries, keys, mixes, logs = [], [], [], []
    for h in range(heads):
        cols = slice(h * size, (h + 1) * size)
        hat, _ = head_norm(pre[:, cols])
        query = ((hat * gains[2:3, :] + shifts[2:3, :]) * (size**-0.5)).astype(BF16)
        hat, _ = head_norm(memory[:, cols])
        key = (hat * gains[3:4, :]).astype(BF16)
        value = value_low[:, cols]
        queries.append(query)
        keys.append(key)
        parts, sums = [], []
        for b in range(length // block):
            scores = dot(key, query[b * block : (b + 1) * block], 1, 1)
            index = lax.broadcasted_iota(jnp.int32, scores.shape, 0)
            scores = jnp.where(index < limit, scores, -jnp.inf)
            top = jnp.max(scores, axis=0, keepdims=True)
            power = jnp.exp(scores - top)
            total = jnp.sum(power, axis=0, keepdims=True)
            shares = (power * (1.0 / total)).astype(BF16)
            parts.append(jnp.transpose(dot(value, shares, 0, 0)))
            sums.append(top + jnp.log(total))
        mixes.append(jnp.concatenate(parts, axis=0))
        logs.append(jnp.concatenate(sums, axis=1))
    low_ref[0] = jnp.concatenate(queries, axis=1)
    memory_ref[0] = jnp.concatenate(keys + [value_low], axis=1)
    att = jnp.concatenate(mixes, axis=1).astype(BF16)
    att_ref[0] = att
    lse_ref[0] = jnp.concatenate(logs, axis=0)
    term = dot(att, weights[:, width:], 1, 1)

    @pl.when(step == 0)
    def _():
        acc[...] = term

    @pl.when(step > 0)
    def _():
        acc[...] += term

    @pl.when(step == pl.num_programs(0) - 1)
    def _():
        own_ref[...] = acc[:own, :]
        other_ref[...] = acc[own:, :].astype(BF16)
    pulse(1)


def cross_forward(x, text, weights, memory_w, bias, memory_bias, gains, shifts, own, limit, work=None):
    length, width = x.shape
    groups, small = weights.shape[1], weights.shape[3] // 2
    text_rows = text.shape[0]
    size = gains.shape[1]
    heads = small // size
    saved = [
        ((groups, length, small), BF16),
        ((groups, length, small), BF16),
        ((groups, text_rows, 2 * small), BF16),
        ((groups, text_rows, small), BF16),
        ((groups, length, small), BF16),
        ((groups, heads, length), F32),
    ]
    return beside(
        functools.partial(cross_forward_kernel, (heads, size, own, limit)), (x, text, weights, memory_w, bias, memory_bias, gains, shifts), groups,
        in_specs=[whole(x.shape), whole(text.shape)]
        + [of_chips(v.shape[3], v.shape) for v in (weights, memory_w)]
        + [per_step(bias.shape), per_step(memory_bias.shape), whole(gains.shape), whole(shifts.shape)],
        out_specs=[per_step(s) for s, _ in saved] + [whole((own, width)), whole((length - own, width))],
        scratch=[pltpu.VMEM((length, width), F32)],
        out_shape=[shape_of(*s) for s in saved]
        + [shape_of((own, width), F32), shape_of((length - own, width), BF16)],
        name="cross_forward", points=2, work=work,
    )


def cross_backward_kernel(counts, pulse, x_ref, grad_ref, text_ref, w_ref, memory_w, low_ref, pre_ref, memory_ref,
                          memory_pre, att_ref, lse_ref, gains, w_out, memory_out, own_ref, other_ref, text_out,
                          column_ref, memory_column, head_ref, acc, grad_t, x_t, text_t):
    heads, size, own, limit = counts
    step = pl.program_id(0)
    pulse(0)
    width = heads * size
    scale = size**-0.5
    weights = flat(w_ref)
    chips, _, rows, _ = w_ref.shape

    @pl.when(step == 0)
    def _():
        grad_t[...] = jnp.transpose(grad_ref[...])
        x_t[...] = jnp.transpose(x_ref[...])
        text_t[...] = jnp.transpose(text_ref[...])

    out_grad = dot(grad_ref[...], weights[:, width:], 1, 0).astype(BF16)
    blend_grad = dot(grad_t[...], att_ref[0], 1, 0).astype(BF16)
    block = min(QUERY_BLOCK, out_grad.shape[0])
    query_grads, key_grads, value_grads = [], [], []
    sums = [None] * 3
    for h in range(heads):
        cols = slice(h * size, (h + 1) * size)
        query = low_ref[0, :, cols]
        key = memory_ref[0, :, cols]
        value = memory_ref[0, :, width + h * size : width + (h + 1) * size]
        dq, dk, dv = attention_back(
            query, key, value, out_grad[:, cols], lse_ref[0, h : h + 1, :], block, limit
        )
        dq = dq * scale
        q_hat, q_inverse = head_norm(pre_ref[0, :, cols].astype(F32))
        k_hat, k_inverse = head_norm(memory_pre[0, :, cols].astype(F32))
        terms = [column_sum(dq * q_hat), column_sum(dk * k_hat), column_sum(dq)]
        sums = terms if h == 0 else [s + t for s, t in zip(sums, terms)]
        query_grads.append(head_norm_back(dq, q_hat, q_inverse, gains[2:3, :]))
        key_grads.append(head_norm_back(dk, k_hat, k_inverse, gains[3:4, :]))
        value_grads.append(dv)
        pulse(h + 1)
    packed = jnp.concatenate(query_grads, axis=1).astype(BF16)
    memory_grad = jnp.concatenate(key_grads + value_grads, axis=1).astype(BF16)
    column_ref[0] = column_sum(packed.astype(F32))
    memory_column[0] = column_sum(memory_grad.astype(F32))
    term = dot(packed, weights[:, :width], 1, 1)
    text_term = dot(memory_grad, flat(memory_w), 1, 1)
    query_grad = dot(x_t[...], packed, 1, 0).astype(BF16)
    w_out[:, 0] = jnp.concatenate([query_grad, blend_grad], axis=1).reshape(chips, rows, 2 * width)
    memory_out[:, 0] = dot(text_t[...], memory_grad, 1, 0).astype(BF16).reshape(chips, -1, 2 * width)
    head_sums = jnp.concatenate(sums, axis=0)

    @pl.when(step == 0)
    def _():
        acc[...] = term
        text_out[...] = text_term
        head_ref[...] = head_sums

    @pl.when(step > 0)
    def _():
        acc[...] += term
        text_out[...] += text_term
        head_ref[...] += head_sums

    @pl.when(step == pl.num_programs(0) - 1)
    def _():
        own_ref[...] = acc[:own, :]
        other_ref[...] = acc[own:, :].astype(BF16)
    pulse(heads + 1)


def cross_backward(x, grad, text, weights, memory_w, low, pre, memory, memory_pre, att, lse, gains, own, limit, work=None):
    length, width = x.shape
    groups, small = weights.shape[1], weights.shape[3] // 2
    size = gains.shape[1]
    heads = small // size
    pieces = (weights, memory_w)
    tail = [
        ((own, width), F32, False),
        ((length - own, width), BF16, False),
        (text.shape, F32, False),
        ((groups, 1, small), F32, True),
        ((groups, 1, 2 * small), F32, True),
        ((3, size), F32, False),
    ]
    return beside(
        functools.partial(cross_backward_kernel, (heads, size, own, limit)), (x, grad, text, *pieces, low, pre, memory, memory_pre, att, lse, gains), groups,
        in_specs=[whole(x.shape), whole(grad.shape), whole(text.shape)]
        + [of_chips(p.shape[3], p.shape) for p in pieces]
        + [per_step(v.shape) for v in (low, pre, memory, memory_pre, att, lse)]
        + [whole(gains.shape)],
        out_specs=[of_chips(p.shape[3], p.shape) for p in pieces]
        + [per_step(s) if stepped else whole(s) for s, _, stepped in tail],
        scratch=[
            pltpu.VMEM((length, width), F32),
            pltpu.VMEM((width, length), BF16),
            pltpu.VMEM((width, length), BF16),
            pltpu.VMEM((text.shape[1], text.shape[0]), BF16),
        ],
        out_shape=[shape_of(p.shape, BF16) for p in pieces] + [shape_of(s, d) for s, d, _ in tail],
        name="cross_backward", points=heads + 2, work=work,
    )


def mlp_kernel(own, x_ref, cot_ref, x_t, cot_t, w_ref, rest_ref, bias_ref, w_out, out_own, out_other, back_own, back_other,
               hidden_ref, acc, back):
    step = pl.program_id(0)
    chips, _, rows, cols = w_ref.shape
    tile = cols // 2
    w = jnp.where(step % MLP_CHUNKS == 0, flat(w_ref), flat(rest_ref))
    hidden = dot(x_ref[...], w[:, :tile], 1, 0) + bias_ref[0]
    square = hidden * hidden
    inner = 0.7978845608028654 * hidden * (1.0 + 0.044715 * square)
    curve = jnp.tanh(inner)
    active = (0.5 * hidden * (1.0 + curve)).astype(BF16)
    slope = 0.5 * (1.0 + curve) + 0.5 * hidden * (1.0 - curve * curve) * (
        0.7978845608028654 * (1.0 + 3 * 0.044715 * square)
    )
    hidden_grad = dot(cot_ref[...], w[:, tile:], 1, 0) * slope
    hidden_grad = hidden_grad.astype(BF16)
    hidden_ref[0] = column_sum(hidden_grad.astype(F32))
    out_term = dot(active, w[:, tile:], 1, 1)
    back_term = dot(hidden_grad, w[:, :tile], 1, 1)

    @pl.when(step == 0)
    def _():
        acc[...] = out_term
        back[...] = back_term

    @pl.when(step > 0)
    def _():
        acc[...] += out_term
        back[...] += back_term

    w_out[:, 0, :, :tile] = dot(x_t[...], hidden_grad, 1, 0).astype(BF16).reshape(chips, rows, tile)
    w_out[:, 0, :, tile:] = dot(cot_t[...], active, 1, 0).astype(BF16).reshape(chips, rows, tile)

    @pl.when(step == pl.num_programs(0) - 1)
    def _():
        out_own[...] = acc[:own, :]
        out_other[...] = acc[own:, :].astype(BF16)
        back_own[...] = back[:own, :]
        back_other[...] = back[own:, :].astype(BF16)


def mlp(x, cot, x_t, cot_t, weights, rest, bias, own):
    length, width = x.shape
    chips, groups, rows, tile = weights.shape
    cols = tile * MLP_CHUNKS
    shape = (chips, groups, rows, cols)
    first = pl.BlockSpec((chips, 1, rows, tile), lambda i: (0, i // MLP_CHUNKS, 0, 0))
    others = pl.BlockSpec(
        (chips, 1, rows, tile),
        lambda i: (0, i // MLP_CHUNKS, 0, jnp.maximum(i % MLP_CHUNKS - 1, 0)),
    )
    part = pl.BlockSpec(
        (chips, 1, rows, cols // MLP_CHUNKS), lambda i: (0, i // MLP_CHUNKS, 0, i % MLP_CHUNKS)
    )
    tail = [((own, width), F32), ((length - own, width), BF16)] * 2
    return pl.pallas_call(
        functools.partial(mlp_kernel, own),
        grid=(groups * MLP_CHUNKS,),
        in_specs=[whole(v.shape) for v in (x, cot, x_t, cot_t)] + [first, others, per_step(bias.shape)],
        out_specs=[part] + [whole(s) for s, _ in tail] + [per_step(bias.shape)],
        scratch_shapes=[pltpu.VMEM((length, width), F32), pltpu.VMEM((length, width), F32)],
        out_shape=[shape_of(shape, BF16)]
        + [shape_of(*s) for s in tail]
        + [shape_of(bias.shape, F32)],
        compiler_params=params(),
        name="mlp",
    )(x, cot, x_t, cot_t, weights, rest, bias)


def row_spec(block, width):
    return pl.BlockSpec((block, width), lambda i, *_: (i, 0))


def merge_kernel(latent_ref, skip_ref, merger_ref, gains, biases, out_ref):
    left, right, _ = joined_norm(latent_ref, skip_ref)
    width = left.shape[1]
    left = (left * gains[0:1, :] + biases[0:1, :]).astype(BF16)
    right = (right * gains[1:2, :] + biases[1:2, :]).astype(BF16)
    total = dot(left, merger_ref[:width, :], 1, 0) + dot(right, merger_ref[width:, :], 1, 0)
    out_ref[...] = (total + biases[5:6, :]).astype(BF16)


def joined_norm(latent_ref, skip_ref):
    left, right = latent_ref[...].astype(F32), skip_ref[...].astype(F32)
    scale = 0.5 / left.shape[1]
    mean = (jnp.sum(left, axis=-1, keepdims=True) + jnp.sum(right, axis=-1, keepdims=True)) * scale
    left, right = left - mean, right - mean
    spread = jnp.sum(left * left, axis=-1, keepdims=True) + jnp.sum(right * right, axis=-1, keepdims=True)
    inverse = lax.rsqrt(spread * scale + EPSILON)
    return left * inverse, right * inverse, inverse


def merge(latents, skips, merger, gains, biases, block=128):
    rows, width = latents.shape
    return pl.pallas_call(
        merge_kernel,
        grid=(rows // block,),
        in_specs=[row_spec(block, width)] * 2
        + [whole(merger.shape), whole(gains.shape), whole(biases.shape)],
        out_specs=row_spec(block, width),
        out_shape=shape_of((rows, width), BF16),
        compiler_params=params(),
        name="merge",
    )(latents, skips, merger, gains, biases)


def merge_back_kernel(latent_ref, skip_ref, low_ref, merger, gains, biases, left_out, right_out, merge_in, sums):
    left, right, inverse = joined_norm(latent_ref, skip_ref)
    width = left.shape[1]
    low = low_ref[...]
    scale = 0.5 / width
    left_grad = dot(low, merger[:width, :], 1, 1)
    right_grad = dot(low, merger[width:, :], 1, 1)
    merge_in[:, :width] = (left * gains[0:1, :] + biases[0:1, :]).astype(BF16)
    merge_in[:, width:] = (right * gains[1:2, :] + biases[1:2, :]).astype(BF16)
    terms = jnp.concatenate(
        [
            column_sum(left_grad * left),
            column_sum(right_grad * right),
            column_sum(left_grad),
            column_sum(right_grad),
            column_sum(low.astype(F32)),
        ],
        axis=0,
    )
    left_grad, right_grad = left_grad * gains[0:1, :], right_grad * gains[1:2, :]
    first = jnp.sum(left_grad, axis=-1, keepdims=True) + jnp.sum(right_grad, axis=-1, keepdims=True)
    second = jnp.sum(left_grad * left, axis=-1, keepdims=True) + jnp.sum(
        right_grad * right, axis=-1, keepdims=True
    )
    first, second = first * scale, second * scale
    left_out[...] = inverse * (left_grad - first - left * second)
    right_out[...] = inverse * (right_grad - first - right * second)

    @pl.when(pl.program_id(0) == 0)
    def _():
        sums[...] = terms

    @pl.when(pl.program_id(0) > 0)
    def _():
        sums[...] += terms


def merge_back(latents, skips, low, merger, gains, biases, block=128):
    rows, width = latents.shape
    return pl.pallas_call(
        merge_back_kernel,
        grid=(rows // block,),
        in_specs=[row_spec(block, width)] * 3
        + [whole(merger.shape), whole(gains.shape), whole(biases.shape)],
        out_specs=[row_spec(block, width)] * 2 + [row_spec(block, 2 * width), whole((5, width))],
        out_shape=[
            shape_of((rows, width), F32),
            shape_of((rows, width), F32),
            shape_of((rows, 2 * width), BF16),
            shape_of((5, width), F32),
        ],
        compiler_params=params(),
        name="merge_back",
    )(latents, skips, low, merger, gains, biases)


def norm_kernel(count, keep, *refs):
    parts, rows, outs = refs[:count], refs[count], refs[count + 1 :]
    total = parts[0][...].astype(F32)
    for part in parts[1:]:
        total = total + part[...].astype(F32)
    total = total + rows[0:1, :]
    hat, _ = head_norm(total)
    outs[0][...] = (hat * rows[1:2, :] + rows[2:3, :]).astype(BF16)
    if keep:
        outs[1][...] = total


def norm(parts, rows, keep=True, block=128):
    length, width = parts[0].shape
    out = pl.pallas_call(
        functools.partial(norm_kernel, len(parts), keep),
        grid=(length // block,),
        in_specs=[row_spec(block, width)] * len(parts) + [whole(rows.shape)],
        out_specs=[row_spec(block, width)] * (1 + keep),
        out_shape=[shape_of((length, width), BF16)] + [shape_of((length, width), F32)] * keep,
        compiler_params=params(),
        name="norm",
    )(*parts, rows)
    return out if keep else out[0]


def norm_back_kernel(count, keep, *refs):
    parts, value_ref, carried, gain = refs[:count], refs[count], refs[count + 1], refs[count + 2]
    outs = refs[count + 3 :]
    grad = parts[0][...].astype(F32)
    for part in parts[1:]:
        grad = grad + part[...].astype(F32)
    hat, inverse = head_norm(value_ref[...].astype(F32))
    total = carried[...].astype(F32) + head_norm_back(grad, hat, inverse, gain[...])
    low = total.astype(BF16)
    outs[0][...] = low
    if keep:
        outs[2][...] = total
    terms = jnp.concatenate(
        [column_sum(grad * hat), column_sum(grad), column_sum(low.astype(F32))], axis=0
    )
    sums = outs[1]

    @pl.when(pl.program_id(0) == 0)
    def _():
        sums[...] = terms

    @pl.when(pl.program_id(0) > 0)
    def _():
        sums[...] += terms


def norm_back(parts, value, carried, gain, keep=True, block=128):
    length, width = value.shape
    return pl.pallas_call(
        functools.partial(norm_back_kernel, len(parts), keep),
        grid=(length // block,),
        in_specs=[row_spec(block, width)] * (len(parts) + 2) + [whole(gain.shape)],
        out_specs=[row_spec(block, width), whole((3, width))] + [row_spec(block, width)] * keep,
        out_shape=[shape_of((length, width), BF16), shape_of((3, width), F32)]
        + [shape_of((length, width), F32)] * keep,
        compiler_params=params(),
        name="norm_back",
    )(*parts, value, carried, gain)


def body(sizes, latents, skips, text_states, time_embedding, merger, modulator, norm_gains, norm_biases,
         output_bias, projector, combiner, cross_query, cross_memory, blender, expander, reducer,
         column_biases, hidden_bias, per_head_norm_gains, head_shifts, cotangent):
    chips, wide, deep = sizes
    chip_index, core, lane, side = (lax.axis_index(n) for n in ("chip", "core", "ta", "tb"))
    shard_len, local, width = latents.shape
    size = per_head_norm_gains.shape[1]
    text_len, text_width = text_states.shape[1:]
    own_len = shard_len * local
    seq_len = shard_len * wide * deep
    devices = chips * 2 * wide * deep
    latent_total = chips * 2 * local
    half_len = shard_len // 2
    tensor_cols = projector.shape[2]
    head_cols = tensor_cols // 2
    hidden_cols = expander.shape[1] // 2
    chip_bits, wide_bits, deep_bits = bits_of(chips), bits_of(wide)[::-1], bits_of(deep)

    everywhere = [("ta", wide, b) for b in bits_of(wide)] + [("tb", deep, b) for b in deep_bits]
    everywhere = [("core", 2, 1)] + everywhere + [("chip", chips, b) for b in chip_bits]
    index_of = {"chip": chip_index, "core": core, "ta": lane, "tb": side}

    def at(value, index, axis=0):
        return lax.dynamic_index_in_dim(value, index, axis, keepdims=False)

    def gather_all(value):
        value = value[None, None, None, None]
        dims = {"chip": 0, "core": 1, "ta": 2, "tb": 3}
        shape = [1, 1, 1, 1]
        for axis, extent, mask in everywhere:
            value = value.reshape((*shape, *value.shape[4:]))
            other = swap(value, axis, extent, mask)
            high = (index_of[axis] & mask) > 0
            low_part = jnp.where(high, other, value)
            high_part = jnp.where(high, value, other)
            value = jnp.concatenate([low_part, high_part], axis=dims[axis])
            shape[dims[axis]] *= 2
        return value

    def sum_scatter_all(value):
        dims = {"chip": 0, "core": 1, "ta": 2, "tb": 3}
        for axis, extent, mask in everywhere[::-1]:
            dim = dims[axis]
            rows = value.shape[dim] // 2
            high = (index_of[axis] & mask) > 0
            low_part = lax.slice_in_dim(value, 0, rows, axis=dim)
            high_part = lax.slice_in_dim(value, rows, 2 * rows, axis=dim)
            kept = jnp.where(high, high_part, low_part)
            value = kept + swap(jnp.where(high, low_part, high_part), axis, extent, mask)
        return value.reshape(value.shape[4:])

    def halves(value):
        mine, other = at(value, core, 1), at(value, 1 - core, 1)
        other = swap(other, "core", 2, 1)
        pair = jnp.where(core == 0, jnp.stack([mine, other]), jnp.stack([other, mine]))
        return pair.reshape((-1,) + pair.shape[2:])

    def unhalves(value):
        value = value.reshape((2, -1) + value.shape[1:])
        mine, other = at(value, core), at(value, 1 - core)
        other = swap(other, "core", 2, 1)
        return jnp.where(core == 0, jnp.stack([mine, other], 1), jnp.stack([other, mine], 1))

    small = jnp.concatenate(
        [v.reshape(-1) for v in (norm_gains, norm_biases, output_bias, column_biases, hidden_bias)]
    )
    times = time_embedding
    silu_own = jax.nn.silu(times.astype(F32)).astype(BF16)
    small = jnp.concatenate([small, silu_own.astype(F32).reshape(-1)])[None]
    rows, tile = projector.shape[0], hidden_cols // MLP_CHUNKS
    mesh_sizes = (chips, wide)

    def with_tb(value):
        value = value[None]
        for mask in deep_bits:
            other = swap(value, "tb", deep, mask)
            high = (side & mask) > 0
            value = jnp.concatenate(
                [jnp.where(high, other, value), jnp.where(high, value, other)], axis=0
            )
        return value.reshape((-1,) + value.shape[2:])

    self_in = jnp.concatenate([projector, combiner.T[:, None]], axis=1)
    self_in = halves(self_in.reshape(rows, 4, 2, head_cols).transpose(0, 2, 1, 3)).reshape(2 * rows, -1)
    small_all, merger_full, modulator_full, self_w = alone(
        Gather(mesh_sizes, [with_tb(small), with_tb(merger), with_tb(modulator), self_in], (True, True, True, False), 1),
        "gather",
    )
    merger_full = merger_full.reshape(2 * width, width)
    modulator_full = modulator_full.reshape(width, width)
    small_all = small_all.reshape(devices, -1)
    part = norm_gains.shape[1]
    hidden_part = hidden_bias.shape[0]
    table = jnp.transpose(small_all[:, : 21 * part].reshape(devices, 21, part), (1, 0, 2)).reshape(21, width)
    gains, biases, out_bias, columns = table[:5], table[5:14], table[14:15], table[15:21]
    silu_at = 21 * part + hidden_part
    hidden_all = small_all[:, 21 * part : silu_at].reshape(wide, deep, 2, hidden_cols)
    silu_all = small_all[:, silu_at:].reshape(chips * 2, wide * deep, local, width)[:, 0]
    silu_all = silu_all.reshape(latent_total, width).astype(BF16)

    def own_columns(value):
        value = value.reshape(value.shape[0], wide, deep, 2, -1)
        value = at(at(value, side, 2), core, 2)
        return jnp.stack([at(value, lane ^ i, 1) for i in range(wide)])

    def all_columns(value):
        value = jnp.stack([at(value, lane ^ i) for i in range(wide)], axis=1)
        there = (jnp.arange(deep) == side)[:, None] & (jnp.arange(2) == core)[None, :]
        value = jnp.where(there[None, None, :, :, None], value[:, :, None, None, :], 0.0)
        return value.reshape(value.shape[0], -1)

    own_biases = own_columns(columns)

    text_rows_w = cross_memory.shape[0]
    cross_in = jnp.stack([cross_query, blender.T], axis=1)
    cross_in = halves(cross_in.reshape(rows, 2, 2, head_cols).transpose(0, 2, 1, 3)).reshape(2 * rows, -1)
    memory_in = halves(cross_memory.reshape(text_rows_w, 2, 2, head_cols).transpose(0, 2, 1, 3))
    memory_in = memory_in.reshape(2 * text_rows_w, 2 * head_cols)
    mlp_in = jnp.stack([expander, reducer.T], axis=1).reshape(rows, 2, 2, MLP_CHUNKS, tile)
    mlp_in = halves(mlp_in.transpose(0, 2, 3, 1, 4)).reshape(2 * rows, 2 * hidden_cols)
    mlp_parts = [mlp_in[:, : 2 * tile], mlp_in[:, 2 * tile :]]

    mod_rows = modulator.shape[0]
    device = ((chip_index * 2 + core) * wide + lane) * deep + side
    silu_cols = at(silu_all.reshape(latent_total, devices, mod_rows), device, 1)
    silu_mine = lax.dynamic_slice_in_dim(silu_all, chip_index * 2 * local + lane, 1, 0)
    mod = jnp.dot(silu_mine, modulator_full, preferred_element_type=F32)

    def to_latent(value):
        value = value.reshape(local, 2, half_len, width)
        mine, other = at(value, core, 1), at(value, 1 - core, 1)
        other = swap(other, "core", 2, 1)
        pair = jnp.where(core == 0, jnp.stack([mine, other]), jnp.stack([other, mine]))
        return exchange(pair.reshape(wide, half_len, width)).reshape(own_len, width)

    def from_latent(value):
        pair = exchange(value.reshape(wide, half_len, width)).reshape(2, local, half_len, width)
        mine, other = at(pair, core), at(pair, 1 - core)
        other = swap(other, "core", 2, 1)
        value = jnp.where(core == 0, jnp.stack([mine, other], 1), jnp.stack([other, mine], 1))
        return value.reshape(own_len, width)

    def exchange(value):
        own = at(value, lane)
        parts = [own] + [
            swap(at(value, lane ^ mask), "ta", wide, mask) for mask in range(1, wide)
        ]
        parts = jnp.stack(parts)
        return jnp.stack([at(parts, lane ^ i) for i in range(wide)])

    def gather_tokens(value):
        value = jnp.concatenate([value, swap(value, "core", 2, 1)], axis=0)
        for mask in deep_bits:
            value = jnp.concatenate([value, swap(value, "tb", deep, mask)], axis=0)
        return value

    def scatter_tokens(other):
        terms = []
        rest = other
        for mask in deep_bits[::-1]:
            rows_sent = (own_len * 2 * deep) // 2
            kept = rest.shape[0] - rows_sent
            received = swap(rest[kept:], "tb", deep, mask)
            terms.append(received[:own_len])
            rest = (rest[:kept].astype(F32) + received[own_len:].astype(F32)).astype(BF16)
        terms.append(swap(rest, "core", 2, 1))
        return terms

    latents_flat = jnp.transpose(latents, (1, 0, 2)).reshape(own_len, width)
    skips_flat = jnp.transpose(skips, (1, 0, 2)).reshape(own_len, width)
    first_local = merge(latents_flat, skips_flat, merger_full, gains, biases)
    first = to_latent(first_local)
    cot = to_latent(jnp.transpose(cotangent, (1, 0, 2)))
    cot_all = gather_tokens(cot)

    block_index = jnp.arange(wide)[:, None]
    inside = jnp.arange(half_len)[None, :]
    places = []
    for b in range(deep):
        for c in range(2):
            slot = (block_index * deep + (side ^ b)) * 2 + (core ^ c)
            places.append((slot * half_len + inside).reshape(-1))
    places = jnp.concatenate(places)
    quarter = size // 4
    frequency = THETA ** (-2.0 * jnp.arange(quarter).astype(F32) / (size // 2))
    row_angle = (places // GRID_W).astype(F32)[:, None] * frequency
    column_angle = (places % GRID_W).astype(F32)[:, None] * frequency
    angles = jnp.concatenate([row_angle, row_angle, column_angle, column_angle], axis=1)
    sign = jnp.where((jnp.arange(size) // quarter) % 2 == 0, -1.0, 1.0)
    cosine, sine = jnp.cos(angles), jnp.sin(angles) * sign

    zero_row = jnp.zeros((1, width), F32)
    rows_of = lambda *parts: jnp.concatenate(parts, axis=0)
    x_self = gather_tokens(
        norm([first], rows_of(zero_row, gains[2:3], biases[2:3] + biases[6:7] + mod), keep=False)
    )
    self_bias = own_biases[:, 0:3].reshape(wide, 1, 3 * head_cols)
    outs, (cross_w, memory_w, mlp_first) = self_forward(
        x_self, self_w, self_bias, per_head_norm_gains, head_shifts, cosine, sine, own_len,
        Gather(mesh_sizes, [cross_in, memory_in, mlp_parts[0]], (False,) * 3, 2, PACES[0]),
    )
    self_low, self_pre, self_att, self_lse, part_own, part_other = outs
    x_cross, second = norm(
        [first, part_own, *scatter_tokens(part_other)], rows_of(biases[7:8], gains[3:4], biases[3:4])
    )
    x_cross = gather_tokens(x_cross)

    text_pad = -text_len % 16
    text_mine = at(text_states, lane % local)
    text_other = swap(text_mine, "core", 2, 1)
    text = jnp.where(core == lane // local, text_mine, text_other)
    text = jnp.pad(text, ((0, text_pad), (0, 0)))
    cross_bias = own_biases[:, 3:4]
    memory_bias = own_biases[:, 4:6].reshape(wide, 1, 2 * head_cols)
    outs, (mlp_rest,) = cross_forward(
        x_cross, text, cross_w, memory_w, cross_bias, memory_bias,
        per_head_norm_gains, head_shifts, own_len, text_len,
        Gather(mesh_sizes, [mlp_parts[1]], (False,), 3, PACES[1]),
    )
    cross_low, cross_pre, memory_low, memory_pre, cross_att, cross_lse, part_own, part_other = outs
    x_mlp, third = norm(
        [second, part_own, *scatter_tokens(part_other)], rows_of(biases[8:9], gains[4:5], biases[4:5])
    )
    x_mlp = gather_tokens(x_mlp)

    own_hidden = at(at(hidden_all, side, 1), core, 1)
    own_hidden = jnp.stack([at(own_hidden, lane ^ i) for i in range(wide)]).reshape(wide * MLP_CHUNKS, 1, tile)
    mlp_g, out_own, out_other, back_own, back_other, hidden_sum = mlp(
        x_mlp, cot_all, x_mlp.T, cot_all.T, mlp_first, mlp_rest, own_hidden, own_len
    )
    mlp_entries = [(mlp_g, 2 * tile * j, 2 * tile) for j in range(MLP_CHUNKS)]
    outs = [third, out_own, *scatter_tokens(out_other)]
    backs = [back_own, *scatter_tokens(back_other)]
    block_total = sum(v.astype(F32) for v in outs) + out_bias
    block_out = from_latent(block_total.astype(BF16))

    third_low, mlp_sums, third_grad = norm_back(backs, third, cot, gains[4:5])
    blender_g_in = gather_tokens(third_low)
    outs, mlp_grad_first = cross_backward(
        x_cross, blender_g_in, text, cross_w, memory_w, cross_low, cross_pre,
        memory_low, memory_pre, cross_att, cross_lse, per_head_norm_gains, own_len, text_len,
        Scatter(mesh_sizes, mlp_entries[:1], (False,), 4, PACES[2]),
    )
    cross_g, memory_g, part_own, part_other, text_part, query_col, memory_col, cross_heads = outs
    second_low, cross_sums, second_grad = norm_back(
        [part_own, *scatter_tokens(part_other)], second, third_grad, gains[3:4]
    )
    outs, mlp_grad_rest = self_backward(
        x_self.T, gather_tokens(second_low), self_w, self_low, self_pre, self_att,
        self_lse, per_head_norm_gains, cosine, sine, own_len,
        Scatter(mesh_sizes, mlp_entries[1:], (False,) * (MLP_CHUNKS - 1), 5, PACES[3]),
    )
    self_g, part_own, part_other, self_col, self_heads = outs
    first_low, self_sums = norm_back(
        [part_own, *scatter_tokens(part_other)], first, second_grad, gains[2:3], keep=False
    )
    low_local = from_latent(first_low)
    left, right, merge_in, merge_sums = merge_back(
        latents_flat, skips_flat, low_local, merger_full, gains, biases
    )
    merger_g = dot(merge_in, low_local, 0, 0).astype(BF16).reshape(chips, 2, -1, width)
    mine, other = at(merger_g, core, 1), at(merger_g, 1 - core, 1)
    value = mine.astype(F32) + swap(other, "core", 2, 1).astype(F32)
    value = value.reshape(chips, wide, deep, -1, width)
    for mask in deep_bits[::-1]:
        low_part, high_part = jnp.split(value, 2, axis=2)
        high = (side & mask) > 0
        sent = jnp.where(high, low_part, high_part).astype(BF16)
        value = jnp.where(high, high_part, low_part) + swap(sent, "tb", deep, mask).astype(F32)
    merger_g = value.astype(BF16).reshape(chips, wide, -1, width)
    self_grad, cross_grad, memory_grads, merger_grads = alone(
        Scatter(
            mesh_sizes, [(v, 0, v.shape[3]) for v in (self_g, cross_g, memory_g, merger_g)],
            (False, False, False, True), 6,
        ),
        "scatter",
    )
    cross_grad = unhalves(cross_grad.reshape(2 * rows, 2, head_cols)).transpose(2, 0, 1, 3)
    query_grads = cross_grad[0].reshape(rows, tensor_cols)
    blender_grads = cross_grad[1].reshape(rows, tensor_cols).T
    memory_grads = unhalves(memory_grads.reshape(2 * text_rows_w, 2, head_cols))
    memory_grads = memory_grads.transpose(0, 2, 1, 3).reshape(text_rows_w, 2, tensor_cols)
    self_grad = unhalves(self_grad.reshape(2 * rows, 4, head_cols)).transpose(0, 2, 1, 3)
    projector_grads = self_grad[:, :3].reshape(rows, 3, tensor_cols)
    combiner_grads = self_grad[:, 3].reshape(rows, tensor_cols).T

    mlp_grad = jnp.stack([*mlp_grad_first, *mlp_grad_rest], axis=1)
    mlp_grad = unhalves(mlp_grad.reshape(2 * rows, MLP_CHUNKS, 2, tile)).transpose(3, 0, 1, 2, 4)
    expander_grads = mlp_grad[0].reshape(rows, 2 * hidden_cols)
    reducer_grads = mlp_grad[1].reshape(rows, 2 * hidden_cols).T

    text_sum = text_part
    for axis, extent, mask in [("core", 2, 1)] + [("tb", deep, b) for b in deep_bits]:
        text_sum = text_sum + swap(text_sum.astype(BF16), axis, extent, mask).astype(F32)
    text_sum = text_sum[:text_len].astype(BF16).reshape(text_len, wide, deep, -1)
    text_sum = at(text_sum, side, 2).transpose(1, 0, 2)
    text_got = exchange(text_sum)
    text_grads = lax.dynamic_slice_in_dim(text_got, core * local, local, 0).astype(F32)

    mod_grad = self_sums[1:2]
    for axis, extent, mask in [("core", 2, 1)] + [("tb", deep, b) for b in deep_bits]:
        mod_grad = mod_grad + swap(mod_grad, axis, extent, mask)
    mod_all = mod_grad[None]
    for mask in bits_of(wide):
        other = swap(mod_all, "ta", wide, mask)
        high = (lane & mask) > 0
        mod_all = jnp.concatenate([jnp.where(high, other, mod_all), jnp.where(high, mod_all, other)], axis=1)
    for mask in chip_bits:
        other = swap(mod_all, "chip", chips, mask)
        high = (chip_index & mask) > 0
        mod_all = jnp.concatenate([jnp.where(high, other, mod_all), jnp.where(high, mod_all, other)], axis=0)
    mod_all = mod_all.reshape(latent_total, width)
    exact = lax.Precision.HIGHEST
    modulator_grads = lax.dot_general(
        silu_cols.astype(F32), mod_all, (((0,), (0,)), ((), ())), precision=exact
    )
    mod_own = lax.dynamic_slice_in_dim(mod_all, (chip_index * 2 + core) * local, local, 0)
    cols_own = width // (wide * deep)
    tensor_index = lane * deep + side
    modulator_own = lax.dynamic_slice_in_dim(modulator_full, tensor_index * cols_own, cols_own, 0)
    time_own = lax.dot_general(
        mod_own, modulator_own.astype(F32), (((1,), (1,)), ((), ())), precision=exact
    )
    times_own = lax.dynamic_slice_in_dim(times, tensor_index * cols_own, cols_own, 1).astype(F32)
    _, silu_pull = jax.vjp(jax.nn.silu, times_own)
    time_grads = silu_pull(time_own)[0]

    output_sum = jnp.sum(cotangent.astype(F32), axis=(0, 1))[None]
    columns_own = jnp.concatenate(
        [self_col.reshape(wide, 3, head_cols), query_col, memory_col.reshape(wide, 2, head_cols)], axis=1
    )
    sums = jnp.concatenate(
        [
            merge_sums[0:2], self_sums[0:1], cross_sums[0:1], mlp_sums[0:1],
            merge_sums[2:4], self_sums[1:2], cross_sums[1:2], mlp_sums[1:2],
            merge_sums[4:5], self_sums[1:2], cross_sums[2:3], mlp_sums[2:3],
            output_sum, all_columns(columns_own),
        ],
        axis=0,
    )
    hidden_sum = hidden_sum.reshape(wide, 1, hidden_cols)
    hidden_sum = all_columns(hidden_sum)
    sums = jnp.transpose(sums.reshape(21, devices, part), (1, 0, 2)).reshape(devices, -1)
    both = jnp.concatenate([sums, hidden_sum.reshape(devices, hidden_part)], axis=1)
    both = sum_scatter_all(both.reshape(chips, 2, wide, deep, -1))
    table = both[: 21 * part].reshape(21, part)
    hidden_grads = both[21 * part :]
    head_sums = jnp.concatenate(
        [self_heads[0:2], cross_heads[0:2], self_heads[2:4], cross_heads[2:3]], axis=0
    )
    for axis, extent, mask in everywhere:
        head_sums = head_sums + swap(head_sums, axis, extent, mask)

    def to_local(value):
        return jnp.transpose(value.reshape(local, shard_len, width), (1, 0, 2)).astype(F32)

    return (
        to_local(block_out), to_local(left), to_local(right), text_grads, time_grads, merger_grads,
        modulator_grads, table[0:5], table[5:14], table[14], projector_grads, combiner_grads, query_grads,
        memory_grads, blender_grads, expander_grads, reducer_grads, table[15:21], hidden_grads,
        head_sums[0:4], head_sums[4:7],
    )


def solution(mesh):
    data, tensor = mesh.shape["dp"], mesh.shape["tensor"]

    def run(*arrays):
        local = arrays[0].shape[1] // data
        wide = min(tensor, 2 * local)
        deep = tensor // wide
        grid = Mesh(
            mesh.devices.reshape(data // 2, 2, wide, deep), ("chip", "core", "ta", "tb")
        )
        dp, tp = ("chip", "core"), ("ta", "tb")
        both = dp + tp
        tokens = P(tp, dp, None)
        in_specs = (
            tokens, tokens, P(dp, None, None), P(dp, None), P(both, None), P(both, None), P(None, both),
            P(None, both), P(both), P(dp, None, tp), P(tp, dp), P(dp, tp), P(dp, None, tp), P(tp, dp),
            P(dp, tp), P(tp, dp), P(None, both), P(both), P(), P(), tokens,
        )
        out_specs = (
            tokens, tokens, tokens, P(dp, None, tp), P(dp, tp), P(both, None), P(both, None),
            P(None, both), P(None, both), P(both), P(dp, None, tp), P(tp, dp), P(dp, tp),
            P(dp, None, tp), P(tp, dp), P(dp, tp), P(tp, dp), P(None, both), P(both), P(), P(),
        )
        return jax.shard_map(
            functools.partial(body, (data // 2, wide, deep)),
            mesh=grid, in_specs=in_specs, out_specs=out_specs, check_vma=False,
        )(*arrays)

    return run
```

```python
import functools

import jax
import jax.numpy as jnp
from jax import lax
from jax.experimental import pallas as pl
from jax.experimental.pallas import tpu as pltpu
from jax.sharding import Mesh, PartitionSpec as P

GRID_W = 32
EPSILON = 1e-06
THETA = 10000.0
F32 = jnp.float32
BF16 = jnp.bfloat16
VMEM_LIMIT = 62 * 1024 * 1024
MLP_CHUNKS = 3
PACES = (0.7, 0.4, 0.8, 0.8)
QUERY_BLOCK = 512
MESH = pl.DeviceIdType.MESH


def bits_of(size):
    return [1 << i for i in range(size.bit_length() - 1)]


def swap(value, axis, size, mask):
    return lax.ppermute(value, axis, [(i, i ^ mask) for i in range(size)])


def dot(left, right, left_dim, right_dim):
    return lax.dot_general(
        left, right, (((left_dim,), (right_dim,)), ((), ())), preferred_element_type=F32
    )


def params(count=1):
    return pltpu.CompilerParams(
        dimension_semantics=("arbitrary",) * count, vmem_limit_bytes=VMEM_LIMIT
    )


def whole(shape):
    zeros = (0,) * len(shape)
    return pl.BlockSpec(shape, lambda *_: zeros, pipeline_mode=pl.Buffered(1))


def per_step(shape):
    rest = (0,) * (len(shape) - 1)
    return pl.BlockSpec((1,) + tuple(shape[1:]), lambda i, *_: (i,) + rest)


def shape_of(shape, dtype):
    return jax.ShapeDtypeStruct(shape, dtype)


def head_norm(values):
    width = values.shape[-1]
    centred = values - jnp.sum(values, axis=-1, keepdims=True) * (1.0 / width)
    inverse = lax.rsqrt(
        jnp.sum(centred * centred, axis=-1, keepdims=True) * (1.0 / width) + EPSILON
    )
    return centred * inverse, inverse


def head_norm_back(grad, hat, inverse, gain):
    scale = 1.0 / grad.shape[-1]
    scaled = grad * gain
    first = jnp.sum(scaled, axis=-1, keepdims=True) * scale
    second = jnp.sum(scaled * hat, axis=-1, keepdims=True) * scale
    return inverse * (scaled - first - hat * second)


def half_turn(values):
    quarter = values.shape[-1] // 4
    part = [values[:, i * quarter : (i + 1) * quarter] for i in range(4)]
    return jnp.concatenate([part[1], part[0], part[3], part[2]], axis=1)


def of_chips(width, shape):
    return pl.BlockSpec(shape[:1] + (1,) + shape[2:3] + (width,), lambda i, *_: (0, i, 0, 0))


def flat(ref):
    chips, _, rows, cols = ref.shape
    return ref[...].reshape(chips * rows, cols)


def flip(index, mask):
    for bit in bits_of(2 * mask + 1):
        if mask & bit:
            index = index + bit - 2 * bit * (index // bit % 2)
    return index


def link_of(k, slot):
    bits = [b for b in bits_of(2 * k + 1) if k & b]
    return bits[-1] if slot % 2 == 0 else bits[0]


def by_distance(chips):
    return sorted(range(1, chips), key=lambda k: (bin(k).count("1"), k))


def greet(chips, wide, with_core):
    chip, core, lane = (lax.axis_index(n) for n in ("chip", "core", "ta"))
    barrier = pltpu.get_barrier_semaphore()
    partners = [{"ta": flip(lane, i)} for i in range(1, wide)]
    partners += [{"chip": flip(chip, b)} for b in bits_of(chips)]
    if with_core:
        partners.append({"core": 1 - core})
    for partner in partners:
        pl.semaphore_signal(barrier, inc=1, device_id=partner, device_id_type=MESH)
    pl.semaphore_wait(barrier, len(partners))


def remote(source, target, device, send_sem, recv_sem, sent):
    copy = pltpu.make_async_remote_copy(
        src_ref=source, dst_ref=target, send_sem=send_sem, recv_sem=recv_sem,
        device_id=device, device_id_type=MESH,
    )
    if sent:
        copy.wait_send()
    else:
        copy.start()


def await_bytes(ref, sem):
    pltpu.make_async_copy(ref, ref, sem).wait()


def here():
    return tuple(lax.axis_index(name) for name in ("chip", "core", "ta"))


class Gather:
    def __init__(self, sizes, shards, full, number, pace=1.0):
        chips, wide = sizes
        n = len(shards)
        dma = pltpu.SemaphoreType.DMA
        self.sizes, self.full, self.number, self.pace = sizes, full, number, pace
        self.args = list(shards)
        self.in_specs = [pl.BlockSpec(memory_space=pltpu.VMEM)] * n
        self.out_specs = [pl.BlockSpec(memory_space=pl.ANY)] * n
        self.out_shape = [
            shape_of(((chips, 2, wide) if f else (chips, wide)) + tuple(v.shape), v.dtype)
            for v, f in zip(shards, full)
        ]
        self.scratch = [
            dma((n,)), dma((n, wide - 1)), dma((n, wide - 1)), dma((n, wide, chips - 1)),
            dma((n, wide, chips - 1)), dma((n, chips)), dma((n, chips)),
        ]

    def plan(self, shards, outs, scratch):
        chips, wide = self.sizes
        full, n = self.full, len(shards)
        local_sem, z_send, z_recv, x_send, x_recv, c_send, c_recv = scratch
        steps, ends, placed, arrived = [], [], [], set()

        def place(w, k, i):
            chip, core, lane = here()
            if full[w]:
                return outs[w].at[flip(chip, k), core, flip(lane, i)]
            return outs[w].at[flip(chip, k), i]

        def take(w, k, i):
            if k == 0 and i == 0 or (w, k, i) in arrived:
                return
            arrived.add((w, k, i))
            sem = z_recv.at[w, i - 1] if k == 0 else x_recv.at[w, i, k - 1]
            steps.append(lambda: await_bytes(place(w, k, i), sem))

        def pass_on(w, k, i, bit, source, sent=False):
            chip = here()[0]
            target = place(w, k ^ bit, i)
            remote(source() if source else target, target, {"chip": flip(chip, bit)},
                   x_send.at[w, i, k - 1], x_recv.at[w, i, k - 1], sent)

        def near(w, i):
            take(w, 0, i)
            for bit in bits_of(chips):
                source = (lambda: shards[w]) if i == 0 else None
                steps.append(lambda bit=bit: pass_on(w, bit, i, bit, source))
                ends.append(lambda bit=bit: pass_on(w, bit, i, bit, source, True))

        def far(w, i):
            for k in by_distance(chips):
                bit = link_of(k, i)
                if k ^ bit:
                    take(w, k ^ bit, i)
                    steps.append(lambda k=k, bit=bit: pass_on(w, k, i, bit, None))
                    ends.append(lambda k=k, bit=bit: pass_on(w, k, i, bit, None, True))

        def along(w, i, sent=False):
            chip, core, lane = here()
            target = outs[w].at[chip, core, lane] if full[w] else outs[w].at[chip, i]
            remote(shards[w], target, {"ta": flip(lane, i)}, z_send.at[w, i - 1], z_recv.at[w, i - 1], sent)

        def over(w, k, sent=False):
            chip, core, _ = here()
            piece = outs[w].at[flip(chip, k), core]
            remote(piece, piece, {"core": 1 - core}, c_send.at[w, k], c_recv.at[w, k], sent)

        def got(w, k):
            chip, core, _ = here()
            await_bytes(outs[w].at[flip(chip, k), 1 - core], c_recv.at[w, k])

        steps.append(lambda: greet(chips, wide, any(full)))
        for w in range(n):
            steps.append(lambda w=w: pltpu.make_async_copy(shards[w], place(w, 0, 0), local_sem.at[w]).start())
            placed.append(len(ends))
            ends.append(lambda w=w: pltpu.make_async_copy(shards[w], place(w, 0, 0), local_sem.at[w]).wait())
            for i in range(1, wide):
                steps.append(lambda w=w, i=i: along(w, i))
                ends.append(lambda w=w, i=i: along(w, i, True))
        for w in range(n):
            near(w, 0)
        first = len(steps)
        order = [(w, 0) for w in range(n)] + [(w, i) for w in range(n) for i in range(1, wide)]
        for t, (w, i) in enumerate(order):
            if t >= n:
                near(w, i)
            if t >= 2:
                far(*order[t - 2])
        for w, i in order[-2:]:
            far(w, i)
        for w in range(n):
            if full[w]:
                steps.append(ends[placed[w]])
                ends[placed[w]] = lambda: None
                for k in range(chips):
                    for i in range(wide):
                        take(w, k, i)
                    steps.append(lambda w=w, k=k: over(w, k))
        for w in range(n):
            for i in range(wide):
                for k in range(chips):
                    take(w, k, i)
            if full[w]:
                for k in range(chips):
                    steps.append(lambda w=w, k=k: got(w, k))
                    ends.append(lambda w=w, k=k: over(w, k, True))
        return steps + ends, first


class Scatter:
    def __init__(self, sizes, entries, absolute, number, pace=1.0):
        chips, wide = sizes
        n = len(entries)
        dma = pltpu.SemaphoreType.DMA
        self.sizes, self.absolute, self.number, self.pace = sizes, absolute, number, pace
        self.args, self.where = [], []
        for array, start, cols in entries:
            known = [j for j, a in enumerate(self.args) if a is array]
            if not known:
                self.args.append(array)
            self.where.append((known[0] if known else len(self.args) - 1, start, cols))
        ends = [(array.shape[2], cols) for array, _, cols in entries]
        self.in_specs = [pl.BlockSpec(memory_space=pl.ANY)] * len(self.args)
        self.out_specs = [pl.BlockSpec(memory_space=pltpu.VMEM)] * n
        self.out_shape = [shape_of(e, F32) for e in ends]
        self.scratch = (
            [pltpu.VMEM((wide, chips - 1) + e, BF16) for e in ends]
            + [pltpu.VMEM((wide - 1,) + e, BF16) for e in ends]
            + [pltpu.VMEM((2,) + e, BF16) for e in ends]
            + [
                dma((n, wide, chips - 1)), dma((n, wide, chips - 1)), dma((n, wide - 1)),
                dma((n, wide - 1)), dma((n, 2)),
            ]
        )

    def plan(self, arrays, outs, scratch):
        chips, wide = self.sizes
        absolute, n = self.absolute, len(outs)
        nearby, along, stage = scratch[:n], scratch[n : 2 * n], scratch[2 * n : 3 * n]
        x_send, x_recv, z_send, z_recv, stage_sem = scratch[3 * n :]
        steps, ends = [], []

        def own(w, k, i):
            chip, _, lane = here()
            j, start, cols = self.where[w]
            slot = flip(lane, i) if absolute[w] else i
            if cols == arrays[j].shape[3]:
                return arrays[j].at[flip(chip, k), slot]
            return arrays[j].at[flip(chip, k), slot, :, pl.ds(start, cols)]

        def children(q, i):
            return [k for k in by_distance(chips) if k ^ link_of(k, i) == q]

        def load(w, q, i, turn):
            pltpu.make_async_copy(own(w, q, i), stage[w].at[turn], stage_sem.at[w, turn]).start()

        def total(w, q, i, turn):
            pltpu.make_async_copy(own(w, q, i), stage[w].at[turn], stage_sem.at[w, turn]).wait()
            value = stage[w][turn].astype(F32)
            for k in children(q, i):
                await_bytes(nearby[w].at[i, k - 1], x_recv.at[w, i, k - 1])
                value = value + nearby[w][i, k - 1].astype(F32)
            return value

        def pass_on(source, w, k, i, sent=False):
            chip = here()[0]
            remote(source, nearby[w].at[i, k - 1], {"chip": flip(chip, link_of(k, i))},
                   x_send.at[w, i, k - 1], x_recv.at[w, i, k - 1], sent)

        def relay(w, k, i, turn):
            place = children(k, i)[0] - 1
            nearby[w][i, place] = total(w, k, i, turn).astype(BF16)
            pass_on(nearby[w].at[i, place], w, k, i)

        def onward(w, i, sent=False):
            lane = here()[2]
            remote(nearby[w].at[i, children(0, i)[0] - 1], along[w].at[i - 1], {"ta": flip(lane, i)},
                   z_send.at[w, i - 1], z_recv.at[w, i - 1], sent)

        def finish(w, i, turn):
            value = total(w, 0, i, turn)
            if i == 0:
                outs[w][...] = value
                return
            nearby[w][i, children(0, i)[0] - 1] = value.astype(BF16)
            onward(w, i)

        def last(w):
            value = outs[w][...]
            for i in range(1, wide):
                await_bytes(along[w].at[i - 1], z_recv.at[w, i - 1])
                value = value + along[w][i - 1].astype(F32)
            outs[w][...] = value

        units = [(w, i) for w in range(n) for i in (*range(1, wide), 0)]
        far_first = by_distance(chips)[::-1]
        raw, sums, turns = [], [], [0] * n
        for w, i in units:
            raw.append([])
            for k in far_first:
                if children(k, i):
                    ends.append(lambda w=w, k=k, i=i: pass_on(
                        nearby[w].at[i, children(k, i)[0] - 1], w, k, i, True))
                else:
                    raw[-1].append(lambda w=w, k=k, i=i: pass_on(own(w, k, i), w, k, i))
                    ends.append(lambda w=w, k=k, i=i: pass_on(own(w, k, i), w, k, i, True))
            if i:
                ends.append(lambda w=w, i=i: onward(w, i, True))
        for u in range(len(units) + 1):
            if u < len(units):
                sums += [(u, k) for k in far_first if children(k, units[u][1])]
            if u:
                sums.append((u - 1, 0))
        todo = []
        for u, k in sums:
            w, i = units[u]
            todo.append((u, w, k, i, turns[w] % 2))
            turns[w] += 1
        steps.append(lambda: greet(chips, wide, False))
        for part in raw[:3]:
            steps += part
        first = len(steps)
        steps.append(lambda t=todo[0]: load(*t[1:]))
        for j, (u, w, k, i, turn) in enumerate(todo):
            if j + 1 < len(todo):
                steps.append(lambda t=todo[j + 1]: load(*t[1:]))
            if k:
                steps.append(lambda w=w, k=k, i=i, turn=turn: relay(w, k, i, turn))
                if u + 3 < len(units) and todo[j + 1][0] != u:
                    steps += raw[u + 3]
            else:
                steps.append(lambda w=w, i=i, turn=turn: finish(w, i, turn))
        for w in range(n):
            steps.append(lambda w=w: last(w))
        return steps + ends, first


def alone(work, name):
    a, o = len(work.args), len(work.out_shape)

    def kernel(*refs):
        for step in work.plan(refs[:a], refs[a : a + o], refs[a + o :])[0]:
            step()

    return pl.pallas_call(
        kernel,
        in_specs=work.in_specs,
        out_specs=work.out_specs,
        out_shape=work.out_shape,
        scratch_shapes=work.scratch,
        compiler_params=pltpu.CompilerParams(
            collective_id=work.number, has_side_effects=True, vmem_limit_bytes=VMEM_LIMIT
        ),
        name=name,
    )(*work.args)


def beside(kernel, args, groups, in_specs, out_specs, out_shape, scratch, name, points, work=None):
    if work is None:
        return pl.pallas_call(
            lambda *refs: kernel(lambda point: None, *refs),
            grid=(groups,), in_specs=in_specs, out_specs=out_specs, out_shape=out_shape,
            scratch_shapes=scratch, compiler_params=params(), name=name,
        )(*args), ()
    a, o, s = len(in_specs), len(out_specs), len(scratch)
    b, p = len(work.args), len(work.out_shape)

    def mixed(*refs):
        ins, refs = refs[:a], refs[a:]
        work_ins, refs = refs[:b], refs[b:]
        outs, refs = refs[:o], refs[o:]
        work_outs, refs = refs[:p], refs[p:]
        steps, first = work.plan(work_ins, work_outs, refs[s:])
        slots = groups * points
        table = [[] for _ in range(slots)]
        table[0] = steps[:first]
        rest = steps[first:]
        until = int(len(rest) * work.pace)
        for j, step in enumerate(rest):
            slot = 1 + j * (slots - 2) // until if j < until else slots - 1
            table[slot].append(step)

        def pulse(point):
            for group in range(groups):
                part = table[group * points + point]
                if part:

                    @pl.when(pl.program_id(0) == group)
                    def _():
                        for step in part:
                            step()

        kernel(pulse, *ins, *outs, *refs[:s])

    out = pl.pallas_call(
        mixed,
        grid=(groups,),
        in_specs=list(in_specs) + work.in_specs,
        out_specs=list(out_specs) + work.out_specs,
        out_shape=list(out_shape) + work.out_shape,
        scratch_shapes=list(scratch) + work.scratch,
        compiler_params=pltpu.CompilerParams(
            dimension_semantics=("arbitrary",), vmem_limit_bytes=VMEM_LIMIT,
            collective_id=work.number, has_side_effects=True,
        ),
        name=name,
    )(*args, *work.args)
    return out[:o], out[o:]


def column_sum(values):
    return jnp.sum(values, axis=0, keepdims=True)


def self_forward_kernel(counts, pulse, x_ref, w_ref, bias_ref, gains, shifts, cosine, sine, low_ref, pre_ref, att_ref,
                        lse_ref, own_ref, other_ref, acc):
    heads, size, own = counts
    step = pl.program_id(0)
    pulse(0)
    width = heads * size
    weights = flat(w_ref)
    packed = dot(x_ref[...], weights[:, : 3 * width], 1, 0) + bias_ref[0]
    pre_ref[0] = packed[:, : 2 * width].astype(BF16)
    value_low = packed[:, 2 * width :].astype(BF16)
    length = packed.shape[0]
    block = min(QUERY_BLOCK, length)
    cos, sin = cosine[...], sine[...]
    queries, keys, mixes, logs = [], [], [], []
    for h in range(heads):
        part = packed[:, h * size : (h + 1) * size]
        hat, _ = head_norm(part)
        turned = hat * gains[0:1, :] + shifts[0:1, :]
        query = ((turned * cos + half_turn(turned) * sin) * (size**-0.5)).astype(BF16)
        part = packed[:, width + h * size : width + (h + 1) * size]
        hat, _ = head_norm(part)
        turned = hat * gains[1:2, :] + shifts[1:2, :]
        key = (turned * cos + half_turn(turned) * sin).astype(BF16)
        value = value_low[:, h * size : (h + 1) * size]
        queries.append(query)
        keys.append(key)
        parts, sums = [], []
        for b in range(length // block):
            scores = dot(key, query[b * block : (b + 1) * block], 1, 1)
            top = jnp.max(scores, axis=0, keepdims=True)
            power = jnp.exp(scores - top)
            total = jnp.sum(power, axis=0, keepdims=True)
            shares = (power * (1.0 / total)).astype(BF16)
            parts.append(jnp.transpose(dot(value, shares, 0, 0)))
            sums.append(top + jnp.log(total))
        mixes.append(jnp.concatenate(parts, axis=0))
        logs.append(jnp.concatenate(sums, axis=1))
    low_ref[0] = jnp.concatenate(queries + keys + [value_low], axis=1)
    att = jnp.concatenate(mixes, axis=1).astype(BF16)
    att_ref[0] = att
    lse_ref[0] = jnp.concatenate(logs, axis=0)
    term = dot(att, weights[:, 3 * width :], 1, 1)

    @pl.when(step == 0)
    def _():
        acc[...] = term

    @pl.when(step > 0)
    def _():
        acc[...] += term

    @pl.when(step == pl.num_programs(0) - 1)
    def _():
        own_ref[...] = acc[:own, :]
        other_ref[...] = acc[own:, :].astype(BF16)
    pulse(1)


def self_forward(x, weights, bias, gains, shifts, cosine, sine, own, work=None):
    length, width = x.shape
    chips, groups, rows, all_cols = weights.shape
    size = gains.shape[1]
    small = all_cols // 4
    cols = 3 * small
    heads = small // size
    return beside(
        functools.partial(self_forward_kernel, (heads, size, own)), (x, weights, bias, gains, shifts, cosine, sine), groups,
        in_specs=[whole(x.shape), of_chips(all_cols, weights.shape), per_step(bias.shape)]
        + [whole(gains.shape), whole(shifts.shape), whole(cosine.shape), whole(sine.shape)],
        out_specs=[
            per_step((groups, length, cols)),
            per_step((groups, length, 2 * small)),
            per_step((groups, length, small)),
            per_step((groups, heads, length)),
            whole((own, width)),
            whole((length - own, width)),
        ],
        scratch=[pltpu.VMEM((length, width), F32)],
        out_shape=[
            shape_of((groups, length, cols), BF16),
            shape_of((groups, length, 2 * small), BF16),
            shape_of((groups, length, small), BF16),
            shape_of((groups, heads, length), F32),
            shape_of((own, width), F32),
            shape_of((length - own, width), BF16),
        ],
        name="self_forward", points=2, work=work,
    )


def attention_back(query, key, value, out_grad, logs, block, limit=None):
    length = query.shape[0]
    key_grad, value_grad, query_parts = None, None, []
    for b in range(length // block):
        rows = slice(b * block, (b + 1) * block)
        query_part, grad_part = query[rows], out_grad[rows]
        scores = dot(key, query_part, 1, 1)
        shares = jnp.exp(scores - logs[:, rows])
        if limit is not None:
            index = lax.broadcasted_iota(jnp.int32, shares.shape, 0)
            shares = jnp.where(index < limit, shares, 0.0)
        share_grad = dot(value, grad_part, 1, 1)
        inner = jnp.sum(shares * share_grad, axis=0, keepdims=True)
        score_grad = (shares * (share_grad - inner)).astype(BF16)
        query_parts.append(jnp.transpose(dot(key, score_grad, 0, 0)))
        key_term = dot(score_grad, query_part, 1, 0)
        value_term = dot(shares.astype(BF16), grad_part, 1, 0)
        key_grad = key_term if b == 0 else key_grad + key_term
        value_grad = value_term if b == 0 else value_grad + value_term
    return jnp.concatenate(query_parts, axis=0), key_grad, value_grad


def self_backward_kernel(counts, pulse, x_t, grad_ref, w_ref, low_ref, pre_ref, att_ref, lse_ref, gains, cosine, sine,
                         w_out, own_ref, other_ref, column_ref, head_ref, acc, grad_t):
    heads, size, own = counts
    step = pl.program_id(0)
    pulse(0)
    width = heads * size
    scale = size**-0.5
    weights = flat(w_ref)
    chips, _, rows, _ = w_ref.shape

    @pl.when(step == 0)
    def _():
        grad_t[...] = jnp.transpose(grad_ref[...])

    out_grad = dot(grad_ref[...], weights[:, 3 * width :], 1, 0).astype(BF16)
    comb_grad = dot(grad_t[...], att_ref[0], 1, 0).astype(BF16)
    cos, sin = cosine[...], sine[...]
    block = min(QUERY_BLOCK, out_grad.shape[0])
    query_grads, key_grads, value_grads = [], [], []
    sums = [None] * 4
    for h in range(heads):
        cut = lambda ref, part: ref[0, :, part * width + h * size : part * width + (h + 1) * size]
        query, key, value = cut(low_ref, 0), cut(low_ref, 1), cut(low_ref, 2)
        dq, dk, dv = attention_back(
            query, key, value, out_grad[:, h * size : (h + 1) * size], lse_ref[0, h : h + 1, :], block
        )
        dq = dq * scale
        dq = dq * cos - half_turn(dq) * sin
        dk = dk * cos - half_turn(dk) * sin
        q_hat, q_inverse = head_norm(cut(pre_ref, 0).astype(F32))
        k_hat, k_inverse = head_norm(cut(pre_ref, 1).astype(F32))
        terms = [column_sum(dq * q_hat), column_sum(dk * k_hat), column_sum(dq), column_sum(dk)]
        sums = terms if h == 0 else [s + t for s, t in zip(sums, terms)]
        query_grads.append(head_norm_back(dq, q_hat, q_inverse, gains[0:1, :]))
        key_grads.append(head_norm_back(dk, k_hat, k_inverse, gains[1:2, :]))
        value_grads.append(dv)
        pulse(h + 1)
    packed = jnp.concatenate(query_grads + key_grads + value_grads, axis=1).astype(BF16)
    column_ref[0] = column_sum(packed.astype(F32))
    term = dot(packed, weights[:, : 3 * width], 1, 1)
    proj_grad = dot(x_t[...], packed, 1, 0).astype(BF16)
    w_out[:, 0] = jnp.concatenate([proj_grad, comb_grad], axis=1).reshape(chips, rows, 4 * width)
    head_sums = jnp.concatenate(sums, axis=0)

    @pl.when(step == 0)
    def _():
        acc[...] = term
        head_ref[...] = head_sums

    @pl.when(step > 0)
    def _():
        acc[...] += term
        head_ref[...] += head_sums

    @pl.when(step == pl.num_programs(0) - 1)
    def _():
        own_ref[...] = acc[:own, :]
        other_ref[...] = acc[own:, :].astype(BF16)
    pulse(heads + 1)


def self_backward(x_t, grad, weights, low, pre, att, lse, gains, cosine, sine, own, work=None):
    width, length = x_t.shape
    chips, groups, rows, all_cols = weights.shape
    size = gains.shape[1]
    small = all_cols // 4
    cols = 3 * small
    heads = small // size
    return beside(
        functools.partial(self_backward_kernel, (heads, size, own)), (x_t, grad, weights, low, pre, att, lse, gains, cosine, sine), groups,
        in_specs=[whole(x_t.shape), whole(grad.shape), of_chips(all_cols, weights.shape)]
        + [per_step(v.shape) for v in (low, pre, att, lse)]
        + [whole(gains.shape), whole(cosine.shape), whole(sine.shape)],
        out_specs=[
            of_chips(all_cols, weights.shape),
            whole((own, width)),
            whole((length - own, width)),
            per_step((groups, 1, cols)),
            whole((4, size)),
        ],
        scratch=[
            pltpu.VMEM((length, width), F32),
            pltpu.VMEM((width, length), BF16),
        ],
        out_shape=[
            shape_of(weights.shape, BF16),
            shape_of((own, width), F32),
            shape_of((length - own, width), BF16),
            shape_of((groups, 1, cols), F32),
            shape_of((4, size), F32),
        ],
        name="self_backward", points=heads + 2, work=work,
    )


def cross_forward_kernel(counts, pulse, x_ref, text_ref, w_ref, memory_w, bias_ref, memory_bias, gains, shifts, low_ref,
                         pre_ref, memory_ref, memory_pre, att_ref, lse_ref, own_ref, other_ref, acc):
    heads, size, own, limit = counts
    step = pl.program_id(0)
    pulse(0)
    width = heads * size
    weights = flat(w_ref)
    pre = dot(x_ref[...], weights[:, :width], 1, 0) + bias_ref[0]
    memory = dot(text_ref[...], flat(memory_w), 1, 0) + memory_bias[0]
    pre_ref[0] = pre.astype(BF16)
    memory_pre[0] = memory[:, :width].astype(BF16)
    value_low = memory[:, width:].astype(BF16)
    length = pre.shape[0]
    block = min(QUERY_BLOCK, length)
    queries, keys, mixes, logs = [], [], [], []
    for h in range(heads):
        cols = slice(h * size, (h + 1) * size)
        hat, _ = head_norm(pre[:, cols])
        query = ((hat * gains[2:3, :] + shifts[2:3, :]) * (size**-0.5)).astype(BF16)
        hat, _ = head_norm(memory[:, cols])
        key = (hat * gains[3:4, :]).astype(BF16)
        value = value_low[:, cols]
        queries.append(query)
        keys.append(key)
        parts, sums = [], []
        for b in range(length // block):
            scores = dot(key, query[b * block : (b + 1) * block], 1, 1)
            index = lax.broadcasted_iota(jnp.int32, scores.shape, 0)
            scores = jnp.where(index < limit, scores, -jnp.inf)
            top = jnp.max(scores, axis=0, keepdims=True)
            power = jnp.exp(scores - top)
            total = jnp.sum(power, axis=0, keepdims=True)
            shares = (power * (1.0 / total)).astype(BF16)
            parts.append(jnp.transpose(dot(value, shares, 0, 0)))
            sums.append(top + jnp.log(total))
        mixes.append(jnp.concatenate(parts, axis=0))
        logs.append(jnp.concatenate(sums, axis=1))
    low_ref[0] = jnp.concatenate(queries, axis=1)
    memory_ref[0] = jnp.concatenate(keys + [value_low], axis=1)
    att = jnp.concatenate(mixes, axis=1).astype(BF16)
    att_ref[0] = att
    lse_ref[0] = jnp.concatenate(logs, axis=0)
    term = dot(att, weights[:, width:], 1, 1)

    @pl.when(step == 0)
    def _():
        acc[...] = term

    @pl.when(step > 0)
    def _():
        acc[...] += term

    @pl.when(step == pl.num_programs(0) - 1)
    def _():
        own_ref[...] = acc[:own, :]
        other_ref[...] = acc[own:, :].astype(BF16)
    pulse(1)


def cross_forward(x, text, weights, memory_w, bias, memory_bias, gains, shifts, own, limit, work=None):
    length, width = x.shape
    groups, small = weights.shape[1], weights.shape[3] // 2
    text_rows = text.shape[0]
    size = gains.shape[1]
    heads = small // size
    saved = [
        ((groups, length, small), BF16),
        ((groups, length, small), BF16),
        ((groups, text_rows, 2 * small), BF16),
        ((groups, text_rows, small), BF16),
        ((groups, length, small), BF16),
        ((groups, heads, length), F32),
    ]
    return beside(
        functools.partial(cross_forward_kernel, (heads, size, own, limit)), (x, text, weights, memory_w, bias, memory_bias, gains, shifts), groups,
        in_specs=[whole(x.shape), whole(text.shape)]
        + [of_chips(v.shape[3], v.shape) for v in (weights, memory_w)]
        + [per_step(bias.shape), per_step(memory_bias.shape), whole(gains.shape), whole(shifts.shape)],
        out_specs=[per_step(s) for s, _ in saved] + [whole((own, width)), whole((length - own, width))],
        scratch=[pltpu.VMEM((length, width), F32)],
        out_shape=[shape_of(*s) for s in saved]
        + [shape_of((own, width), F32), shape_of((length - own, width), BF16)],
        name="cross_forward", points=2, work=work,
    )


def cross_backward_kernel(counts, pulse, x_ref, grad_ref, text_ref, w_ref, memory_w, low_ref, pre_ref, memory_ref,
                          memory_pre, att_ref, lse_ref, gains, w_out, memory_out, own_ref, other_ref, text_out,
                          column_ref, memory_column, head_ref, acc, grad_t, x_t, text_t):
    heads, size, own, limit = counts
    step = pl.program_id(0)
    pulse(0)
    width = heads * size
    scale = size**-0.5
    weights = flat(w_ref)
    chips, _, rows, _ = w_ref.shape

    @pl.when(step == 0)
    def _():
        grad_t[...] = jnp.transpose(grad_ref[...])
        x_t[...] = jnp.transpose(x_ref[...])
        text_t[...] = jnp.transpose(text_ref[...])

    out_grad = dot(grad_ref[...], weights[:, width:], 1, 0).astype(BF16)
    blend_grad = dot(grad_t[...], att_ref[0], 1, 0).astype(BF16)
    block = min(QUERY_BLOCK, out_grad.shape[0])
    query_grads, key_grads, value_grads = [], [], []
    sums = [None] * 3
    for h in range(heads):
        cols = slice(h * size, (h + 1) * size)
        query = low_ref[0, :, cols]
        key = memory_ref[0, :, cols]
        value = memory_ref[0, :, width + h * size : width + (h + 1) * size]
        dq, dk, dv = attention_back(
            query, key, value, out_grad[:, cols], lse_ref[0, h : h + 1, :], block, limit
        )
        dq = dq * scale
        q_hat, q_inverse = head_norm(pre_ref[0, :, cols].astype(F32))
        k_hat, k_inverse = head_norm(memory_pre[0, :, cols].astype(F32))
        terms = [column_sum(dq * q_hat), column_sum(dk * k_hat), column_sum(dq)]
        sums = terms if h == 0 else [s + t for s, t in zip(sums, terms)]
        query_grads.append(head_norm_back(dq, q_hat, q_inverse, gains[2:3, :]))
        key_grads.append(head_norm_back(dk, k_hat, k_inverse, gains[3:4, :]))
        value_grads.append(dv)
        pulse(h + 1)
    packed = jnp.concatenate(query_grads, axis=1).astype(BF16)
    memory_grad = jnp.concatenate(key_grads + value_grads, axis=1).astype(BF16)
    column_ref[0] = column_sum(packed.astype(F32))
    memory_column[0] = column_sum(memory_grad.astype(F32))
    term = dot(packed, weights[:, :width], 1, 1)
    text_term = dot(memory_grad, flat(memory_w), 1, 1)
    query_grad = dot(x_t[...], packed, 1, 0).astype(BF16)
    w_out[:, 0] = jnp.concatenate([query_grad, blend_grad], axis=1).reshape(chips, rows, 2 * width)
    memory_out[:, 0] = dot(text_t[...], memory_grad, 1, 0).astype(BF16).reshape(chips, -1, 2 * width)
    head_sums = jnp.concatenate(sums, axis=0)

    @pl.when(step == 0)
    def _():
        acc[...] = term
        text_out[...] = text_term
        head_ref[...] = head_sums

    @pl.when(step > 0)
    def _():
        acc[...] += term
        text_out[...] += text_term
        head_ref[...] += head_sums

    @pl.when(step == pl.num_programs(0) - 1)
    def _():
        own_ref[...] = acc[:own, :]
        other_ref[...] = acc[own:, :].astype(BF16)
    pulse(heads + 1)


def cross_backward(x, grad, text, weights, memory_w, low, pre, memory, memory_pre, att, lse, gains, own, limit, work=None):
    length, width = x.shape
    groups, small = weights.shape[1], weights.shape[3] // 2
    size = gains.shape[1]
    heads = small // size
    pieces = (weights, memory_w)
    tail = [
        ((own, width), F32, False),
        ((length - own, width), BF16, False),
        (text.shape, F32, False),
        ((groups, 1, small), F32, True),
        ((groups, 1, 2 * small), F32, True),
        ((3, size), F32, False),
    ]
    return beside(
        functools.partial(cross_backward_kernel, (heads, size, own, limit)), (x, grad, text, *pieces, low, pre, memory, memory_pre, att, lse, gains), groups,
        in_specs=[whole(x.shape), whole(grad.shape), whole(text.shape)]
        + [of_chips(p.shape[3], p.shape) for p in pieces]
        + [per_step(v.shape) for v in (low, pre, memory, memory_pre, att, lse)]
        + [whole(gains.shape)],
        out_specs=[of_chips(p.shape[3], p.shape) for p in pieces]
        + [per_step(s) if stepped else whole(s) for s, _, stepped in tail],
        scratch=[
            pltpu.VMEM((length, width), F32),
            pltpu.VMEM((width, length), BF16),
            pltpu.VMEM((width, length), BF16),
            pltpu.VMEM((text.shape[1], text.shape[0]), BF16),
        ],
        out_shape=[shape_of(p.shape, BF16) for p in pieces] + [shape_of(s, d) for s, d, _ in tail],
        name="cross_backward", points=heads + 2, work=work,
    )


def mlp_kernel(own, x_ref, cot_ref, x_t, cot_t, w_ref, rest_ref, bias_ref, w_out, out_own, out_other, back_own, back_other,
               hidden_ref, acc, back):
    step = pl.program_id(0)
    chips, _, rows, cols = w_ref.shape
    tile = cols // 2
    w = jnp.where(step % MLP_CHUNKS == 0, flat(w_ref), flat(rest_ref))
    hidden = dot(x_ref[...], w[:, :tile], 1, 0) + bias_ref[0]
    square = hidden * hidden
    inner = 0.7978845608028654 * hidden * (1.0 + 0.044715 * square)
    curve = jnp.tanh(inner)
    active = (0.5 * hidden * (1.0 + curve)).astype(BF16)
    slope = 0.5 * (1.0 + curve) + 0.5 * hidden * (1.0 - curve * curve) * (
        0.7978845608028654 * (1.0 + 3 * 0.044715 * square)
    )
    hidden_grad = dot(cot_ref[...], w[:, tile:], 1, 0) * slope
    hidden_grad = hidden_grad.astype(BF16)
    hidden_ref[0] = column_sum(hidden_grad.astype(F32))
    out_term = dot(active, w[:, tile:], 1, 1)
    back_term = dot(hidden_grad, w[:, :tile], 1, 1)

    @pl.when(step == 0)
    def _():
        acc[...] = out_term
        back[...] = back_term

    @pl.when(step > 0)
    def _():
        acc[...] += out_term
        back[...] += back_term

    w_out[:, 0, :, :tile] = dot(x_t[...], hidden_grad, 1, 0).astype(BF16).reshape(chips, rows, tile)
    w_out[:, 0, :, tile:] = dot(cot_t[...], active, 1, 0).astype(BF16).reshape(chips, rows, tile)

    @pl.when(step == pl.num_programs(0) - 1)
    def _():
        out_own[...] = acc[:own, :]
        out_other[...] = acc[own:, :].astype(BF16)
        back_own[...] = back[:own, :]
        back_other[...] = back[own:, :].astype(BF16)


def mlp(x, cot, x_t, cot_t, weights, rest, bias, own):
    length, width = x.shape
    chips, groups, rows, tile = weights.shape
    cols = tile * MLP_CHUNKS
    shape = (chips, groups, rows, cols)
    first = pl.BlockSpec((chips, 1, rows, tile), lambda i: (0, i // MLP_CHUNKS, 0, 0))
    others = pl.BlockSpec(
        (chips, 1, rows, tile),
        lambda i: (0, i // MLP_CHUNKS, 0, jnp.maximum(i % MLP_CHUNKS - 1, 0)),
    )
    part = pl.BlockSpec(
        (chips, 1, rows, cols // MLP_CHUNKS), lambda i: (0, i // MLP_CHUNKS, 0, i % MLP_CHUNKS)
    )
    tail = [((own, width), F32), ((length - own, width), BF16)] * 2
    return pl.pallas_call(
        functools.partial(mlp_kernel, own),
        grid=(groups * MLP_CHUNKS,),
        in_specs=[whole(v.shape) for v in (x, cot, x_t, cot_t)] + [first, others, per_step(bias.shape)],
        out_specs=[part] + [whole(s) for s, _ in tail] + [per_step(bias.shape)],
        scratch_shapes=[pltpu.VMEM((length, width), F32), pltpu.VMEM((length, width), F32)],
        out_shape=[shape_of(shape, BF16)]
        + [shape_of(*s) for s in tail]
        + [shape_of(bias.shape, F32)],
        compiler_params=params(),
        name="mlp",
    )(x, cot, x_t, cot_t, weights, rest, bias)


def row_spec(block, width):
    return pl.BlockSpec((block, width), lambda i, *_: (i, 0))


def merge_kernel(latent_ref, skip_ref, merger_ref, gains, biases, out_ref):
    left, right, _ = joined_norm(latent_ref, skip_ref)
    width = left.shape[1]
    left = (left * gains[0:1, :] + biases[0:1, :]).astype(BF16)
    right = (right * gains[1:2, :] + biases[1:2, :]).astype(BF16)
    total = dot(left, merger_ref[:width, :], 1, 0) + dot(right, merger_ref[width:, :], 1, 0)
    out_ref[...] = (total + biases[5:6, :]).astype(BF16)


def joined_norm(latent_ref, skip_ref):
    left, right = latent_ref[...].astype(F32), skip_ref[...].astype(F32)
    scale = 0.5 / left.shape[1]
    mean = (jnp.sum(left, axis=-1, keepdims=True) + jnp.sum(right, axis=-1, keepdims=True)) * scale
    left, right = left - mean, right - mean
    spread = jnp.sum(left * left, axis=-1, keepdims=True) + jnp.sum(right * right, axis=-1, keepdims=True)
    inverse = lax.rsqrt(spread * scale + EPSILON)
    return left * inverse, right * inverse, inverse


def merge(latents, skips, merger, gains, biases, block=128):
    rows, width = latents.shape
    return pl.pallas_call(
        merge_kernel,
        grid=(rows // block,),
        in_specs=[row_spec(block, width)] * 2
        + [whole(merger.shape), whole(gains.shape), whole(biases.shape)],
        out_specs=row_spec(block, width),
        out_shape=shape_of((rows, width), BF16),
        compiler_params=params(),
        name="merge",
    )(latents, skips, merger, gains, biases)


def merge_back_kernel(latent_ref, skip_ref, low_ref, merger, gains, biases, left_out, right_out, merge_in, sums):
    left, right, inverse = joined_norm(latent_ref, skip_ref)
    width = left.shape[1]
    low = low_ref[...]
    scale = 0.5 / width
    left_grad = dot(low, merger[:width, :], 1, 1)
    right_grad = dot(low, merger[width:, :], 1, 1)
    merge_in[:, :width] = (left * gains[0:1, :] + biases[0:1, :]).astype(BF16)
    merge_in[:, width:] = (right * gains[1:2, :] + biases[1:2, :]).astype(BF16)
    terms = jnp.concatenate(
        [
            column_sum(left_grad * left),
            column_sum(right_grad * right),
            column_sum(left_grad),
            column_sum(right_grad),
            column_sum(low.astype(F32)),
        ],
        axis=0,
    )
    left_grad, right_grad = left_grad * gains[0:1, :], right_grad * gains[1:2, :]
    first = jnp.sum(left_grad, axis=-1, keepdims=True) + jnp.sum(right_grad, axis=-1, keepdims=True)
    second = jnp.sum(left_grad * left, axis=-1, keepdims=True) + jnp.sum(
        right_grad * right, axis=-1, keepdims=True
    )
    first, second = first * scale, second * scale
    left_out[...] = inverse * (left_grad - first - left * second)
    right_out[...] = inverse * (right_grad - first - right * second)

    @pl.when(pl.program_id(0) == 0)
    def _():
        sums[...] = terms

    @pl.when(pl.program_id(0) > 0)
    def _():
        sums[...] += terms


def merge_back(latents, skips, low, merger, gains, biases, block=128):
    rows, width = latents.shape
    return pl.pallas_call(
        merge_back_kernel,
        grid=(rows // block,),
        in_specs=[row_spec(block, width)] * 3
        + [whole(merger.shape), whole(gains.shape), whole(biases.shape)],
        out_specs=[row_spec(block, width)] * 2 + [row_spec(block, 2 * width), whole((5, width))],
        out_shape=[
            shape_of((rows, width), F32),
            shape_of((rows, width), F32),
            shape_of((rows, 2 * width), BF16),
            shape_of((5, width), F32),
        ],
        compiler_params=params(),
        name="merge_back",
    )(latents, skips, low, merger, gains, biases)


def norm_kernel(count, keep, *refs):
    parts, rows, outs = refs[:count], refs[count], refs[count + 1 :]
    total = parts[0][...].astype(F32)
    for part in parts[1:]:
        total = total + part[...].astype(F32)
    total = total + rows[0:1, :]
    hat, _ = head_norm(total)
    outs[0][...] = (hat * rows[1:2, :] + rows[2:3, :]).astype(BF16)
    if keep:
        outs[1][...] = total


def norm(parts, rows, keep=True, block=128):
    length, width = parts[0].shape
    out = pl.pallas_call(
        functools.partial(norm_kernel, len(parts), keep),
        grid=(length // block,),
        in_specs=[row_spec(block, width)] * len(parts) + [whole(rows.shape)],
        out_specs=[row_spec(block, width)] * (1 + keep),
        out_shape=[shape_of((length, width), BF16)] + [shape_of((length, width), F32)] * keep,
        compiler_params=params(),
        name="norm",
    )(*parts, rows)
    return out if keep else out[0]


def norm_back_kernel(count, keep, *refs):
    parts, value_ref, carried, gain = refs[:count], refs[count], refs[count + 1], refs[count + 2]
    outs = refs[count + 3 :]
    grad = parts[0][...].astype(F32)
    for part in parts[1:]:
        grad = grad + part[...].astype(F32)
    hat, inverse = head_norm(value_ref[...].astype(F32))
    total = carried[...].astype(F32) + head_norm_back(grad, hat, inverse, gain[...])
    low = total.astype(BF16)
    outs[0][...] = low
    if keep:
        outs[2][...] = total
    terms = jnp.concatenate(
        [column_sum(grad * hat), column_sum(grad), column_sum(low.astype(F32))], axis=0
    )
    sums = outs[1]

    @pl.when(pl.program_id(0) == 0)
    def _():
        sums[...] = terms

    @pl.when(pl.program_id(0) > 0)
    def _():
        sums[...] += terms


def norm_back(parts, value, carried, gain, keep=True, block=128):
    length, width = value.shape
    return pl.pallas_call(
        functools.partial(norm_back_kernel, len(parts), keep),
        grid=(length // block,),
        in_specs=[row_spec(block, width)] * (len(parts) + 2) + [whole(gain.shape)],
        out_specs=[row_spec(block, width), whole((3, width))] + [row_spec(block, width)] * keep,
        out_shape=[shape_of((length, width), BF16), shape_of((3, width), F32)]
        + [shape_of((length, width), F32)] * keep,
        compiler_params=params(),
        name="norm_back",
    )(*parts, value, carried, gain)


def body(sizes, latents, skips, text_states, time_embedding, merger, modulator, norm_gains, norm_biases,
         output_bias, projector, combiner, cross_query, cross_memory, blender, expander, reducer,
         column_biases, hidden_bias, per_head_norm_gains, head_shifts, cotangent):
    chips, wide, deep = sizes
    chip_index, core, lane, side = (lax.axis_index(n) for n in ("chip", "core", "ta", "tb"))
    shard_len, local, width = latents.shape
    size = per_head_norm_gains.shape[1]
    text_len, text_width = text_states.shape[1:]
    own_len = shard_len * local
    seq_len = shard_len * wide * deep
    devices = chips * 2 * wide * deep
    latent_total = chips * 2 * local
    half_len = shard_len // 2
    tensor_cols = projector.shape[2]
    head_cols = tensor_cols // 2
    hidden_cols = expander.shape[1] // 2
    chip_bits, wide_bits, deep_bits = bits_of(chips), bits_of(wide)[::-1], bits_of(deep)

    everywhere = [("ta", wide, b) for b in bits_of(wide)] + [("tb", deep, b) for b in deep_bits]
    everywhere = [("core", 2, 1)] + everywhere + [("chip", chips, b) for b in chip_bits]
    index_of = {"chip": chip_index, "core": core, "ta": lane, "tb": side}

    def at(value, index, axis=0):
        return lax.dynamic_index_in_dim(value, index, axis, keepdims=False)

    def gather_all(value):
        value = value[None, None, None, None]
        dims = {"chip": 0, "core": 1, "ta": 2, "tb": 3}
        shape = [1, 1, 1, 1]
        for axis, extent, mask in everywhere:
            value = value.reshape((*shape, *value.shape[4:]))
            other = swap(value, axis, extent, mask)
            high = (index_of[axis] & mask) > 0
            low_part = jnp.where(high, other, value)
            high_part = jnp.where(high, value, other)
            value = jnp.concatenate([low_part, high_part], axis=dims[axis])
            shape[dims[axis]] *= 2
        return value

    def sum_scatter_all(value):
        dims = {"chip": 0, "core": 1, "ta": 2, "tb": 3}
        for axis, extent, mask in everywhere[::-1]:
            dim = dims[axis]
            rows = value.shape[dim] // 2
            high = (index_of[axis] & mask) > 0
            low_part = lax.slice_in_dim(value, 0, rows, axis=dim)
            high_part = lax.slice_in_dim(value, rows, 2 * rows, axis=dim)
            kept = jnp.where(high, high_part, low_part)
            value = kept + swap(jnp.where(high, low_part, high_part), axis, extent, mask)
        return value.reshape(value.shape[4:])

    def halves(value):
        mine, other = at(value, core, 1), at(value, 1 - core, 1)
        other = swap(other, "core", 2, 1)
        pair = jnp.where(core == 0, jnp.stack([mine, other]), jnp.stack([other, mine]))
        return pair.reshape((-1,) + pair.shape[2:])

    def unhalves(value):
        value = value.reshape((2, -1) + value.shape[1:])
        mine, other = at(value, core), at(value, 1 - core)
        other = swap(other, "core", 2, 1)
        return jnp.where(core == 0, jnp.stack([mine, other], 1), jnp.stack([other, mine], 1))

    small = jnp.concatenate(
        [v.reshape(-1) for v in (norm_gains, norm_biases, output_bias, column_biases, hidden_bias)]
    )
    times = time_embedding
    silu_own = jax.nn.silu(times.astype(F32)).astype(BF16)
    small = jnp.concatenate([small, silu_own.astype(F32).reshape(-1)])[None]
    rows, tile = projector.shape[0], hidden_cols // MLP_CHUNKS
    mesh_sizes = (chips, wide)

    def with_tb(value):
        value = value[None]
        for mask in deep_bits:
            other = swap(value, "tb", deep, mask)
            high = (side & mask) > 0
            value = jnp.concatenate(
                [jnp.where(high, other, value), jnp.where(high, value, other)], axis=0
            )
        return value.reshape((-1,) + value.shape[2:])

    self_in = jnp.concatenate([projector, combiner.T[:, None]], axis=1)
    self_in = halves(self_in.reshape(rows, 4, 2, head_cols).transpose(0, 2, 1, 3)).reshape(2 * rows, -1)
    small_all, merger_full, modulator_full, self_w = alone(
        Gather(mesh_sizes, [with_tb(small), with_tb(merger), with_tb(modulator), self_in], (True, True, True, False), 1),
        "gather",
    )
    merger_full = merger_full.reshape(2 * width, width)
    modulator_full = modulator_full.reshape(width, width)
    small_all = small_all.reshape(devices, -1)
    part = norm_gains.shape[1]
    hidden_part = hidden_bias.shape[0]
    table = jnp.transpose(small_all[:, : 21 * part].reshape(devices, 21, part), (1, 0, 2)).reshape(21, width)
    gains, biases, out_bias, columns = table[:5], table[5:14], table[14:15], table[15:21]
    silu_at = 21 * part + hidden_part
    hidden_all = small_all[:, 21 * part : silu_at].reshape(wide, deep, 2, hidden_cols)
    silu_all = small_all[:, silu_at:].reshape(chips * 2, wide * deep, local, width)[:, 0]
    silu_all = silu_all.reshape(latent_total, width).astype(BF16)

    def own_columns(value):
        value = value.reshape(value.shape[0], wide, deep, 2, -1)
        value = at(at(value, side, 2), core, 2)
        return jnp.stack([at(value, lane ^ i, 1) for i in range(wide)])

    def all_columns(value):
        value = jnp.stack([at(value, lane ^ i) for i in range(wide)], axis=1)
        there = (jnp.arange(deep) == side)[:, None] & (jnp.arange(2) == core)[None, :]
        value = jnp.where(there[None, None, :, :, None], value[:, :, None, None, :], 0.0)
        return value.reshape(value.shape[0], -1)

    own_biases = own_columns(columns)

    text_rows_w = cross_memory.shape[0]
    cross_in = jnp.stack([cross_query, blender.T], axis=1)
    cross_in = halves(cross_in.reshape(rows, 2, 2, head_cols).transpose(0, 2, 1, 3)).reshape(2 * rows, -1)
    memory_in = halves(cross_memory.reshape(text_rows_w, 2, 2, head_cols).transpose(0, 2, 1, 3))
    memory_in = memory_in.reshape(2 * text_rows_w, 2 * head_cols)
    mlp_in = jnp.stack([expander, reducer.T], axis=1).reshape(rows, 2, 2, MLP_CHUNKS, tile)
    mlp_in = halves(mlp_in.transpose(0, 2, 3, 1, 4)).reshape(2 * rows, 2 * hidden_cols)
    mlp_parts = [mlp_in[:, : 2 * tile], mlp_in[:, 2 * tile :]]

    mod_rows = modulator.shape[0]
    device = ((chip_index * 2 + core) * wide + lane) * deep + side
    silu_cols = at(silu_all.reshape(latent_total, devices, mod_rows), device, 1)
    silu_mine = lax.dynamic_slice_in_dim(silu_all, chip_index * 2 * local + lane, 1, 0)
    mod = jnp.dot(silu_mine, modulator_full, preferred_element_type=F32)

    def to_latent(value):
        value = value.reshape(local, 2, half_len, width)
        mine, other = at(value, core, 1), at(value, 1 - core, 1)
        other = swap(other, "core", 2, 1)
        pair = jnp.where(core == 0, jnp.stack([mine, other]), jnp.stack([other, mine]))
        return exchange(pair.reshape(wide, half_len, width)).reshape(own_len, width)

    def from_latent(value):
        pair = exchange(value.reshape(wide, half_len, width)).reshape(2, local, half_len, width)
        mine, other = at(pair, core), at(pair, 1 - core)
        other = swap(other, "core", 2, 1)
        value = jnp.where(core == 0, jnp.stack([mine, other], 1), jnp.stack([other, mine], 1))
        return value.reshape(own_len, width)

    def exchange(value):
        own = at(value, lane)
        parts = [own] + [
            swap(at(value, lane ^ mask), "ta", wide, mask) for mask in range(1, wide)
        ]
        parts = jnp.stack(parts)
        return jnp.stack([at(parts, lane ^ i) for i in range(wide)])

    def gather_tokens(value):
        value = jnp.concatenate([value, swap(value, "core", 2, 1)], axis=0)
        for mask in deep_bits:
            value = jnp.concatenate([value, swap(value, "tb", deep, mask)], axis=0)
        return value

    def scatter_tokens(other):
        terms = []
        rest = other
        for mask in deep_bits[::-1]:
            rows_sent = (own_len * 2 * deep) // 2
            kept = rest.shape[0] - rows_sent
            received = swap(rest[kept:], "tb", deep, mask)
            terms.append(received[:own_len])
            rest = (rest[:kept].astype(F32) + received[own_len:].astype(F32)).astype(BF16)
        terms.append(swap(rest, "core", 2, 1))
        return terms

    latents_flat = jnp.transpose(latents, (1, 0, 2)).reshape(own_len, width)
    skips_flat = jnp.transpose(skips, (1, 0, 2)).reshape(own_len, width)
    first_local = merge(latents_flat, skips_flat, merger_full, gains, biases)
    first = to_latent(first_local)
    cot = to_latent(jnp.transpose(cotangent, (1, 0, 2)))
    cot_all = gather_tokens(cot)

    block_index = jnp.arange(wide)[:, None]
    inside = jnp.arange(half_len)[None, :]
    places = []
    for b in range(deep):
        for c in range(2):
            slot = (block_index * deep + (side ^ b)) * 2 + (core ^ c)
            places.append((slot * half_len + inside).reshape(-1))
    places = jnp.concatenate(places)
    quarter = size // 4
    frequency = THETA ** (-2.0 * jnp.arange(quarter).astype(F32) / (size // 2))
    row_angle = (places // GRID_W).astype(F32)[:, None] * frequency
    column_angle = (places % GRID_W).astype(F32)[:, None] * frequency
    angles = jnp.concatenate([row_angle, row_angle, column_angle, column_angle], axis=1)
    sign = jnp.where((jnp.arange(size) // quarter) % 2 == 0, -1.0, 1.0)
    cosine, sine = jnp.cos(angles), jnp.sin(angles) * sign

    zero_row = jnp.zeros((1, width), F32)
    rows_of = lambda *parts: jnp.concatenate(parts, axis=0)
    x_self = gather_tokens(
        norm([first], rows_of(zero_row, gains[2:3], biases[2:3] + biases[6:7] + mod), keep=False)
    )
    self_bias = own_biases[:, 0:3].reshape(wide, 1, 3 * head_cols)
    outs, (cross_w, memory_w, mlp_first) = self_forward(
        x_self, self_w, self_bias, per_head_norm_gains, head_shifts, cosine, sine, own_len,
        Gather(mesh_sizes, [cross_in, memory_in, mlp_parts[0]], (False,) * 3, 2, PACES[0]),
    )
    self_low, self_pre, self_att, self_lse, part_own, part_other = outs
    x_cross, second = norm(
        [first, part_own, *scatter_tokens(part_other)], rows_of(biases[7:8], gains[3:4], biases[3:4])
    )
    x_cross = gather_tokens(x_cross)

    text_pad = -text_len % 16
    text_mine = at(text_states, lane % local)
    text_other = swap(text_mine, "core", 2, 1)
    text = jnp.where(core == lane // local, text_mine, text_other)
    text = jnp.pad(text, ((0, text_pad), (0, 0)))
    cross_bias = own_biases[:, 3:4]
    memory_bias = own_biases[:, 4:6].reshape(wide, 1, 2 * head_cols)
    outs, (mlp_rest,) = cross_forward(
        x_cross, text, cross_w, memory_w, cross_bias, memory_bias,
        per_head_norm_gains, head_shifts, own_len, text_len,
        Gather(mesh_sizes, [mlp_parts[1]], (False,), 3, PACES[1]),
    )
    cross_low, cross_pre, memory_low, memory_pre, cross_att, cross_lse, part_own, part_other = outs
    x_mlp, third = norm(
        [second, part_own, *scatter_tokens(part_other)], rows_of(biases[8:9], gains[4:5], biases[4:5])
    )
    x_mlp = gather_tokens(x_mlp)

    own_hidden = at(at(hidden_all, side, 1), core, 1)
    own_hidden = jnp.stack([at(own_hidden, lane ^ i) for i in range(wide)]).reshape(wide * MLP_CHUNKS, 1, tile)
    mlp_g, out_own, out_other, back_own, back_other, hidden_sum = mlp(
        x_mlp, cot_all, x_mlp.T, cot_all.T, mlp_first, mlp_rest, own_hidden, own_len
    )
    mlp_entries = [(mlp_g, 2 * tile * j, 2 * tile) for j in range(MLP_CHUNKS)]
    outs = [third, out_own, *scatter_tokens(out_other)]
    backs = [back_own, *scatter_tokens(back_other)]
    block_total = sum(v.astype(F32) for v in outs) + out_bias
    block_out = from_latent(block_total.astype(BF16))

    third_low, mlp_sums, third_grad = norm_back(backs, third, cot, gains[4:5])
    blender_g_in = gather_tokens(third_low)
    outs, mlp_grad_first = cross_backward(
        x_cross, blender_g_in, text, cross_w, memory_w, cross_low, cross_pre,
        memory_low, memory_pre, cross_att, cross_lse, per_head_norm_gains, own_len, text_len,
        Scatter(mesh_sizes, mlp_entries[:1], (False,), 4, PACES[2]),
    )
    cross_g, memory_g, part_own, part_other, text_part, query_col, memory_col, cross_heads = outs
    second_low, cross_sums, second_grad = norm_back(
        [part_own, *scatter_tokens(part_other)], second, third_grad, gains[3:4]
    )
    outs, mlp_grad_rest = self_backward(
        x_self.T, gather_tokens(second_low), self_w, self_low, self_pre, self_att,
        self_lse, per_head_norm_gains, cosine, sine, own_len,
        Scatter(mesh_sizes, mlp_entries[1:], (False,) * (MLP_CHUNKS - 1), 5, PACES[3]),
    )
    self_g, part_own, part_other, self_col, self_heads = outs
    first_low, self_sums = norm_back(
        [part_own, *scatter_tokens(part_other)], first, second_grad, gains[2:3], keep=False
    )
    low_local = from_latent(first_low)
    left, right, merge_in, merge_sums = merge_back(
        latents_flat, skips_flat, low_local, merger_full, gains, biases
    )
    merger_g = dot(merge_in, low_local, 0, 0).astype(BF16).reshape(chips, 2, -1, width)
    mine, other = at(merger_g, core, 1), at(merger_g, 1 - core, 1)
    value = mine.astype(F32) + swap(other, "core", 2, 1).astype(F32)
    value = value.reshape(chips, wide, deep, -1, width)
    for mask in deep_bits[::-1]:
        low_part, high_part = jnp.split(value, 2, axis=2)
        high = (side & mask) > 0
        sent = jnp.where(high, low_part, high_part).astype(BF16)
        value = jnp.where(high, high_part, low_part) + swap(sent, "tb", deep, mask).astype(F32)
    merger_g = value.astype(BF16).reshape(chips, wide, -1, width)
    self_grad, cross_grad, memory_grads, merger_grads = alone(
        Scatter(
            mesh_sizes, [(v, 0, v.shape[3]) for v in (self_g, cross_g, memory_g, merger_g)],
            (False, False, False, True), 6,
        ),
        "scatter",
    )
    cross_grad = unhalves(cross_grad.reshape(2 * rows, 2, head_cols)).transpose(2, 0, 1, 3)
    query_grads = cross_grad[0].reshape(rows, tensor_cols)
    blender_grads = cross_grad[1].reshape(rows, tensor_cols).T
    memory_grads = unhalves(memory_grads.reshape(2 * text_rows_w, 2, head_cols))
    memory_grads = memory_grads.transpose(0, 2, 1, 3).reshape(text_rows_w, 2, tensor_cols)
    self_grad = unhalves(self_grad.reshape(2 * rows, 4, head_cols)).transpose(0, 2, 1, 3)
    projector_grads = self_grad[:, :3].reshape(rows, 3, tensor_cols)
    combiner_grads = self_grad[:, 3].reshape(rows, tensor_cols).T

    mlp_grad = jnp.stack([*mlp_grad_first, *mlp_grad_rest], axis=1)
    mlp_grad = unhalves(mlp_grad.reshape(2 * rows, MLP_CHUNKS, 2, tile)).transpose(3, 0, 1, 2, 4)
    expander_grads = mlp_grad[0].reshape(rows, 2 * hidden_cols)
    reducer_grads = mlp_grad[1].reshape(rows, 2 * hidden_cols).T

    text_sum = text_part
    for axis, extent, mask in [("core", 2, 1)] + [("tb", deep, b) for b in deep_bits]:
        text_sum = text_sum + swap(text_sum.astype(BF16), axis, extent, mask).astype(F32)
    text_sum = text_sum[:text_len].astype(BF16).reshape(text_len, wide, deep, -1)
    text_sum = at(text_sum, side, 2).transpose(1, 0, 2)
    text_got = exchange(text_sum)
    text_grads = lax.dynamic_slice_in_dim(text_got, core * local, local, 0).astype(F32)

    mod_grad = self_sums[1:2]
    for axis, extent, mask in [("core", 2, 1)] + [("tb", deep, b) for b in deep_bits]:
        mod_grad = mod_grad + swap(mod_grad, axis, extent, mask)
    mod_all = mod_grad[None]
    for mask in bits_of(wide):
        other = swap(mod_all, "ta", wide, mask)
        high = (lane & mask) > 0
        mod_all = jnp.concatenate([jnp.where(high, other, mod_all), jnp.where(high, mod_all, other)], axis=1)
    for mask in chip_bits:
        other = swap(mod_all, "chip", chips, mask)
        high = (chip_index & mask) > 0
        mod_all = jnp.concatenate([jnp.where(high, other, mod_all), jnp.where(high, mod_all, other)], axis=0)
    mod_all = mod_all.reshape(latent_total, width)
    exact = lax.Precision.HIGHEST
    modulator_grads = lax.dot_general(
        silu_cols.astype(F32), mod_all, (((0,), (0,)), ((), ())), precision=exact
    )
    mod_own = lax.dynamic_slice_in_dim(mod_all, (chip_index * 2 + core) * local, local, 0)
    cols_own = width // (wide * deep)
    tensor_index = lane * deep + side
    modulator_own = lax.dynamic_slice_in_dim(modulator_full, tensor_index * cols_own, cols_own, 0)
    time_own = lax.dot_general(
        mod_own, modulator_own.astype(F32), (((1,), (1,)), ((), ())), precision=exact
    )
    times_own = lax.dynamic_slice_in_dim(times, tensor_index * cols_own, cols_own, 1).astype(F32)
    _, silu_pull = jax.vjp(jax.nn.silu, times_own)
    time_grads = silu_pull(time_own)[0]

    output_sum = jnp.sum(cotangent.astype(F32), axis=(0, 1))[None]
    columns_own = jnp.concatenate(
        [self_col.reshape(wide, 3, head_cols), query_col, memory_col.reshape(wide, 2, head_cols)], axis=1
    )
    sums = jnp.concatenate(
        [
            merge_sums[0:2], self_sums[0:1], cross_sums[0:1], mlp_sums[0:1],
            merge_sums[2:4], self_sums[1:2], cross_sums[1:2], mlp_sums[1:2],
            merge_sums[4:5], self_sums[1:2], cross_sums[2:3], mlp_sums[2:3],
            output_sum, all_columns(columns_own),
        ],
        axis=0,
    )
    hidden_sum = hidden_sum.reshape(wide, 1, hidden_cols)
    hidden_sum = all_columns(hidden_sum)
    sums = jnp.transpose(sums.reshape(21, devices, part), (1, 0, 2)).reshape(devices, -1)
    both = jnp.concatenate([sums, hidden_sum.reshape(devices, hidden_part)], axis=1)
    both = sum_scatter_all(both.reshape(chips, 2, wide, deep, -1))
    table = both[: 21 * part].reshape(21, part)
    hidden_grads = both[21 * part :]
    head_sums = jnp.concatenate(
        [self_heads[0:2], cross_heads[0:2], self_heads[2:4], cross_heads[2:3]], axis=0
    )
    for axis, extent, mask in everywhere:
        head_sums = head_sums + swap(head_sums, axis, extent, mask)

    def to_local(value):
        return jnp.transpose(value.reshape(local, shard_len, width), (1, 0, 2)).astype(F32)

    return (
        to_local(block_out), to_local(left), to_local(right), text_grads, time_grads, merger_grads,
        modulator_grads, table[0:5], table[5:14], table[14], projector_grads, combiner_grads, query_grads,
        memory_grads, blender_grads, expander_grads, reducer_grads, table[15:21], hidden_grads,
        head_sums[0:4], head_sums[4:7],
    )


def solution(mesh):
    data, tensor = mesh.shape["dp"], mesh.shape["tensor"]

    def run(*arrays):
        local = arrays[0].shape[1] // data
        wide = min(tensor, 2 * local)
        deep = tensor // wide
        grid = Mesh(
            mesh.devices.reshape(data // 2, 2, wide, deep), ("chip", "core", "ta", "tb")
        )
        dp, tp = ("chip", "core"), ("ta", "tb")
        both = dp + tp
        tokens = P(tp, dp, None)
        in_specs = (
            tokens, tokens, P(dp, None, None), P(dp, None), P(both, None), P(both, None), P(None, both),
            P(None, both), P(both), P(dp, None, tp), P(tp, dp), P(dp, tp), P(dp, None, tp), P(tp, dp),
            P(dp, tp), P(tp, dp), P(None, both), P(both), P(), P(), tokens,
        )
        out_specs = (
            tokens, tokens, tokens, P(dp, None, tp), P(dp, tp), P(both, None), P(both, None),
            P(None, both), P(None, both), P(both), P(dp, None, tp), P(tp, dp), P(dp, tp),
            P(dp, None, tp), P(tp, dp), P(dp, tp), P(tp, dp), P(None, both), P(both), P(), P(),
        )
        return jax.shard_map(
            functools.partial(body, (data // 2, wide, deep)),
            mesh=grid, in_specs=in_specs, out_specs=out_specs, check_vma=False,
        )(*arrays)

    return run
```
